32 devices in a mesh: lon: 2 (over x), lat: 4 (over z), mem: 4 (over y, core).
Axes of the slice: x: 2, y: 2, z: 4, core: 2. Of those that a mesh axis runs over, the one named last changes fastest.
Arguments:
- control: float32 [640, 32, 256], P('mem', 'lat', 'lon'), may hold values from -6 to 6
- residual: float32 [640, 32, 256], P('mem', 'lat', 'lon'), may hold values from -6 to 6
- direction: float32 [640, 32, 256], P('mem', 'lat', 'lon'), may hold values from -6 to 6
- members: bfloat16 [80, 32, 32, 256], P('mem', None, 'lat', 'lon'), may hold values from -0.625 to 0.625
- vert_modes: float32 [8, 32], replicated, may hold values from -2 to 2
- eig_count: int32 [80], P('mem'), may hold values from 1 to 8, as said below
- lon_decay: float32 [32], P('lat'), may hold values from 0.001953125 to 0.125
- lat_decay: float32 [256], P('lon'), may hold values from 0.015625 to 1
- obs_weight: float32 [32, 32, 256], P(None, 'lat', 'lon'), may hold values from 0.25 to 4
Outputs:
- new_control: float32 [640, 32, 256], P('mem', 'lat', 'lon')
- new_residual: float32 [640, 32, 256], P('mem', 'lat', 'lon')
- new_direction: float32 [640, 32, 256], P('mem', 'lat', 'lon')
The draws below stay inside these ranges and needn't reach their ends.
Inputs may be any that keep to these rules, and one draw needn't show every extreme that they name: Member m uses its first eig_count[m] vertical modes; some member uses all 8.
All inputs are finite; a program needn't handle non-finite values.
Results may differ from the reference program's by a relative error of at most 0.0009.
Values sent between devices are 32-bit elements; how exact they have to be, the bound alone decides.
No kernel may reach another device: no remote copies, remote signals or barrier semaphores. Data moves between devices by JAX's collectives and lax.ppermute only.
A program may use at most 64 MiB of HBM per device.

```python
import math
import jax
import jax.numpy as jnp
from jax import lax

LEV = 32
E = 8
MEMBERS = 80
KMOD = 640
NLON = 256
NLAT = 32


def draw_eig_count(key, part):
    counts = jax.random.randint(jax.random.fold_in(key, 11), (MEMBERS,), 1, E + 1)
    chosen = jax.random.randint(jax.random.fold_in(key, 12), (), 0, MEMBERS)
    return jnp.where(jnp.arange(MEMBERS) == chosen, E, counts).astype(jnp.int32)


def steps_of(own_key, shape, cuts, least, high):
    gain = 1.0
    for dim, shards_of in cuts:
        heights = jax.random.uniform(jax.random.fold_in(jax.random.fold_in(own_key, 6), dim), (shards_of,), jnp.float32, least / len(cuts), high / len(cuts))
        gain = gain * jnp.repeat(jnp.exp(heights), shape[dim] // shards_of).reshape((-1,) + (1,) * (len(shape) - 1 - dim))
    return gain


def normal_values(own_key, shape, scale, reach, split=(), kind=jnp.bfloat16):
    array = scale * jax.random.normal(own_key, shape, jnp.float32)
    if split:
        array = array * steps_of(own_key, shape, split, -0.22, 0.18)
    return jnp.clip(array, -reach, reach).astype(kind)


def setup_inputs(seed: int = 0) -> dict:
    splits = jax.random.split(jax.random.key(seed), 10)
    return {
        "control": normal_values(splits[0], (KMOD, NLAT, NLON), 1.0, 6.0, ((0, 4), (1, 4), (2, 2)), jnp.float32),
        "residual": normal_values(splits[1], (KMOD, NLAT, NLON), 1.0, 6.0, ((0, 4), (1, 4), (2, 2)), jnp.float32),
        "direction": normal_values(splits[2], (KMOD, NLAT, NLON), 1.0, 6.0, ((0, 4), (1, 4), (2, 2)), jnp.float32),
        "members": normal_values(splits[3], (MEMBERS, LEV, NLAT, NLON), (1.0 / MEMBERS ** 0.5), 0.625, ((0, 4), (2, 4), (3, 2))),
        "vert_modes": normal_values(splits[4], (E, LEV), (1.0 / E ** 0.5), 2.0, (), jnp.float32),
        "eig_count": draw_eig_count(jax.random.fold_in(splits[9], 71), 0),
        "lon_decay": jnp.clip(jnp.exp(math.log(0.125) - 4.158883 * jax.random.uniform(splits[6], (NLAT,), jnp.float32) ** steps_of(splits[6], (NLAT,), ((0, 4),), -0.2, 0.2)), 0.001953125, 0.125),
        "lat_decay": jnp.clip(jnp.exp(math.log(1.0) - 4.158883 * jax.random.uniform(splits[7], (NLON,), jnp.float32) ** steps_of(splits[7], (NLON,), ((0, 2),), -0.2, 0.2)), 0.015625, 1.0),
        "obs_weight": jnp.clip(jnp.exp(math.log(4.0) - 2.7725887 * jax.random.uniform(splits[8], (LEV, NLAT, NLON), jnp.float32) ** steps_of(splits[8], (LEV, NLAT, NLON), ((1, 4), (2, 2)), -0.2, 0.2)), 0.25, 4.0),
    }


highest = lax.Precision.HIGHEST

def binomial(offset, degree):
    result = jnp.ones_like(offset)
    for factor in range(degree):
        result = result * (offset + factor + 1.0) / (factor + 1.0)
    return result

def transition(decays, length):
    leakage = 1.0 - jnp.exp(-decays)
    closing = jnp.exp(-length * decays)
    zeroes = jnp.zeros_like(decays)
    matrix_rows = []
    for target in range(4):
        entries = []
        for source in range(4):
            if source <= target:
                spread = target - source
                entries.append(binomial(jnp.full_like(decays, length - 1.0), spread) * leakage ** spread * closing)
            else:
                entries.append(zeroes)
        matrix_rows.append(jnp.stack(entries))
    return jnp.stack(matrix_rows)

def periodic_start(matrix, totals):
    solved = []
    for target in range(4):
        running = totals[target]
        for source in range(target):
            running = running + matrix[target, source] * solved[source]
        solved.append(running / (1.0 - matrix[target, target]))
    return jnp.stack(solved)

def filter_last(fields, decays, periodic, backward):
    retain = jnp.exp(-decays)
    leakage = 1.0 - retain
    scaled = fields * (2.5 / jnp.sqrt(leakage))[:, None]
    if backward:
        scaled = scaled[:, :, ::-1]
    inputs = jnp.moveaxis(scaled, 2, 0)

    def advance(states, column):
        section_one = retain * states[0] + leakage * column
        section_two = retain * states[1] + leakage * section_one
        section_three = retain * states[2] + leakage * section_two
        section_four = retain * states[3] + leakage * section_three
        return (jnp.stack([section_one, section_two, section_three, section_four]), section_four)
    anchor = jnp.zeros((4,) + fields.shape[:2], jnp.float32)
    if periodic:
        totals, unused = lax.scan(advance, anchor, inputs)
        anchor = periodic_start(transition(decays, fields.shape[2]), totals)
    unused, outputs = lax.scan(advance, anchor, inputs)
    outputs = jnp.moveaxis(outputs, 0, 2)
    if backward:
        outputs = outputs[:, :, ::-1]
    return outputs

def localize(fields, lon_decay, lat_decay):
    along_lon = filter_last(fields, lon_decay, True, False)
    across = filter_last(jnp.swapaxes(along_lon, 1, 2), lat_decay, False, False)
    return jnp.swapaxes(across, 1, 2)

def localize_adjoint(fields, lon_decay, lat_decay):
    across = filter_last(jnp.swapaxes(fields, 1, 2), lat_decay, False, True)
    return filter_last(jnp.swapaxes(across, 1, 2), lon_decay, True, True)

def reference(control, residual, direction, members, vert_modes, eig_count, lon_decay, lat_decay, obs_weight):
    mode_count = vert_modes.shape[0]
    member_count = eig_count.shape[0]
    active = (jnp.arange(mode_count)[None, :] < eig_count[:, None]).astype(jnp.float32)
    smooth = localize(direction, lon_decay, lat_decay)
    smooth = smooth.reshape(member_count, mode_count, NLAT, NLON) * active[:, :, None, None]

    def add_member(running, inputs):
        ensemble, weights = inputs
        profile = jnp.einsum('el,eyx->lyx', vert_modes, weights, precision=highest)
        return (running + ensemble.astype(jnp.float32) * profile, None)
    increment, unused = lax.scan(add_member, jnp.zeros((LEV, NLAT, NLON), jnp.float32), (members, smooth))
    weighted = obs_weight * increment

    def member_grad(carry, ensemble):
        projected = jnp.einsum('el,lyx->eyx', vert_modes, ensemble.astype(jnp.float32) * weighted, precision=highest)
        return (carry, projected)
    unused, gradient = lax.scan(member_grad, jnp.zeros((), jnp.float32), members)
    gradient = (gradient * active[:, :, None, None]).reshape(member_count * mode_count, NLAT, NLON)
    hessian = direction + localize_adjoint(gradient, lon_decay, lat_decay)
    norm_old = jnp.sum(residual * residual)
    curvature = jnp.sum(direction * hessian)
    step_size = norm_old / curvature
    new_control = control + step_size * direction
    new_residual = residual - step_size * hessian
    norm_new = jnp.sum(new_residual * new_residual)
    new_direction = new_residual + norm_new / norm_old * direction
    return (new_control, new_residual, new_direction)
```

```python
import functools
import jax
import jax.numpy as jnp
from jax import lax
from jax.experimental import pallas as pl
from jax.experimental.pallas import tpu as pltpu
from jax.sharding import PartitionSpec as P

f32 = jnp.float32
VM = pl.BlockSpec(memory_space=pltpu.VMEM)
SM = pl.BlockSpec(memory_space=pltpu.SMEM)
HI = lax.Precision.HIGHEST


def choose(length, i):
    r = 1.0
    for k in range(i):
        r = r * (length + k) / (k + 1)
    return r


def rising(v, degree):
    r = jnp.ones_like(v)
    for k in range(degree):
        r = r * (v + (k + 1.0)) * (1.0 / (k + 1.0))
    return r


def mm(a, b, dims):
    return lax.dot_general(a, b, (dims, ((), ())), precision=HI, preferred_element_type=f32)


def iota(shape, dim):
    return lax.broadcasted_iota(jnp.int32, shape, dim).astype(f32)


def lon_consts(dec_ref, cells):
    c = jnp.broadcast_to(dec_ref[...], (dec_ref.shape[0], cells))
    q = jnp.exp(-c)
    leak = 1.0 - q
    return c, leak, 2.5 / jnp.sqrt(leak)


def lon_kernel_matrix(c_row, gain_row, cells, backward):
    a = iota((cells, cells), 0)
    b = iota((cells, cells), 1)
    lag = a - b if backward else b - a
    pos = jnp.maximum(lag, 0.0)
    shaped = rising(pos, 3) * jnp.exp(-pos * c_row) * gain_row
    return jnp.where(lag >= 0.0, shaped, 0.0)


def masked_rows(parts, y):
    rows = iota(parts[0].shape, 0)
    return jnp.concatenate([jnp.where(rows == float(y), p, 0.0) for p in parts], axis=0)


def lon_finals(c, leak, scale, cells, backward):
    x = iota(c.shape, 1)
    remain = x if backward else (cells - 1.0) - x
    decay = jnp.exp(-remain * c)
    return [leak ** (s + 1) * scale * rising(remain, s) * decay for s in range(4)]


def lon_entering(c, leak, cells, backward):
    x = iota(c.shape, 1)
    place = (cells - 1.0) - x if backward else x
    decay = jnp.exp(-(place + 1.0) * c)
    return [leak ** (3 - s) * rising(place, 3 - s) * decay for s in range(4)]


def lon_local_rows(load_row, dec_ref, rows, cells, backward, inside_ref, carried_ref):
    c, leak, scale = lon_consts(dec_ref, cells)
    gain = leak**4 * scale
    finals = lon_finals(c, leak, scale, cells, backward)
    carried = None
    for y in range(rows):
        f = load_row(y)
        table = lon_kernel_matrix(c[y : y + 1], gain[y : y + 1], cells, backward)
        inside_ref[y] = mm(f, table, ((1,), (0,)))
        part = mm(masked_rows(finals, y), f, ((1,), (1,)))
        carried = part if carried is None else carried + part
    carried_ref[...] = carried


def lon_incoming(dec_ref, own, others, rows):
    count = len(others) + 1
    k = own.shape[1]
    return count, k


def lon_incoming_states(dec_ref, blocks, rows, cells):
    k = blocks[0].shape[1]
    n = len(blocks)
    c = jnp.broadcast_to(dec_ref[...], (rows, k))
    leak = 1.0 - jnp.exp(-c)

    def trans(r):
        closing = jnp.exp(-float(r * cells) * c)
        return [choose(r * cells, i) * leak**i * closing for i in range(4)]

    total = [jnp.zeros((rows, k), f32) for _ in range(4)]
    for r in range(n):
        part = [blocks[r][s * rows : (s + 1) * rows] for s in range(4)]
        if r:
            t = trans(r)
            part = [sum(t[i - j] * part[j] for j in range(i + 1)) for i in range(4)]
        total = [a + b for a, b in zip(total, part)]
    t = trans(n)
    solved = []
    for i in range(4):
        v = total[i]
        for j in range(i):
            v = v + t[i - j] * solved[j]
        solved.append(v / (1.0 - t[0]))
    return jnp.concatenate(solved, axis=0)


def lon_correction(states_t, entering, y):
    return mm(states_t, masked_rows(entering, y), ((1,), (0,)))


def lat_consts(dec_ref):
    q = jnp.exp(-dec_ref[...])
    leak = 1.0 - q
    return q, leak, leak * (2.5 / jnp.sqrt(leak))


def lat_sweep(load, store, start, dec_ref, rows, k, backward, block):
    q1, l1, g1 = lat_consts(dec_ref)
    x = dec_ref.shape[1]
    q = jnp.broadcast_to(q1, (block, x))
    leak = jnp.broadcast_to(l1, (block, x))
    gain = jnp.broadcast_to(g1, (block, x))
    order = range(rows - 1, -1, -1) if backward else range(rows)

    def step(i, carry):
        at = pl.ds(pl.multiple_of(i * block, 8), block)
        u = start(at)
        for y in order:
            feed = gain * load(y, at, i * block)
            u0 = q * u[0] + feed
            u1 = q * u[1] + leak * u0
            u2 = q * u[2] + leak * u1
            u3 = q * u[3] + leak * u2
            u = [u0, u1, u2, u3]
            store(y, at, i * block, u3, u if y == order[-1] else None)
        return carry

    lax.fori_loop(0, k // block, step, 0)


def k_lon_fwd(rows, k, cells, d_ref, dec_ref, inside_ref, carried_ref):
    lon_local_rows(
        lambda y: d_ref[pl.ds(y, k, stride=rows), :], dec_ref, rows, cells, False, inside_ref, carried_ref
    )


def k_lat_first(rows, k, cells, n, *refs):
    inside_ref, lon_ref, lat_ref, *rest = refs
    blocks = [r[...] for r in rest[:n]]
    f_ref, lat_carried_ref = rest[n:]
    states = lon_incoming_states(lon_ref, blocks, rows, cells).T
    c, leak, _ = lon_consts(lon_ref, cells)
    entering = lon_entering(c, leak, cells, False)
    for y in range(rows):
        f_ref[y] = inside_ref[y] + lon_correction(states, entering, y)
    zero = jnp.zeros((8, cells), f32)

    def store(y, at, base, value, last):
        if last is not None:
            for s in range(4):
                lat_carried_ref[s, at, :] = last[s]

    lat_sweep(
        lambda y, at, base: f_ref[y, at, :], store, lambda at: [zero] * 4, lat_ref, rows, k, False, 8
    )


def k_pass_on(rows, carried_ref, got_ref, dec_ref, out_ref):
    c = dec_ref[...]
    leak = 1.0 - jnp.exp(-c)
    closing = jnp.exp(-float(rows) * c)
    t = [choose(rows, i) * leak**i * closing for i in range(4)]
    got = [got_ref[s] for s in range(4)]
    for i in range(4):
        v = carried_ref[i]
        for j in range(i + 1):
            v = v + t[i - j] * got[j]
        out_ref[i] = v


def sum_states(parts):
    def at_state(s, at):
        v = parts[0][s, at, :]
        for p in parts[1:]:
            v = v + p[s, at, :]
        return v

    return at_state


def member_blocks(members):
    for size in (4, 5, 2, 1):
        if members % size == 0:
            return size


def k_increment(rows, k, chunks, hops, members, modes, levels, *refs):
    f_ref, lat_ref, m_ref, v_ref, eig_ref, *rest = refs
    got = rest[: chunks * hops]
    inc_ref, s_ref = rest[chunks * hops :]
    cells = lat_ref.shape[1]
    size = k // chunks
    for ch in range(chunks):
        at_state = sum_states(got[ch * hops : (ch + 1) * hops])

        def load(y, at, base, ch=ch):
            return f_ref[y, pl.ds(pl.multiple_of(ch * size + base, 8), 8), :]

        def store(y, at, base, value, last, ch=ch):
            s_ref[pl.ds((ch * size + base) * rows + y, 8, stride=rows), :] = value

        lat_sweep(load, store, lambda at: [at_state(s, at) for s in range(4)], lat_ref, rows, size, False, 8)

    per = member_blocks(members)
    for b in range(members // per):
        fields = []
        for m in range(per):
            count = eig_ref[b * per + m]
            for e in range(modes):
                scale = jnp.where(e < count, 1.0, 0.0).astype(f32)
                at = ((b * per + m) * modes + e) * rows
                fields.append(s_ref[at : at + rows, :] * scale)

        def level(l, carry, b=b, fields=fields):
            total = None
            for m in range(per):
                p = None
                for e in range(modes):
                    t = v_ref[e, l] * fields[m * modes + e]
                    p = t if p is None else p + t
                p = m_ref[b * per + m, l].astype(f32) * p
                total = p if total is None else total + p
            if b == 0:
                inc_ref[l] = total
            else:
                inc_ref[l] += total
            return carry

        lax.fori_loop(0, levels, level, 0, unroll=4)


def k_gradient(rows, k, cells, members, modes, levels, inc_ref, got_ref, obs_ref, m_ref, v_ref, eig_ref, lat_ref, g_ref, carried_ref, w_ref):
    w_ref[...] = (inc_ref[...] + got_ref[...]) * obs_ref[...]
    per = member_blocks(members)
    for b in range(members // per):

        def level(l, acc, b=b):
            w = w_ref[l]
            vs = [v_ref[e, l] for e in range(modes)]
            out = []
            for m in range(per):
                t = m_ref[b * per + m, l].astype(f32) * w
                for e in range(modes):
                    out.append(acc[m * modes + e] + vs[e] * t)
            return tuple(out)

        zero = jnp.zeros((rows, cells), f32)
        acc = lax.fori_loop(0, levels, level, (zero,) * (per * modes), unroll=4)
        for m in range(per):
            count = eig_ref[b * per + m]
            for e in range(modes):
                scale = jnp.where(e < count, 1.0, 0.0).astype(f32)
                at = ((b * per + m) * modes + e) * rows
                g_ref[at : at + rows, :] = acc[m * modes + e] * scale
    zero8 = jnp.zeros((8, cells), f32)

    def store(y, at, base, value, last):
        if last is not None:
            for s in range(4):
                carried_ref[s, at, :] = last[s]

    lat_sweep(
        lambda y, at, base: g_ref[pl.ds(base * rows + y, 8, stride=rows), :],
        store,
        lambda at: [zero8] * 4,
        lat_ref,
        rows,
        k,
        True,
        8,
    )


def k_lon_bwd(rows, k, cells, chunks, hops, *refs):
    g_ref, lat_ref, lon_ref, *rest = refs
    got = rest[: chunks * hops]
    inside_ref, carried_ref, p_ref = rest[chunks * hops :]
    size = k // chunks
    for ch in range(chunks):
        at_state = sum_states(got[ch * hops : (ch + 1) * hops])

        def load(y, at, base, ch=ch):
            return g_ref[pl.ds((ch * size + base) * rows + y, 8, stride=rows), :]

        def store(y, at, base, value, last, ch=ch):
            p_ref[y, pl.ds(pl.multiple_of(ch * size + base, 8), 8), :] = value

        lat_sweep(load, store, lambda at: [at_state(s, at) for s in range(4)], lat_ref, rows, size, True, 8)
    lon_local_rows(lambda y: p_ref[y], lon_ref, rows, cells, True, inside_ref, carried_ref)


def k_sums(rows, k, cells, n, *refs):
    inside_ref, lon_ref, d_ref, r_ref, *rest = refs
    blocks = [r[...] for r in rest[:n]]
    h_ref, sums_ref = rest[n:]
    states = lon_incoming_states(lon_ref, blocks, rows, cells).T
    c, leak, _ = lon_consts(lon_ref, cells)
    entering = lon_entering(c, leak, cells, True)
    for y in range(rows):
        at = pl.ds(y, k, stride=rows)
        h_ref[at, :] = inside_ref[y] + lon_correction(states, entering, y)
    block = 64
    zero = jnp.zeros((8, cells), f32)

    def step(i, acc):
        at = pl.ds(pl.multiple_of(i * block, 8), block)
        d = d_ref[at, :]
        r = r_ref[at, :]
        h = h_ref[at, :] + d
        h_ref[at, :] = h
        fold = lambda v: v.reshape(block // 8, 8, cells).sum(axis=0)
        return (acc[0] + fold(r * r), acc[1] + fold(d * h), acc[2] + fold(r * h), acc[3] + fold(h * h))

    acc = lax.fori_loop(0, (k * rows) // block, step, (zero,) * 4)
    out = [a.sum(axis=0, keepdims=True) for a in acc]
    sums_ref[...] = jnp.concatenate(out + [jnp.zeros((4, cells), f32)], axis=0)


def k_update(sums_ref, control_ref, r_ref, d_ref, h_ref, nc_ref, nr_ref, nd_ref):
    sums = jnp.sum(sums_ref[...], axis=1, keepdims=True)
    rr, dh, rh, hh = (sums[i : i + 1, :] for i in range(4))
    step = rr / dh
    norm_new = rr - 2.0 * step * rh + step * step * hh
    beta = norm_new / rr
    d = d_ref[...]
    nr = r_ref[...] - step * h_ref[...]
    nc_ref[...] = control_ref[...] + step * d
    nr_ref[...] = nr
    nd_ref[...] = nr + beta * d


def call(body, outs, ins, specs=None, scratch=(), name=None, cost=None):
    return pl.pallas_call(
        body,
        out_shape=outs,
        in_specs=specs or [VM] * len(ins),
        out_specs=jax.tree.map(lambda _: VM, outs),
        scratch_shapes=scratch,
        name=name,
        cost_estimate=cost,
        compiler_params=pltpu.CompilerParams(vmem_limit_bytes=56 * 1024 * 1024),
    )(*ins)


def sds(*shape):
    return jax.ShapeDtypeStruct(shape, f32)


def lon_exchange(carried, backward):
    n = lax.axis_size("lon")
    sign = -1 if backward else 1
    got = [
        lax.ppermute(carried, "lon", [(j, (j + sign * r) % n) for j in range(n)]) for r in range(1, n)
    ]
    return got + [carried]


def lat_chain(carried, lat_dec, rows, chunks, backward):
    n = lax.axis_size("lat")
    size = carried.shape[1] // chunks
    cells = carried.shape[2]
    parts = [carried[:, c * size : (c + 1) * size] for c in range(chunks)]
    sends = list(parts)
    got = [[] for _ in range(chunks)]
    for h in range(n - 1):
        pair = (n - 1 - h, n - 2 - h) if backward else (h, h + 1)
        for c in range(chunks):
            if h:
                sends[c] = call(
                    functools.partial(k_pass_on, rows),
                    sds(4, size, cells),
                    [parts[c], got[c][-1], lat_dec],
                    name="pass_on",
                )
            got[c].append(lax.ppermute(sends[c], "lat", [pair]))
    return [g for c in range(chunks) for g in got[c]]


def butterfly(v, axis):
    n = lax.axis_size(axis)
    d = 1
    while d < n:
        v = v + lax.ppermute(v, axis, [(i, i ^ d) for i in range(n)])
        d *= 2
    return v


def body(control, residual, direction, members, vert_modes, eig_count, lon_decay, lat_decay, obs_weight):
    k, rows, cells = direction.shape
    mcount, levels = members.shape[:2]
    modes = vert_modes.shape[0]
    n_lon, n_lat, n_mem = (lax.axis_size(a) for a in ("lon", "lat", "mem"))
    chunks = 2
    hops = n_lat - 1
    flat = lambda v: v.reshape(k * rows, cells)
    d, r, ctl = flat(direction), flat(residual), flat(control)
    lon_dec = lon_decay.reshape(rows, 1)
    lat_dec = lat_decay.reshape(1, cells)

    inside, carried = call(
        functools.partial(k_lon_fwd, rows, k, cells),
        (sds(rows, k, cells), sds(4 * rows, k)),
        [d, lon_dec],
        name="lon_fwd",
    )
    blocks = lon_exchange(carried, False)
    f, lat_carried = call(
        functools.partial(k_lat_first, rows, k, cells, n_lon),
        (sds(rows, k, cells), sds(4, k, cells)),
        [inside, lon_dec, lat_dec, *blocks],
        name="lat_first",
    )
    got = lat_chain(lat_carried, lat_dec, rows, chunks, False)
    inc = call(
        functools.partial(k_increment, rows, k, chunks, hops, mcount, modes, levels),
        sds(levels, rows, cells),
        [f, lat_dec, members, vert_modes, eig_count, *got],
        specs=[VM, VM, VM, SM, SM] + [VM] * len(got),
        scratch=[pltpu.VMEM((k * rows, cells), f32)],
        name="increment",
    )
    step = 1
    while step * 2 < n_mem:
        inc = inc + lax.ppermute(inc, "mem", [(i, i ^ step) for i in range(n_mem)])
        step *= 2
    other = lax.ppermute(inc, "mem", [(i, i ^ step) for i in range(n_mem)])
    g, lat_carried = call(
        functools.partial(k_gradient, rows, k, cells, mcount, modes, levels),
        (sds(k * rows, cells), sds(4, k, cells)),
        [inc, other, obs_weight, members, vert_modes, eig_count, lat_dec],
        specs=[VM, VM, VM, VM, SM, SM, VM],
        scratch=[pltpu.VMEM((levels, rows, cells), f32)],
        name="gradient",
    )
    got = lat_chain(lat_carried, lat_dec, rows, chunks, True)
    inside, carried = call(
        functools.partial(k_lon_bwd, rows, k, cells, chunks, hops),
        (sds(rows, k, cells), sds(4 * rows, k)),
        [g, lat_dec, lon_dec, *got],
        scratch=[pltpu.VMEM((rows, k, cells), f32)],
        name="lon_bwd",
    )
    blocks = lon_exchange(carried, True)
    h, sums = call(
        functools.partial(k_sums, rows, k, cells, n_lon),
        (sds(k * rows, cells), sds(8, cells)),
        [inside, lon_dec, d, r, *blocks],
        name="sums",
    )
    for axis in ("mem", "lon", "lat"):
        sums = butterfly(sums, axis)
    outs = call(
        k_update,
        (sds(k * rows, cells),) * 3,
        [sums, ctl, r, d, h],
        name="update",
    )
    return tuple(o.reshape(k, rows, cells) for o in outs)


def solution(mesh):
    field = P("mem", "lat", "lon")
    placed = (
        field,
        field,
        field,
        P("mem", None, "lat", "lon"),
        P(),
        P("mem"),
        P("lat"),
        P("lon"),
        P(None, "lat", "lon"),
    )
    return jax.shard_map(body, mesh=mesh, in_specs=placed, out_specs=(field,) * 3, check_vma=False)
```

```python
import functools
import jax
import jax.numpy as jnp
from jax import lax
from jax.experimental import pallas as pl
from jax.experimental.pallas import tpu as pltpu
from jax.sharding import PartitionSpec as P

f32 = jnp.float32
VM = pl.BlockSpec(memory_space=pltpu.VMEM)
SM = pl.BlockSpec(memory_space=pltpu.SMEM)
HI = lax.Precision.HIGHEST


def choose(length, i):
    r = 1.0
    for k in range(i):
        r = r * (length + k) / (k + 1)
    return r


def rising(v, degree):
    r = jnp.ones_like(v)
    for k in range(degree):
        r = r * (v + (k + 1.0)) * (1.0 / (k + 1.0))
    return r


def mm(a, b, dims):
    return lax.dot_general(a, b, (dims, ((), ())), precision=HI, preferred_element_type=f32)


def iota(shape, dim):
    return lax.broadcasted_iota(jnp.int32, shape, dim).astype(f32)


def lon_consts(dec_ref, cells):
    c = jnp.broadcast_to(dec_ref[...], (dec_ref.shape[0], cells))
    q = jnp.exp(-c)
    leak = 1.0 - q
    return c, leak, 2.5 / jnp.sqrt(leak)


def lon_kernel_matrix(c_row, gain_row, cells, backward):
    a = iota((cells, cells), 0)
    b = iota((cells, cells), 1)
    lag = a - b if backward else b - a
    pos = jnp.maximum(lag, 0.0)
    shaped = rising(pos, 3) * jnp.exp(-pos * c_row) * gain_row
    return jnp.where(lag >= 0.0, shaped, 0.0)


def masked_rows(parts, y):
    rows = iota(parts[0].shape, 0)
    return jnp.concatenate([jnp.where(rows == float(y), p, 0.0) for p in parts], axis=0)


def lon_finals(c, leak, scale, cells, backward):
    x = iota(c.shape, 1)
    remain = x if backward else (cells - 1.0) - x
    decay = jnp.exp(-remain * c)
    return [leak ** (s + 1) * scale * rising(remain, s) * decay for s in range(4)]


def lon_entering(c, leak, cells, backward):
    x = iota(c.shape, 1)
    place = (cells - 1.0) - x if backward else x
    decay = jnp.exp(-(place + 1.0) * c)
    return [leak ** (3 - s) * rising(place, 3 - s) * decay for s in range(4)]


def lon_local_rows(load_row, dec_ref, rows, cells, backward, inside_ref, carried_ref):
    c, leak, scale = lon_consts(dec_ref, cells)
    gain = leak**4 * scale
    finals = lon_finals(c, leak, scale, cells, backward)
    carried = None
    for y in range(rows):
        f = load_row(y)
        table = lon_kernel_matrix(c[y : y + 1], gain[y : y + 1], cells, backward)
        inside_ref[y] = mm(f, table, ((1,), (0,)))
        part = mm(masked_rows(finals, y), f, ((1,), (1,)))
        carried = part if carried is None else carried + part
    carried_ref[...] = carried


def lon_incoming_states(dec_ref, blocks, rows, cells):
    k = blocks[0].shape[1]
    n = len(blocks)
    c = jnp.broadcast_to(dec_ref[...], (rows, k))
    leak = 1.0 - jnp.exp(-c)

    def trans(r):
        closing = jnp.exp(-float(r * cells) * c)
        return [choose(r * cells, i) * leak**i * closing for i in range(4)]

    total = [jnp.zeros((rows, k), f32) for _ in range(4)]
    for r in range(n):
        part = [blocks[r][s * rows : (s + 1) * rows] for s in range(4)]
        if r:
            t = trans(r)
            part = [sum(t[i - j] * part[j] for j in range(i + 1)) for i in range(4)]
        total = [a + b for a, b in zip(total, part)]
    t = trans(n)
    solved = []
    for i in range(4):
        v = total[i]
        for j in range(i):
            v = v + t[i - j] * solved[j]
        solved.append(v / (1.0 - t[0]))
    return jnp.concatenate(solved, axis=0)


def lon_correction(states_t, entering, y):
    return mm(states_t, masked_rows(entering, y), ((1,), (0,)))


def lat_consts(dec_ref):
    q = jnp.exp(-dec_ref[...])
    leak = 1.0 - q
    return q, leak, leak * (2.5 / jnp.sqrt(leak))


def lat_sweep(load, store, start, dec_ref, rows, k, backward, block):
    q1, l1, g1 = lat_consts(dec_ref)
    x = dec_ref.shape[1]
    q = jnp.broadcast_to(q1, (block, x))
    leak = jnp.broadcast_to(l1, (block, x))
    gain = jnp.broadcast_to(g1, (block, x))
    order = range(rows - 1, -1, -1) if backward else range(rows)

    def step(i, carry):
        at = pl.ds(pl.multiple_of(i * block, 8), block)
        u = start(at)
        for y in order:
            feed = gain * load(y, at, i * block)
            u0 = q * u[0] + feed
            u1 = q * u[1] + leak * u0
            u2 = q * u[2] + leak * u1
            u3 = q * u[3] + leak * u2
            u = [u0, u1, u2, u3]
            store(y, at, i * block, u3, u if y == order[-1] else None)
        return carry

    lax.fori_loop(0, k // block, step, 0)


def k_lon_fwd(rows, k, cells, d_ref, dec_ref, inside_ref, carried_ref):
    d_ref = d_ref.reshape(k * rows, cells)
    lon_local_rows(
        lambda y: d_ref[pl.ds(y, k, stride=rows), :], dec_ref, rows, cells, False, inside_ref, carried_ref
    )


def k_lat_first(rows, k, cells, n, *refs):
    inside_ref, lon_ref, lat_ref, *rest = refs
    blocks = [r[...] for r in rest[:n]]
    f_ref, *chunk_refs = rest[n:]
    states = lon_incoming_states(lon_ref, blocks, rows, cells).T
    c, leak, _ = lon_consts(lon_ref, cells)
    entering = lon_entering(c, leak, cells, False)
    for y in range(rows):
        f_ref[y] = inside_ref[y] + lon_correction(states, entering, y)
    zero = jnp.zeros((8, cells), f32)

    size = k // len(chunk_refs)
    for ch, out_ref in enumerate(chunk_refs):

        def store(y, at, base, value, last, out_ref=out_ref):
            if last is not None:
                for s in range(4):
                    out_ref[s, at, :] = last[s]

        def load(y, at, base, ch=ch):
            return f_ref[y, pl.ds(pl.multiple_of(ch * size + base, 8), 8), :]

        lat_sweep(load, store, lambda at: [zero] * 4, lat_ref, rows, size, False, 8)


def k_pass_on(rows, carried_ref, got_ref, dec_ref, out_ref):
    c = dec_ref[...]
    leak = 1.0 - jnp.exp(-c)
    closing = jnp.exp(-float(rows) * c)
    t = [choose(rows, i) * leak**i * closing for i in range(4)]
    got = [got_ref[s] for s in range(4)]
    for i in range(4):
        v = carried_ref[i]
        for j in range(i + 1):
            v = v + t[i - j] * got[j]
        out_ref[i] = v


def sum_states(parts):
    def at_state(s, at):
        v = parts[0][s, at, :]
        for p in parts[1:]:
            v = v + p[s, at, :]
        return v

    return at_state


def member_blocks(members):
    for size in (4, 5, 2, 1):
        if members % size == 0:
            return size


def k_increment(rows, k, chunks, hops, members, modes, levels, *refs):
    f_ref, lat_ref, m_ref, v_ref, eig_ref, *rest = refs
    got = rest[: chunks * hops]
    inc_ref, s_ref = rest[chunks * hops :]
    cells = lat_ref.shape[1]
    size = k // chunks
    for ch in range(chunks):
        at_state = sum_states(got[ch * hops : (ch + 1) * hops])

        def load(y, at, base, ch=ch):
            return f_ref[y, pl.ds(pl.multiple_of(ch * size + base, 8), 8), :]

        def store(y, at, base, value, last, ch=ch):
            s_ref[pl.ds((ch * size + base) * rows + y, 8, stride=rows), :] = value

        lat_sweep(load, store, lambda at: [at_state(s, at) for s in range(4)], lat_ref, rows, size, False, 8)

    per = member_blocks(members)
    for b in range(members // per):
        fields = []
        for m in range(per):
            count = eig_ref[b * per + m]
            for e in range(modes):
                scale = jnp.where(e < count, 1.0, 0.0).astype(f32)
                at = ((b * per + m) * modes + e) * rows
                fields.append(s_ref[at : at + rows, :] * scale)

        def level(l, carry, b=b, fields=fields):
            total = None
            for m in range(per):
                p = None
                for e in range(modes):
                    t = v_ref[e, l] * fields[m * modes + e]
                    p = t if p is None else p + t
                p = m_ref[b * per + m, l].astype(f32) * p
                total = p if total is None else total + p
            if b == 0:
                inc_ref[l] = total
            else:
                inc_ref[l] += total
            return carry

        lax.fori_loop(0, levels, level, 0, unroll=4)


def k_gradient(rows, k, cells, members, modes, levels, inc_ref, got_ref, obs_ref, m_ref, v_ref, eig_ref, lat_ref, g_ref, *rest):
    *chunk_refs, w_ref = rest
    w_ref[...] = (inc_ref[...] + got_ref[...]) * obs_ref[...]
    per = member_blocks(members)
    for b in range(members // per):

        def level(l, acc, b=b):
            w = w_ref[l]
            vs = [v_ref[e, l] for e in range(modes)]
            out = []
            for m in range(per):
                t = m_ref[b * per + m, l].astype(f32) * w
                for e in range(modes):
                    out.append(acc[m * modes + e] + vs[e] * t)
            return tuple(out)

        zero = jnp.zeros((rows, cells), f32)
        acc = lax.fori_loop(0, levels, level, (zero,) * (per * modes), unroll=4)
        for m in range(per):
            count = eig_ref[b * per + m]
            for e in range(modes):
                scale = jnp.where(e < count, 1.0, 0.0).astype(f32)
                at = ((b * per + m) * modes + e) * rows
                g_ref[at : at + rows, :] = acc[m * modes + e] * scale
    zero8 = jnp.zeros((8, cells), f32)

    size = k // len(chunk_refs)
    for ch, out_ref in enumerate(chunk_refs):

        def store(y, at, base, value, last, out_ref=out_ref):
            if last is not None:
                for s in range(4):
                    out_ref[s, at, :] = last[s]

        def load(y, at, base, ch=ch):
            return g_ref[pl.ds((ch * size + base) * rows + y, 8, stride=rows), :]

        lat_sweep(load, store, lambda at: [zero8] * 4, lat_ref, rows, size, True, 8)


def k_lon_bwd(rows, k, cells, chunks, hops, *refs):
    g_ref, lat_ref, lon_ref, *rest = refs
    got = rest[: chunks * hops]
    inside_ref, carried_ref, p_ref = rest[chunks * hops :]
    size = k // chunks
    for ch in range(chunks):
        at_state = sum_states(got[ch * hops : (ch + 1) * hops])

        def load(y, at, base, ch=ch):
            return g_ref[pl.ds((ch * size + base) * rows + y, 8, stride=rows), :]

        def store(y, at, base, value, last, ch=ch):
            p_ref[y, pl.ds(pl.multiple_of(ch * size + base, 8), 8), :] = value

        lat_sweep(load, store, lambda at: [at_state(s, at) for s in range(4)], lat_ref, rows, size, True, 8)
    lon_local_rows(lambda y: p_ref[y], lon_ref, rows, cells, True, inside_ref, carried_ref)


def k_sums(rows, k, cells, n, *refs):
    inside_ref, lon_ref, d_ref, r_ref, *rest = refs
    d_ref = d_ref.reshape(k * rows, cells)
    r_ref = r_ref.reshape(k * rows, cells)
    blocks = [r[...] for r in rest[:n]]
    h_ref, sums_ref = rest[n:]
    states = lon_incoming_states(lon_ref, blocks, rows, cells).T
    c, leak, _ = lon_consts(lon_ref, cells)
    entering = lon_entering(c, leak, cells, True)
    for y in range(rows):
        at = pl.ds(y, k, stride=rows)
        h_ref[at, :] = inside_ref[y] + lon_correction(states, entering, y)
    block = 64
    zero = jnp.zeros((8, cells), f32)

    def step(i, acc):
        at = pl.ds(pl.multiple_of(i * block, 8), block)
        d = d_ref[at, :]
        r = r_ref[at, :]
        h = h_ref[at, :] + d
        h_ref[at, :] = h
        fold = lambda v: v.reshape(block // 8, 8, cells).sum(axis=0)
        return (acc[0] + fold(r * r), acc[1] + fold(d * h), acc[2] + fold(r * h), acc[3] + fold(h * h))

    acc = lax.fori_loop(0, (k * rows) // block, step, (zero,) * 4)
    out = [a.sum(axis=0, keepdims=True) for a in acc]
    sums_ref[...] = jnp.concatenate(out + [jnp.zeros((4, cells), f32)], axis=0)


def k_update(sums_ref, control_ref, r_ref, d_ref, h_ref, nc_ref, nr_ref, nd_ref):
    sums = jnp.sum(sums_ref[...], axis=1, keepdims=True)
    rr, dh, rh, hh = (sums[i : i + 1].reshape(1, 1, 1) for i in range(4))
    step = rr / dh
    norm_new = rr - 2.0 * step * rh + step * step * hh
    beta = norm_new / rr
    d = d_ref[...]
    nr = r_ref[...] - step * h_ref[...]
    nc_ref[...] = control_ref[...] + step * d
    nr_ref[...] = nr
    nd_ref[...] = nr + beta * d


def call(body, outs, ins, specs=None, scratch=(), name=None, cost=None):
    return pl.pallas_call(
        body,
        out_shape=outs,
        in_specs=specs or [VM] * len(ins),
        out_specs=jax.tree.map(lambda _: VM, outs),
        scratch_shapes=scratch,
        name=name,
        cost_estimate=cost,
        compiler_params=pltpu.CompilerParams(vmem_limit_bytes=16 * 1024 * 1024),
    )(*ins)


def sds(*shape):
    return jax.ShapeDtypeStruct(shape, f32)


def lon_exchange(carried, backward):
    n = lax.axis_size("lon")
    sign = -1 if backward else 1
    got = [
        lax.ppermute(carried, "lon", [(j, (j + sign * r) % n) for j in range(n)]) for r in range(1, n)
    ]
    return got + [carried]


def lat_chain(parts, lat_dec, rows, backward):
    n = lax.axis_size("lat")
    chunks = len(parts)
    _, size, cells = parts[0].shape
    sends = list(parts)
    got = [[] for _ in range(chunks)]
    for h in range(n - 1):
        pair = (n - 1 - h, n - 2 - h) if backward else (h, h + 1)
        for c in range(chunks):
            if h:
                sends[c] = call(
                    functools.partial(k_pass_on, rows),
                    sds(4, size, cells),
                    [parts[c], got[c][-1], lat_dec],
                    name="pass_on",
                )
            got[c].append(lax.ppermute(sends[c], "lat", [pair]))
    return [g for c in range(chunks) for g in got[c]]


def butterfly(v, axis):
    n = lax.axis_size(axis)
    d = 1
    while d < n:
        v = v + lax.ppermute(v, axis, [(i, i ^ d) for i in range(n)])
        d *= 2
    return v


def body(control, residual, direction, members, vert_modes, eig_count, lon_decay, lat_decay, obs_weight):
    k, rows, cells = direction.shape
    mcount, levels = members.shape[:2]
    modes = vert_modes.shape[0]
    n_lon, n_lat, n_mem = (lax.axis_size(a) for a in ("lon", "lat", "mem"))
    chunks = 2
    hops = n_lat - 1
    d, r, ctl = direction, residual, control
    lon_dec = lon_decay.reshape(rows, 1)
    lat_dec = lat_decay.reshape(1, cells)

    inside, carried = call(
        functools.partial(k_lon_fwd, rows, k, cells),
        (sds(rows, k, cells), sds(4 * rows, k)),
        [d, lon_dec],
        name="lon_fwd",
    )
    blocks = lon_exchange(carried, False)
    f, *parts = call(
        functools.partial(k_lat_first, rows, k, cells, n_lon),
        (sds(rows, k, cells),) + (sds(4, k // chunks, cells),) * chunks,
        [inside, lon_dec, lat_dec, *blocks],
        name="lat_first",
    )
    got = lat_chain(parts, lat_dec, rows, False)
    inc = call(
        functools.partial(k_increment, rows, k, chunks, hops, mcount, modes, levels),
        sds(levels, rows, cells),
        [f, lat_dec, members, vert_modes, eig_count, *got],
        specs=[VM, VM, VM, SM, SM] + [VM] * len(got),
        scratch=[pltpu.VMEM((k * rows, cells), f32)],
        name="increment",
    )
    step = 1
    while step * 2 < n_mem:
        inc = inc + lax.ppermute(inc, "mem", [(i, i ^ step) for i in range(n_mem)])
        step *= 2
    other = lax.ppermute(inc, "mem", [(i, i ^ step) for i in range(n_mem)])
    g, *parts = call(
        functools.partial(k_gradient, rows, k, cells, mcount, modes, levels),
        (sds(k * rows, cells),) + (sds(4, k // chunks, cells),) * chunks,
        [inc, other, obs_weight, members, vert_modes, eig_count, lat_dec],
        specs=[VM, VM, VM, VM, SM, SM, VM],
        scratch=[pltpu.VMEM((levels, rows, cells), f32)],
        name="gradient",
    )
    got = lat_chain(parts, lat_dec, rows, True)
    inside, carried = call(
        functools.partial(k_lon_bwd, rows, k, cells, chunks, hops),
        (sds(rows, k, cells), sds(4 * rows, k)),
        [g, lat_dec, lon_dec, *got],
        scratch=[pltpu.VMEM((rows, k, cells), f32)],
        name="lon_bwd",
    )
    blocks = lon_exchange(carried, True)
    h, sums = call(
        functools.partial(k_sums, rows, k, cells, n_lon),
        (sds(k * rows, cells), sds(8, cells)),
        [inside, lon_dec, d, r, *blocks],
        name="sums",
    )
    for axis in ("mem", "lon", "lat"):
        sums = butterfly(sums, axis)
    outs = call(
        k_update,
        (sds(k, rows, cells),) * 3,
        [sums, ctl, r, d, h.reshape(k, rows, cells)],
        name="update",
    )
    return tuple(outs)


def solution(mesh):
    field = P("mem", "lat", "lon")
    placed = (
        field,
        field,
        field,
        P("mem", None, "lat", "lon"),
        P(),
        P("mem"),
        P("lat"),
        P("lon"),
        P(None, "lat", "lon"),
    )
    return jax.shard_map(body, mesh=mesh, in_specs=placed, out_specs=(field,) * 3, check_vma=False)
```

```python
import functools
import jax
import jax.numpy as jnp
from jax import lax
from jax.experimental import pallas as pl
from jax.experimental.pallas import tpu as pltpu
from jax.sharding import PartitionSpec as P

f32 = jnp.float32
VM = pl.BlockSpec(memory_space=pltpu.VMEM)
SM = pl.BlockSpec(memory_space=pltpu.SMEM)
HI = lax.Precision.HIGHEST


def choose(length, i):
    r = 1.0
    for k in range(i):
        r = r * (length + k) / (k + 1)
    return r


def rising(v, degree):
    r = jnp.ones_like(v)
    for k in range(degree):
        r = r * (v + (k + 1.0)) * (1.0 / (k + 1.0))
    return r


def mm(a, b, dims):
    return lax.dot_general(a, b, (dims, ((), ())), precision=HI, preferred_element_type=f32)


def iota(shape, dim):
    return lax.broadcasted_iota(jnp.int32, shape, dim).astype(f32)


def lon_consts(lonc):
    c = lonc
    q = jnp.exp(-c)
    leak = 1.0 - q
    return c, leak, 2.5 / jnp.sqrt(leak)


def lon_kernel_matrix(c_row, gain_row, cells, backward):
    a = iota((cells, cells), 0)
    b = iota((cells, cells), 1)
    lag = a - b if backward else b - a
    pos = jnp.maximum(lag, 0.0)
    shaped = rising(pos, 3) * jnp.exp(-pos * c_row) * gain_row
    return jnp.where(lag >= 0.0, shaped, 0.0)


def masked_rows(parts, y):
    rows = iota(parts[0].shape, 0)
    return jnp.concatenate([jnp.where(rows == float(y), p, 0.0) for p in parts], axis=0)


def lon_finals(c, leak, scale, cells, backward):
    x = iota(c.shape, 1)
    remain = x if backward else (cells - 1.0) - x
    decay = jnp.exp(-remain * c)
    return [leak ** (s + 1) * scale * rising(remain, s) * decay for s in range(4)]


def lon_entering(c, leak, cells, backward):
    x = iota(c.shape, 1)
    place = (cells - 1.0) - x if backward else x
    decay = jnp.exp(-(place + 1.0) * c)
    return [leak ** (3 - s) * rising(place, 3 - s) * decay for s in range(4)]


def lon_local_rows(load_row, lonc, rows, cells, backward, inside_ref, carried_ref):
    c, leak, scale = lon_consts(lonc)
    gain = leak**4 * scale
    finals = lon_finals(c, leak, scale, cells, backward)
    carried = None
    for y in range(rows):
        f = load_row(y)
        table = lon_kernel_matrix(c[y : y + 1], gain[y : y + 1], cells, backward)
        inside_ref[y] = mm(f, table, ((1,), (0,)))
        part = mm(masked_rows(finals, y), f, ((1,), (1,)))
        carried = part if carried is None else carried + part
    carried_ref[...] = carried


def lon_incoming_states(lonc, blocks, rows, cells):
    k = blocks[0].shape[1]
    n = len(blocks)
    c = jnp.broadcast_to(lonc[:, :1], (rows, k))
    leak = 1.0 - jnp.exp(-c)

    def trans(r):
        closing = jnp.exp(-float(r * cells) * c)
        return [choose(r * cells, i) * leak**i * closing for i in range(4)]

    total = [jnp.zeros((rows, k), f32) for _ in range(4)]
    for r in range(n):
        part = [blocks[r][s * rows : (s + 1) * rows] for s in range(4)]
        if r:
            t = trans(r)
            part = [sum(t[i - j] * part[j] for j in range(i + 1)) for i in range(4)]
        total = [a + b for a, b in zip(total, part)]
    t = trans(n)
    solved = []
    for i in range(4):
        v = total[i]
        for j in range(i):
            v = v + t[i - j] * solved[j]
        solved.append(v / (1.0 - t[0]))
    return jnp.concatenate(solved, axis=0)


def lon_correction(states_t, entering, y):
    return mm(states_t, masked_rows(entering, y), ((1,), (0,)))


def lat_consts(dec):
    q = jnp.exp(-dec)
    leak = 1.0 - q
    return q, leak, leak * (2.5 / jnp.sqrt(leak))


def lat_sweep(load, store, start, dec, rows, k, backward, block):
    q1, l1, g1 = lat_consts(dec)
    x = dec.shape[1]
    q = jnp.broadcast_to(q1, (block, x))
    leak = jnp.broadcast_to(l1, (block, x))
    gain = jnp.broadcast_to(g1, (block, x))
    order = range(rows - 1, -1, -1) if backward else range(rows)

    def step(i, carry):
        at = pl.ds(pl.multiple_of(i * block, 8), block)
        u = start(at)
        for y in order:
            feed = gain * load(y, at, i * block)
            u0 = q * u[0] + feed
            u1 = q * u[1] + leak * u0
            u2 = q * u[2] + leak * u1
            u3 = q * u[3] + leak * u2
            u = [u0, u1, u2, u3]
            store(y, at, i * block, u3, u if y == order[-1] else None)
        return carry

    lax.fori_loop(0, k // block, step, 0)


def swap_halves(a, b):
    half = a.shape[-1] // 2
    low = iota((1,) * (a.ndim - 1) + (a.shape[-1],), a.ndim - 1) < float(half)
    turn = lambda v: pltpu.roll(v, half, v.ndim - 1)
    return jnp.where(low, a, turn(b)), jnp.where(low, turn(a), b)


def both_halves(v):
    return swap_halves(v, v)


def sum_states(parts):
    def at_state(s, at):
        v = parts[0][s, at, :]
        for p in parts[1:]:
            v = v + p[s, at, :]
        return v

    return at_state


def member_blocks(members):
    for size in (5, 4, 2, 1):
        if members % size == 0:
            return size


def k_lon_fwd(rows, k, cells, d_ref, lon_ref, lat_ref, inside_ref, carried_ref, lonc_ref, latc_ref):
    d_ref = d_ref.reshape(k * rows, cells)
    row = jnp.broadcast_to(lon_ref[...], (rows, rows))
    own = iota((rows, rows), 0) == iota((rows, rows), 1)
    column = jnp.sum(jnp.where(own, row, 0.0), axis=1, keepdims=True)
    lonc = jnp.broadcast_to(column, (rows, cells))
    lonc_ref[...] = lonc
    first, second = both_halves(jnp.broadcast_to(lat_ref[...], (8, cells)))
    latc_ref[0] = first
    latc_ref[1] = second
    lon_local_rows(
        lambda y: d_ref[pl.ds(y, k, stride=rows), :], lonc, rows, cells, False, inside_ref, carried_ref
    )


def k_pack_members(m_ref, a_ref, b_ref):
    half = a_ref.shape[0]

    def step(i, carry):
        a, b = swap_halves(m_ref[i].astype(f32), m_ref[i + half].astype(f32))
        a_ref[i] = a
        b_ref[i] = b
        return carry

    lax.fori_loop(0, half, step, 0)


def k_lat_first(rows, k, cells, n, *refs):
    inside_ref, lon_ref, lat_ref, *rest = refs
    blocks = [r[...] for r in rest[:n]]
    *f_refs, a_ref, b_ref = rest[n:]
    lonc = lon_ref[...]
    states = lon_incoming_states(lonc, blocks, rows, cells).T
    c, leak, _ = lon_consts(lonc)
    entering = lon_entering(c, leak, cells, False)
    half = k // 2
    for y in range(rows):
        row = inside_ref[y] + lon_correction(states, entering, y)
        f_refs[0][y], f_refs[1][y] = swap_halves(row[:half], row[half:])
    zero = jnp.zeros((8, cells), f32)
    for part, (f_ref, out_ref) in enumerate(zip(f_refs, (a_ref, b_ref))):

        def store(y, at, base, value, last, out_ref=out_ref):
            if last is not None:
                for s in range(4):
                    out_ref[s, at, :] = last[s]

        lat_sweep(
            lambda y, at, base: f_ref[y, at, :],
            store,
            lambda at: [zero] * 4,
            lat_ref[part, :1],
            rows,
            half,
            False,
            8,
        )


def k_pass_on(rows, part, carried_ref, got_ref, lat_ref, out_ref):
    c = lat_ref[part, :1]
    leak = 1.0 - jnp.exp(-c)
    closing = jnp.exp(-float(rows) * c)
    t = [choose(rows, i) * leak**i * closing for i in range(4)]
    got = [got_ref[s] for s in range(4)]
    for i in range(4):
        v = carried_ref[i]
        for j in range(i + 1):
            v = v + t[i - j] * got[j]
        out_ref[i] = v


def active_pair(eig_ref, m, pairs, e, cells):
    low = iota((1, cells), 1) < float(cells // 2)
    first = jnp.where(e < eig_ref[m], 1.0, 0.0).astype(f32)
    second = jnp.where(e < eig_ref[m + pairs], 1.0, 0.0).astype(f32)
    return jnp.where(low, first, second)


def k_increment(rows, k, part, hops, pairs, modes, levels, *refs):
    f_ref, lat_ref, m_ref, v_ref, eig_ref, *rest = refs
    got = rest[:hops]
    out_ref, s_ref, inc_ref = rest[hops:]
    cells = lat_ref.shape[-1]
    at_state = sum_states(got)

    def store(y, at, base, value, last):
        s_ref[pl.ds(base * rows + y, 8, stride=rows), :] = value

    lat_sweep(
        lambda y, at, base: f_ref[y, at, :],
        store,
        lambda at: [at_state(s, at) for s in range(4)],
        lat_ref[part, :1],
        rows,
        k,
        False,
        8,
    )
    per = member_blocks(pairs)
    for b in range(pairs // per):
        fields = []
        for m in range(per):
            for e in range(modes):
                scale = active_pair(eig_ref, b * per + m, pairs, e, cells)
                at = ((b * per + m) * modes + e) * rows
                fields.append(s_ref[at : at + rows, :] * scale)

        def level(l, carry, b=b, fields=fields):
            total = None
            for m in range(per):
                p = None
                for e in range(modes):
                    t = v_ref[e, l] * fields[m * modes + e]
                    p = t if p is None else p + t
                p = m_ref[b * per + m, l] * p
                total = p if total is None else total + p
            if b == 0:
                inc_ref[l] = total
            else:
                inc_ref[l] += total
            return carry

        lax.fori_loop(0, levels, level, 0, unroll=4)
    half = levels // 2
    low = iota((1, 1, cells), 2) < float(cells // 2)
    full = inc_ref[...]
    full = full + pltpu.roll(full, cells // 2, 2)
    out_ref[...] = jnp.where(low, full[:half], full[half:])


def k_gradient(rows, k, part, pairs, modes, levels, *refs):
    inc_ref, got_ref, obs_ref, m_ref, v_ref, eig_ref, lat_ref, g_ref, carried_ref, w_ref = refs
    cells = lat_ref.shape[-1]
    half = levels // 2
    first, second = both_halves(inc_ref[...] + got_ref[...])
    obs = both_halves(obs_ref[...])[part]
    w_ref[:half] = first * obs[:half]
    w_ref[half:] = second * obs[half:]
    per = member_blocks(pairs)
    for b in range(pairs // per):

        def level(l, acc, b=b):
            w = w_ref[l]
            vs = [v_ref[e, l] for e in range(modes)]
            out = []
            for m in range(per):
                t = m_ref[b * per + m, l] * w
                for e in range(modes):
                    out.append(acc[m * modes + e] + vs[e] * t)
            return tuple(out)

        zero = jnp.zeros((rows, cells), f32)
        acc = lax.fori_loop(0, levels, level, (zero,) * (per * modes), unroll=4)
        for m in range(per):
            for e in range(modes):
                scale = active_pair(eig_ref, b * per + m, pairs, e, cells)
                at = ((b * per + m) * modes + e) * rows
                g_ref[at : at + rows, :] = acc[m * modes + e] * scale
    zero8 = jnp.zeros((8, cells), f32)

    def store(y, at, base, value, last):
        if last is not None:
            for s in range(4):
                carried_ref[s, at, :] = last[s]

    lat_sweep(
        lambda y, at, base: g_ref[pl.ds(base * rows + y, 8, stride=rows), :],
        store,
        lambda at: [zero8] * 4,
        lat_ref[part, :1],
        rows,
        k,
        True,
        8,
    )


def k_lon_bwd(rows, k, cells, hops, *refs):
    g_refs, lat_ref, lon_ref, rest = refs[:2], refs[2], refs[3], refs[4:]
    got = rest[: 2 * hops]
    inside_ref, carried_ref, p_ref = rest[2 * hops :]
    half = k // 2
    for part in range(2):
        at_state = sum_states(got[part * hops : (part + 1) * hops])
        g_ref = g_refs[part]

        def store(y, at, base, value, last, part=part):
            p_ref[part, y, at, :] = value

        lat_sweep(
            lambda y, at, base: g_ref[pl.ds(base * rows + y, 8, stride=rows), :],
            store,
            lambda at: [at_state(s, at) for s in range(4)],
            lat_ref[part, :1],
            rows,
            half,
            True,
            8,
        )

    def load_row(y):
        return jnp.concatenate(swap_halves(p_ref[0, y], p_ref[1, y]), axis=0)

    lon_local_rows(load_row, lon_ref[...], rows, cells, True, inside_ref, carried_ref)


def k_sums(rows, k, cells, n, *refs):
    inside_ref, lon_ref, d_ref, r_ref, *rest = refs
    d_ref = d_ref.reshape(k * rows, cells)
    r_ref = r_ref.reshape(k * rows, cells)
    blocks = [r[...] for r in rest[:n]]
    h_ref, sums_ref = rest[n:]
    lonc = lon_ref[...]
    states = lon_incoming_states(lonc, blocks, rows, cells).T
    c, leak, _ = lon_consts(lonc)
    entering = lon_entering(c, leak, cells, True)
    for y in range(rows):
        at = pl.ds(y, k, stride=rows)
        h_ref[at, :] = inside_ref[y] + lon_correction(states, entering, y)
    block = 64
    zero = jnp.zeros((8, cells), f32)

    def step(i, acc):
        at = pl.ds(pl.multiple_of(i * block, 8), block)
        d = d_ref[at, :]
        r = r_ref[at, :]
        h = h_ref[at, :] + d
        h_ref[at, :] = h
        fold = lambda v: v.reshape(block // 8, 8, cells).sum(axis=0)
        return (acc[0] + fold(r * r), acc[1] + fold(d * h), acc[2] + fold(r * h), acc[3] + fold(h * h))

    acc = lax.fori_loop(0, (k * rows) // block, step, (zero,) * 4)
    out = [a.sum(axis=0, keepdims=True) for a in acc]
    sums_ref[...] = jnp.concatenate(out + [jnp.zeros((4, cells), f32)], axis=0)


def k_update(sums_ref, control_ref, r_ref, d_ref, h_ref, nc_ref, nr_ref, nd_ref):
    sums = jnp.sum(sums_ref[...], axis=1, keepdims=True)
    rr, dh, rh, hh = (sums[i : i + 1].reshape(1, 1, 1) for i in range(4))
    step = rr / dh
    norm_new = rr - 2.0 * step * rh + step * step * hh
    beta = norm_new / rr
    d = d_ref[...]
    nr = r_ref[...] - step * h_ref[...]
    nc_ref[...] = control_ref[...] + step * d
    nr_ref[...] = nr
    nd_ref[...] = nr + beta * d


def call(body, outs, ins, specs=None, scratch=(), name=None, cost=None):
    return pl.pallas_call(
        body,
        out_shape=outs,
        in_specs=specs or [VM] * len(ins),
        out_specs=jax.tree.map(lambda _: VM, outs),
        scratch_shapes=scratch,
        name=name,
        cost_estimate=None if cost is None else pl.CostEstimate(flops=cost, bytes_accessed=1000, transcendentals=0),
        compiler_params=pltpu.CompilerParams(vmem_limit_bytes=16 * 1024 * 1024),
    )(*ins)


def sds(*shape):
    return jax.ShapeDtypeStruct(shape, f32)


def lon_exchange(carried, backward):
    n = lax.axis_size("lon")
    sign = -1 if backward else 1
    got = [
        lax.ppermute(carried, "lon", [(j, (j + sign * r) % n) for j in range(n)]) for r in range(1, n)
    ]
    return got + [carried]


def lat_chain(parts, latc, rows, backward):
    n = lax.axis_size("lat")
    sends = list(parts)
    got = [[] for _ in parts]
    for h in range(n - 1):
        pair = (n - 1 - h, n - 2 - h) if backward else (h, h + 1)
        for c, part in enumerate(parts):
            if h:
                sends[c] = call(
                    functools.partial(k_pass_on, rows, c),
                    sds(*part.shape),
                    [part, got[c][-1], latc],
                    name="pass_on",
                )
            got[c].append(lax.ppermute(sends[c], "lat", [pair]))
    return got


def all_sum(v, axes, steps):
    total = 1
    for a in axes:
        total *= lax.axis_size(a)
    masks = [0]
    for s in steps:
        masks = masks + [m ^ s for m in masks]
    got = [lax.ppermute(v, axes, [(i, i ^ m) for i in range(total)]) for m in masks[1:]]
    for g in got:
        v = v + g
    return v


def powers(n):
    out, d = [], 1
    while d < n:
        out.append(d)
        d *= 2
    return out


def reduce_everywhere(v):
    n_lon, n_lat, n_mem = (lax.axis_size(a) for a in ("lon", "lat", "mem"))
    mem = powers(n_mem)
    if n_lon == 2 and len(mem) == 2:
        v = all_sum(v, ("mem",), mem[:1])
        v = all_sum(v, ("lon", "mem"), [mem[1], n_mem])
    else:
        for s in mem:
            v = all_sum(v, ("mem",), [s])
        for s in powers(n_lon):
            v = all_sum(v, ("lon",), [s])
    lat = powers(n_lat)
    for i in range(0, len(lat), 2):
        v = all_sum(v, ("lat",), lat[i : i + 2])
    return v


def body(control, residual, direction, members, vert_modes, eig_count, lon_decay, lat_decay, obs_weight):
    k, rows, cells = direction.shape
    mcount, levels = members.shape[:2]
    modes = vert_modes.shape[0]
    n_lon, n_lat, n_mem = (lax.axis_size(a) for a in ("lon", "lat", "mem"))
    hops = n_lat - 1
    half = k // 2
    pairs = mcount // 2
    state = sds(4, half, cells)

    inside, carried, lonc, latc = call(
        functools.partial(k_lon_fwd, rows, k, cells),
        (sds(rows, k, cells), sds(4 * rows, k), sds(rows, cells), sds(2, 8, cells)),
        [direction, lon_decay.reshape(1, rows), lat_decay.reshape(1, cells)],
        name="lon_fwd",
    )
    packed = call(
        k_pack_members, (sds(pairs, levels, rows, cells),) * 2, [members], name="pack_members", cost=10**9
    )
    blocks = lon_exchange(carried, False)
    fa, fb, pa, pb = call(
        functools.partial(k_lat_first, rows, k, cells, n_lon),
        (sds(rows, half, cells),) * 2 + (state,) * 2,
        [inside, lonc, latc, *blocks],
        name="lat_first",
    )
    got = lat_chain([pa, pb], latc, rows, False)
    fields = (fa, fb)
    inc = [None, None]
    for part in range(2):
        inc[part] = call(
            functools.partial(k_increment, rows, half, part, hops, pairs, modes, levels),
            sds(levels // 2, rows, cells),
            [fields[part], latc, packed[part], vert_modes, eig_count, *got[part]],
            specs=[VM, VM, VM, SM, SM] + [VM] * hops,
            scratch=[pltpu.VMEM((half * rows, cells), f32), pltpu.VMEM((levels, rows, cells), f32)],
            name="increment",
        )
    grads, sends = [None, None], [None, None]
    for part in range(2):
        v = inc[part]
        step = 1
        while step * 2 < n_mem:
            v = v + lax.ppermute(v, "mem", [(i, i ^ step) for i in range(n_mem)])
            step *= 2
        other = lax.ppermute(v, "mem", [(i, i ^ step) for i in range(n_mem)])
        grads[part], sends[part] = call(
            functools.partial(k_gradient, rows, half, part, pairs, modes, levels),
            (sds(half * rows, cells), state),
            [v, other, obs_weight, packed[part], vert_modes, eig_count, latc],
            specs=[VM, VM, VM, VM, SM, SM, VM],
            scratch=[pltpu.VMEM((levels, rows, cells), f32)],
            name="gradient",
        )
    got = lat_chain(sends, latc, rows, True)
    inside, carried = call(
        functools.partial(k_lon_bwd, rows, k, cells, hops),
        (sds(rows, k, cells), sds(4 * rows, k)),
        [*grads, latc, lonc, *got[0], *got[1]],
        scratch=[pltpu.VMEM((2, rows, half, cells), f32)],
        name="lon_bwd",
    )
    blocks = lon_exchange(carried, True)
    h, sums = call(
        functools.partial(k_sums, rows, k, cells, n_lon),
        (sds(k * rows, cells), sds(8, cells)),
        [inside, lonc, direction, residual, *blocks],
        name="sums",
    )
    sums = reduce_everywhere(sums)
    outs = call(
        k_update,
        (sds(k, rows, cells),) * 3,
        [sums, control, residual, direction, h.reshape(k, rows, cells)],
        name="update",
    )
    return tuple(outs)


def solution(mesh):
    field = P("mem", "lat", "lon")
    placed = (
        field,
        field,
        field,
        P("mem", None, "lat", "lon"),
        P(),
        P("mem"),
        P("lat"),
        P("lon"),
        P(None, "lat", "lon"),
    )
    return jax.shard_map(body, mesh=mesh, in_specs=placed, out_specs=(field,) * 3, check_vma=False)
```

```python
import functools
import jax
import jax.numpy as jnp
from jax import lax
from jax.experimental import pallas as pl
from jax.experimental.pallas import tpu as pltpu
from jax.sharding import PartitionSpec as P


f32 = jnp.float32
VM = pl.BlockSpec(memory_space=pltpu.VMEM)
SM = pl.BlockSpec(memory_space=pltpu.SMEM)
HI = lax.Precision.HIGHEST


def choose(length, i):
    r = 1.0
    for k in range(i):
        r = r * (length + k) / (k + 1)
    return r


def rising(v, degree):
    r = jnp.ones_like(v)
    for k in range(degree):
        r = r * (v + (k + 1.0)) * (1.0 / (k + 1.0))
    return r


def mm(a, b, dims):
    return lax.dot_general(a, b, (dims, ((), ())), precision=HI, preferred_element_type=f32)


def iota(shape, dim):
    return lax.broadcasted_iota(jnp.int32, shape, dim).astype(f32)


def lon_consts(lonc):
    c = lonc
    q = jnp.exp(-c)
    leak = 1.0 - q
    return c, leak, 2.5 / jnp.sqrt(leak)


def lon_kernel_matrix(c_row, gain_row, cells, backward):
    a = iota((cells, cells), 0)
    b = iota((cells, cells), 1)
    lag = a - b if backward else b - a
    pos = jnp.maximum(lag, 0.0)
    shaped = rising(pos, 3) * jnp.exp(-pos * c_row) * gain_row
    return jnp.where(lag >= 0.0, shaped, 0.0)


def masked_rows(parts, y):
    rows = iota(parts[0].shape, 0)
    return jnp.concatenate([jnp.where(rows == float(y), p, 0.0) for p in parts], axis=0)


def lon_finals(c, leak, scale, cells, backward):
    x = iota(c.shape, 1)
    remain = x if backward else (cells - 1.0) - x
    decay = jnp.exp(-remain * c)
    return [leak ** (s + 1) * scale * rising(remain, s) * decay for s in range(4)]


def lon_entering(c, leak, cells, backward):
    x = iota(c.shape, 1)
    place = (cells - 1.0) - x if backward else x
    decay = jnp.exp(-(place + 1.0) * c)
    return [leak ** (3 - s) * rising(place, 3 - s) * decay for s in range(4)]


def lon_tables(lonc, rows, cells, backward, table_ref):
    c, leak, scale = lon_consts(lonc)
    gain = leak**4 * scale
    for y in range(rows):
        table_ref[y] = lon_kernel_matrix(c[y : y + 1], gain[y : y + 1], cells, backward)


def lon_local_rows(load_row, lonc, table_ref, rows, cells, backward, inside_ref, carried_ref):
    c, leak, scale = lon_consts(lonc)
    finals = lon_finals(c, leak, scale, cells, backward)
    carried = None
    for y in range(rows):
        f = load_row(y)
        inside_ref[y] = mm(f, table_ref[y], ((1,), (0,)))
        part = mm(masked_rows(finals, y), f, ((1,), (1,)))
        carried = part if carried is None else carried + part
    carried_ref[...] = carried


def lon_incoming_states(lonc, blocks, rows, cells):
    k = blocks[0].shape[1]
    n = len(blocks)
    c = jnp.broadcast_to(lonc[:, :1], (rows, k))
    leak = 1.0 - jnp.exp(-c)

    def trans(r):
        closing = jnp.exp(-float(r * cells) * c)
        return [choose(r * cells, i) * leak**i * closing for i in range(4)]

    total = [jnp.zeros((rows, k), f32) for _ in range(4)]
    for r in range(n):
        part = [blocks[r][s * rows : (s + 1) * rows] for s in range(4)]
        if r:
            t = trans(r)
            part = [sum(t[i - j] * part[j] for j in range(i + 1)) for i in range(4)]
        total = [a + b for a, b in zip(total, part)]
    t = trans(n)
    solved = []
    for i in range(4):
        v = total[i]
        for j in range(i):
            v = v + t[i - j] * solved[j]
        solved.append(v / (1.0 - t[0]))
    return jnp.concatenate(solved, axis=0)


def lon_correction(states_t, entering, y):
    return mm(states_t, masked_rows(entering, y), ((1,), (0,)))


def lat_consts(dec):
    q = jnp.exp(-dec)
    leak = 1.0 - q
    return q, leak, leak * (2.5 / jnp.sqrt(leak))


def lat_sweep(load, store, start, dec, rows, k, backward, block):
    q1, l1, g1 = lat_consts(dec)
    x = dec.shape[1]
    q = jnp.broadcast_to(q1, (block, x))
    leak = jnp.broadcast_to(l1, (block, x))
    gain = jnp.broadcast_to(g1, (block, x))
    order = range(rows - 1, -1, -1) if backward else range(rows)

    def step(i, carry):
        at = pl.ds(pl.multiple_of(i * block, 8), block)
        u = start(at)
        for y in order:
            feed = gain * load(y, at, i * block)
            u0 = q * u[0] + feed
            u1 = q * u[1] + leak * u0
            u2 = q * u[2] + leak * u1
            u3 = q * u[3] + leak * u2
            u = [u0, u1, u2, u3]
            store(y, at, i * block, u3, u if y == order[-1] else None)
        return carry

    lax.fori_loop(0, k // block, step, 0)


def swap_halves(a, b):
    half = a.shape[-1] // 2
    low = iota((1,) * (a.ndim - 1) + (a.shape[-1],), a.ndim - 1) < float(half)
    turn = lambda v: pltpu.roll(v, half, v.ndim - 1)
    return jnp.where(low, a, turn(b)), jnp.where(low, turn(a), b)


def both_halves(v):
    return swap_halves(v, v)


def lat_trans(dec, rows):
    leak = 1.0 - jnp.exp(-dec)
    closing = jnp.exp(-float(rows) * dec)
    return [choose(rows, i) * leak**i * closing for i in range(4)]


def incoming_states(plain, carried_on, dec, rows):
    t = lat_trans(dec, rows)

    def at(where):
        out = []
        far = [[p[s, where, :] for s in range(4)] for p in carried_on]
        for s in range(4):
            v = None
            for p in plain:
                v = p[s, where, :] if v is None else v + p[s, where, :]
            for f in far:
                for j in range(s + 1):
                    v = v + t[s - j] * f[j]
            out.append(v)
        return out

    return at


def member_blocks(members):
    for size in (5, 4, 2, 1):
        if members % size == 0:
            return size


def k_tables(rows, cells, dec_ref, lonc_ref, latc_ref, table_ref):
    row = jnp.broadcast_to(dec_ref[:1, :rows], (rows, rows))
    own = iota((rows, rows), 0) == iota((rows, rows), 1)
    column = jnp.sum(jnp.where(own, row, 0.0), axis=1, keepdims=True)
    lonc = jnp.broadcast_to(column, (rows, cells))
    lonc_ref[...] = lonc
    first, second = both_halves(jnp.broadcast_to(dec_ref[1:], (8, cells)))
    latc_ref[0] = first
    latc_ref[1] = second
    lon_tables(lonc, rows, cells, False, table_ref)


def k_lon_fwd(rows, k, cells, d_ref, lon_ref, table_ref, inside_ref, carried_ref):
    d_ref = d_ref.reshape(k * rows, cells)
    lon_local_rows(
        lambda y: d_ref[pl.ds(y, k, stride=rows), :],
        lon_ref[...],
        table_ref,
        rows,
        cells,
        False,
        inside_ref,
        carried_ref,
    )


def k_prepare(m_ref, lon_ref, a_ref, b_ref, table_ref):
    half = a_ref.shape[0]
    lon_tables(lon_ref[...], *lon_ref.shape, True, table_ref)

    def step(i, carry):
        a, b = swap_halves(m_ref[i].astype(f32), m_ref[i + half].astype(f32))
        a_ref[i] = a
        b_ref[i] = b
        return carry

    lax.fori_loop(0, half, step, 0)


def k_lat_first(rows, k, cells, n, *refs):
    inside_ref, lon_ref, lat_ref, *rest = refs
    blocks = [r[...] for r in rest[:n]]
    *f_refs, a_ref, b_ref = rest[n:]
    lonc = lon_ref[...]
    states = lon_incoming_states(lonc, blocks, rows, cells).T
    c, leak, _ = lon_consts(lonc)
    entering = lon_entering(c, leak, cells, False)
    half = k // 2
    for y in range(rows):
        row = inside_ref[y] + lon_correction(states, entering, y)
        f_refs[0][y], f_refs[1][y] = swap_halves(row[:half], row[half:])
    zero = jnp.zeros((8, cells), f32)
    for part, (f_ref, out_ref) in enumerate(zip(f_refs, (a_ref, b_ref))):

        def store(y, at, base, value, last, out_ref=out_ref):
            if last is not None:
                for s in range(4):
                    out_ref[s, at, :] = last[s]

        lat_sweep(
            lambda y, at, base: f_ref[y, at, :],
            store,
            lambda at: [zero] * 4,
            lat_ref[part, :1],
            rows,
            half,
            False,
            8,
        )


def k_pass_on(rows, part, carried_ref, got_ref, lat_ref, out_ref):
    t = lat_trans(lat_ref[part, :1], rows)
    got = [got_ref[s] for s in range(4)]
    for i in range(4):
        v = carried_ref[i]
        for j in range(i + 1):
            v = v + t[i - j] * got[j]
        out_ref[i] = v


def active_pair(eig_ref, m, pairs, e, cells):
    low = iota((1, cells), 1) < float(cells // 2)
    first = jnp.where(e < eig_ref[m], 1.0, 0.0).astype(f32)
    second = jnp.where(e < eig_ref[m + pairs], 1.0, 0.0).astype(f32)
    return jnp.where(low, first, second)


def k_increment(rows, k, part, plain, far, pairs, modes, levels, *refs):
    f_ref, lat_ref, m_ref, v_ref, eig_ref, *rest = refs
    out_ref, s_ref, inc_ref = rest[plain + far :]
    cells = lat_ref.shape[-1]
    start = incoming_states(rest[:plain], rest[plain : plain + far], lat_ref[part, :1], rows)

    def store(y, at, base, value, last):
        s_ref[pl.ds(base * rows + y, 8, stride=rows), :] = value

    lat_sweep(
        lambda y, at, base: f_ref[y, at, :],
        store,
        start,
        lat_ref[part, :1],
        rows,
        k,
        False,
        8,
    )
    per = member_blocks(pairs)
    for b in range(pairs // per):
        fields = []
        for m in range(per):
            for e in range(modes):
                scale = active_pair(eig_ref, b * per + m, pairs, e, cells)
                at = ((b * per + m) * modes + e) * rows
                fields.append(s_ref[at : at + rows, :] * scale)

        def level(l, carry, b=b, fields=fields):
            total = None
            for m in range(per):
                p = None
                for e in range(modes):
                    t = v_ref[e, l] * fields[m * modes + e]
                    p = t if p is None else p + t
                p = m_ref[b * per + m, l] * p
                total = p if total is None else total + p
            if b == 0:
                inc_ref[l] = total
            else:
                inc_ref[l] += total
            return carry

        lax.fori_loop(0, levels, level, 0, unroll=4)
    half = levels // 2
    low = iota((1, 1, cells), 2) < float(cells // 2)
    full = inc_ref[...]
    full = full + pltpu.roll(full, cells // 2, 2)
    out_ref[...] = jnp.where(low, full[:half], full[half:])


def k_gradient(rows, k, part, pairs, modes, levels, *refs):
    inc_ref, got_ref, obs_ref, m_ref, v_ref, eig_ref, lat_ref, g_ref, carried_ref, w_ref = refs
    cells = lat_ref.shape[-1]
    half = levels // 2
    first, second = both_halves(inc_ref[...] + got_ref[...])
    obs = both_halves(obs_ref[...])[part]
    w_ref[:half] = first * obs[:half]
    w_ref[half:] = second * obs[half:]
    per = member_blocks(pairs)
    for b in range(pairs // per):

        def level(l, acc, b=b):
            w = w_ref[l]
            vs = [v_ref[e, l] for e in range(modes)]
            out = []
            for m in range(per):
                t = m_ref[b * per + m, l] * w
                for e in range(modes):
                    out.append(acc[m * modes + e] + vs[e] * t)
            return tuple(out)

        zero = jnp.zeros((rows, cells), f32)
        acc = lax.fori_loop(0, levels, level, (zero,) * (per * modes), unroll=4)
        for m in range(per):
            for e in range(modes):
                scale = active_pair(eig_ref, b * per + m, pairs, e, cells)
                at = ((b * per + m) * modes + e) * rows
                g_ref[at : at + rows, :] = acc[m * modes + e] * scale
    zero8 = jnp.zeros((8, cells), f32)

    def store(y, at, base, value, last):
        if last is not None:
            for s in range(4):
                carried_ref[s, at, :] = last[s]

    lat_sweep(
        lambda y, at, base: g_ref[pl.ds(base * rows + y, 8, stride=rows), :],
        store,
        lambda at: [zero8] * 4,
        lat_ref[part, :1],
        rows,
        k,
        True,
        8,
    )


def k_lon_bwd(rows, k, cells, plain, far, *refs):
    g_refs, lat_ref, lon_ref, table_ref, rest = refs[:2], refs[2], refs[3], refs[4], refs[5:]
    each = plain + far
    inside_ref, carried_ref, p_ref = rest[2 * each :]
    half = k // 2
    for part in range(2):
        got = rest[part * each : (part + 1) * each]
        start = incoming_states(got[:plain], got[plain:], lat_ref[part, :1], rows)
        g_ref = g_refs[part]

        def store(y, at, base, value, last, part=part):
            p_ref[part, y, at, :] = value

        lat_sweep(
            lambda y, at, base: g_ref[pl.ds(base * rows + y, 8, stride=rows), :],
            store,
            start,
            lat_ref[part, :1],
            rows,
            half,
            True,
            8,
        )

    def load_row(y):
        return jnp.concatenate(swap_halves(p_ref[0, y], p_ref[1, y]), axis=0)

    lon_local_rows(load_row, lon_ref[...], table_ref, rows, cells, True, inside_ref, carried_ref)


def k_sums(rows, k, cells, n, *refs):
    inside_ref, lon_ref, d_ref, r_ref, *rest = refs
    d_ref = d_ref.reshape(k * rows, cells)
    r_ref = r_ref.reshape(k * rows, cells)
    blocks = [r[...] for r in rest[:n]]
    h_ref, sums_ref = rest[n:]
    lonc = lon_ref[...]
    states = lon_incoming_states(lonc, blocks, rows, cells).T
    c, leak, _ = lon_consts(lonc)
    entering = lon_entering(c, leak, cells, True)
    for y in range(rows):
        at = pl.ds(y, k, stride=rows)
        h_ref[at, :] = inside_ref[y] + lon_correction(states, entering, y)
    block = 64
    zero = jnp.zeros((8, cells), f32)

    def step(i, acc):
        at = pl.ds(pl.multiple_of(i * block, 8), block)
        d = d_ref[at, :]
        r = r_ref[at, :]
        h = h_ref[at, :] + d
        h_ref[at, :] = h
        fold = lambda v: v.reshape(block // 8, 8, cells).sum(axis=0)
        return (acc[0] + fold(r * r), acc[1] + fold(d * h), acc[2] + fold(r * h), acc[3] + fold(h * h))

    acc = lax.fori_loop(0, (k * rows) // block, step, (zero,) * 4)
    out = [a.sum(axis=0, keepdims=True) for a in acc]
    sums_ref[...] = jnp.concatenate(out + [jnp.zeros((4, cells), f32)], axis=0)


def k_update(sums_ref, control_ref, r_ref, d_ref, h_ref, nc_ref, nr_ref, nd_ref):
    sums = jnp.sum(sums_ref[...], axis=1, keepdims=True)
    rr, dh, rh, hh = (sums[i : i + 1].reshape(1, 1, 1) for i in range(4))
    step = rr / dh
    norm_new = rr - 2.0 * step * rh + step * step * hh
    beta = norm_new / rr
    d = d_ref[...]
    nr = r_ref[...] - step * h_ref[...]
    nc_ref[...] = control_ref[...] + step * d
    nr_ref[...] = nr
    nd_ref[...] = nr + beta * d


def call(body, outs, ins, specs=None, scratch=(), cost=None):
    return pl.pallas_call(
        body,
        out_shape=outs,
        in_specs=specs or [VM] * len(ins),
        out_specs=jax.tree.map(lambda _: VM, outs),
        scratch_shapes=scratch,
        cost_estimate=None if cost is None else pl.CostEstimate(flops=cost, bytes_accessed=1000, transcendentals=0),
        compiler_params=pltpu.CompilerParams(vmem_limit_bytes=16 * 1024 * 1024),
    )(*ins)


def sds(*shape):
    return jax.ShapeDtypeStruct(shape, f32)


def lon_exchange(carried, backward):
    n = lax.axis_size("lon")
    sign = -1 if backward else 1
    got = [
        lax.ppermute(carried, "lon", [(j, (j + sign * r) % n) for j in range(n)]) for r in range(1, n)
    ]
    return got + [carried]


def pass_on(part, got, latc, rows, c):
    return call(functools.partial(k_pass_on, rows, c), sds(*part.shape), [part, got, latc])


def lat_carry(parts, latc, rows, backward):
    n = lax.axis_size("lat")
    at = (lambda i: n - 1 - i) if backward else (lambda i: i)

    def send(v, *pairs):
        return lax.ppermute(v, "lat", [(at(a), at(b)) for a, b in pairs])

    if n == 4:
        near = [send(v, (0, 1), (2, 3)) for v in parts]
        both = [pass_on(v, g, latc, rows, c) for c, (v, g) in enumerate(zip(parts, near))]
        mid, far = [], []
        for v in both:
            far.append(send(v, (1, 3)))
            mid.append(send(v, (1, 2)))
        return [([a, b], [c]) for a, b, c in zip(near, mid, far)]
    sends = list(parts)
    got = [[] for _ in parts]
    for h in range(n - 1):
        for c, part in enumerate(parts):
            if h:
                sends[c] = pass_on(part, got[c][-1], latc, rows, c)
            got[c].append(send(sends[c], (h, h + 1)))
    return [(g, []) for g in got]


def all_sum(v, axes, steps):
    total = 1
    for a in axes:
        total *= lax.axis_size(a)
    masks = [0]
    for s in steps:
        masks = masks + [m ^ s for m in masks]
    got = [lax.ppermute(v, axes, [(i, i ^ m) for i in range(total)]) for m in masks[1:]]
    for g in got:
        v = v + g
    return v


def powers(n):
    out, d = [], 1
    while d < n:
        out.append(d)
        d *= 2
    return out


def reduce_everywhere(v):
    n_lon, n_lat, n_mem = (lax.axis_size(a) for a in ("lon", "lat", "mem"))
    for s in powers(n_mem):
        v = all_sum(v, ("mem",), [s])
    for s in powers(n_lon):
        v = all_sum(v, ("lon",), [s])
    lat = powers(n_lat)
    for i in range(0, len(lat), 2):
        v = all_sum(v, ("lat",), lat[i : i + 2])
    return v


def iteration(control, residual, direction, members, vert_modes, eig_count, lon_decay, lat_decay, obs_weight):
    k, rows, cells = direction.shape
    mcount, levels = members.shape[:2]
    modes = vert_modes.shape[0]
    n_lon, n_mem = lax.axis_size("lon"), lax.axis_size("mem")
    half = k // 2
    pairs = mcount // 2
    state = sds(4, half, cells)

    decays = jnp.stack([jnp.pad(lon_decay, (0, cells - rows)), lat_decay])
    lonc, latc, tables = call(
        functools.partial(k_tables, rows, cells),
        (sds(rows, cells), sds(2, 8, cells), sds(rows, cells, cells)),
        [decays],
        cost=10**9,
    )
    inside, carried = call(
        functools.partial(k_lon_fwd, rows, k, cells),
        (sds(rows, k, cells), sds(4 * rows, k)),
        [direction, lonc, tables],
    )
    *packed, tables = call(
        k_prepare,
        (sds(pairs, levels, rows, cells),) * 2 + (sds(rows, cells, cells),),
        [members, lonc],
        cost=10**9,
    )
    blocks = lon_exchange(carried, False)
    fa, fb, pa, pb = call(
        functools.partial(k_lat_first, rows, k, cells, n_lon),
        (sds(rows, half, cells),) * 2 + (state,) * 2,
        [inside, lonc, latc, *blocks],
    )
    got = lat_carry([pa, pb], latc, rows, False)
    plain, far = (len(g) for g in got[0])
    fields = (fa, fb)
    inc = [None, None]
    for part in range(2):
        inc[part] = call(
            functools.partial(k_increment, rows, half, part, plain, far, pairs, modes, levels),
            sds(levels // 2, rows, cells),
            [fields[part], latc, packed[part], vert_modes, eig_count, *got[part][0], *got[part][1]],
            specs=[VM, VM, VM, SM, SM] + [VM] * (plain + far),
            scratch=[pltpu.VMEM((half * rows, cells), f32), pltpu.VMEM((levels, rows, cells), f32)],
        )
    grads, sends = [None, None], [None, None]
    for part in range(2):
        v = inc[part]
        step = 1
        while step * 2 < n_mem:
            v = v + lax.ppermute(v, "mem", [(i, i ^ step) for i in range(n_mem)])
            step *= 2
        other = lax.ppermute(v, "mem", [(i, i ^ step) for i in range(n_mem)])
        grads[part], sends[part] = call(
            functools.partial(k_gradient, rows, half, part, pairs, modes, levels),
            (sds(half * rows, cells), state),
            [v, other, obs_weight, packed[part], vert_modes, eig_count, latc],
            specs=[VM, VM, VM, VM, SM, SM, VM],
            scratch=[pltpu.VMEM((levels, rows, cells), f32)],
        )
    got = lat_carry(sends, latc, rows, True)
    inside, carried = call(
        functools.partial(k_lon_bwd, rows, k, cells, plain, far),
        (sds(rows, k, cells), sds(4 * rows, k)),
        [*grads, latc, lonc, tables, *got[0][0], *got[0][1], *got[1][0], *got[1][1]],
        scratch=[pltpu.VMEM((2, rows, half, cells), f32)],
    )
    blocks = lon_exchange(carried, True)
    h, sums = call(
        functools.partial(k_sums, rows, k, cells, n_lon),
        (sds(k * rows, cells), sds(8, cells)),
        [inside, lonc, direction, residual, *blocks],
    )
    sums = reduce_everywhere(sums)
    outs = call(
        k_update,
        (sds(k, rows, cells),) * 3,
        [sums, control, residual, direction, h.reshape(k, rows, cells)],
    )
    return tuple(outs)


def solution(mesh):
    field = P("mem", "lat", "lon")
    placed = (
        field,
        field,
        field,
        P("mem", None, "lat", "lon"),
        P(),
        P("mem"),
        P("lat"),
        P("lon"),
        P(None, "lat", "lon"),
    )
    return jax.shard_map(iteration, mesh=mesh, in_specs=placed, out_specs=(field,) * 3, check_vma=False)
```

```python
import functools
import jax
import jax.numpy as jnp
from jax import lax
from jax.experimental import pallas as pl
from jax.experimental.pallas import tpu as pltpu
from jax.sharding import PartitionSpec as P

f32 = jnp.float32
VM = pl.BlockSpec(memory_space=pltpu.VMEM)
SM = pl.BlockSpec(memory_space=pltpu.SMEM)
HI = lax.Precision.HIGHEST


def choose(length, i):
    r = 1.0
    for k in range(i):
        r = r * (length + k) / (k + 1)
    return r


def rising(v, degree):
    r = jnp.ones_like(v)
    for k in range(degree):
        r = r * (v + (k + 1.0)) * (1.0 / (k + 1.0))
    return r


def mm(a, b, dims):
    return lax.dot_general(a, b, (dims, ((), ())), precision=HI, preferred_element_type=f32)


def iota(shape, dim):
    return lax.broadcasted_iota(jnp.int32, shape, dim).astype(f32)


def lon_consts(lonc):
    c = lonc
    q = jnp.exp(-c)
    leak = 1.0 - q
    return c, leak, 2.5 / jnp.sqrt(leak)


def lon_kernel_matrix(c_row, gain_row, cells, backward):
    a = iota((cells, cells), 0)
    b = iota((cells, cells), 1)
    lag = a - b if backward else b - a
    pos = jnp.maximum(lag, 0.0)
    shaped = rising(pos, 3) * jnp.exp(-pos * c_row) * gain_row
    return jnp.where(lag >= 0.0, shaped, 0.0)


def masked_rows(parts, y):
    rows = iota(parts[0].shape, 0)
    return jnp.concatenate([jnp.where(rows == float(y), p, 0.0) for p in parts], axis=0)


def lon_finals(c, leak, scale, cells, backward):
    x = iota(c.shape, 1)
    remain = x if backward else (cells - 1.0) - x
    decay = jnp.exp(-remain * c)
    return [leak ** (s + 1) * scale * rising(remain, s) * decay for s in range(4)]


def lon_entering(c, leak, cells, backward):
    x = iota(c.shape, 1)
    place = (cells - 1.0) - x if backward else x
    decay = jnp.exp(-(place + 1.0) * c)
    return [leak ** (3 - s) * rising(place, 3 - s) * decay for s in range(4)]


def lon_tables(lonc, rows, cells, backward, table_ref):
    c, leak, scale = lon_consts(lonc)
    gain = leak**4 * scale
    for y in range(rows):
        table_ref[y] = lon_kernel_matrix(c[y : y + 1], gain[y : y + 1], cells, backward)


def lon_local_rows(load_row, lonc, table_ref, rows, cells, backward, inside_ref, carried_ref):
    c, leak, scale = lon_consts(lonc)
    finals = lon_finals(c, leak, scale, cells, backward)
    carried = None
    for y in range(rows):
        f = load_row(y)
        inside_ref[y] = mm(f, table_ref[y], ((1,), (0,)))
        part = mm(masked_rows(finals, y), f, ((1,), (1,)))
        carried = part if carried is None else carried + part
    carried_ref[...] = carried


def lon_incoming_states(lonc, blocks, rows, cells):
    k = blocks[0].shape[1]
    n = len(blocks)
    c = jnp.broadcast_to(lonc[:, :1], (rows, k))
    leak = 1.0 - jnp.exp(-c)

    def trans(r):
        closing = jnp.exp(-float(r * cells) * c)
        return [choose(r * cells, i) * leak**i * closing for i in range(4)]

    total = [jnp.zeros((rows, k), f32) for _ in range(4)]
    for r in range(n):
        part = [blocks[r][s * rows : (s + 1) * rows] for s in range(4)]
        if r:
            t = trans(r)
            part = [sum(t[i - j] * part[j] for j in range(i + 1)) for i in range(4)]
        total = [a + b for a, b in zip(total, part)]
    t = trans(n)
    solved = []
    for i in range(4):
        v = total[i]
        for j in range(i):
            v = v + t[i - j] * solved[j]
        solved.append(v / (1.0 - t[0]))
    return jnp.concatenate(solved, axis=0)


def lon_correction(states_t, entering, y):
    return mm(states_t, masked_rows(entering, y), ((1,), (0,)))


def lat_consts(dec):
    q = jnp.exp(-dec)
    leak = 1.0 - q
    return q, leak, leak * (2.5 / jnp.sqrt(leak))


def lat_sweep(load, store, start, dec, rows, k, backward, block):
    q1, l1, g1 = lat_consts(dec)
    x = dec.shape[1]
    q = jnp.broadcast_to(q1, (block, x))
    leak = jnp.broadcast_to(l1, (block, x))
    gain = jnp.broadcast_to(g1, (block, x))
    order = range(rows - 1, -1, -1) if backward else range(rows)

    def step(i, carry):
        at = pl.ds(pl.multiple_of(i * block, 8), block)
        u = start(at)
        for y in order:
            feed = gain * load(y, at, i * block)
            u0 = q * u[0] + feed
            u1 = q * u[1] + leak * u0
            u2 = q * u[2] + leak * u1
            u3 = q * u[3] + leak * u2
            u = [u0, u1, u2, u3]
            store(y, at, i * block, u3, u if y == order[-1] else None)
        return carry

    lax.fori_loop(0, k // block, step, 0)


def swap_halves(a, b):
    half = a.shape[-1] // 2
    low = iota((1,) * (a.ndim - 1) + (a.shape[-1],), a.ndim - 1) < float(half)
    turn = lambda v: pltpu.roll(v, half, v.ndim - 1)
    return jnp.where(low, a, turn(b)), jnp.where(low, turn(a), b)


def both_halves(v):
    return swap_halves(v, v)


def lat_trans(dec, rows):
    leak = 1.0 - jnp.exp(-dec)
    closing = jnp.exp(-float(rows) * dec)
    return [choose(rows, i) * leak**i * closing for i in range(4)]


def entering_states(got, chunks):
    hops = len(got) // chunks

    def at(chunk, where):
        out = []
        for s in range(4):
            v = None
            for p in got[chunk * hops : (chunk + 1) * hops]:
                v = p[s, where, :] if v is None else v + p[s, where, :]
            out.append(v)
        return out

    return at


def sweep_chunks(load, store, start, dec, rows, k, chunks, backward):
    size = k // chunks
    for ch in range(chunks):
        lat_sweep(
            lambda y, at, base, ch=ch: load(y, ch * size + base),
            lambda y, at, base, value, last, ch=ch: store(y, ch, at, ch * size + base, value, last),
            lambda at, ch=ch: start(ch, at),
            dec,
            rows,
            size,
            backward,
            8,
        )


def member_blocks(members):
    for size in (5, 4, 2, 1):
        if members % size == 0:
            return size


def k_tables(rows, cells, dec_ref, lonc_ref, latc_ref, table_ref):
    row = jnp.broadcast_to(dec_ref[:1, :rows], (rows, rows))
    own = iota((rows, rows), 0) == iota((rows, rows), 1)
    column = jnp.sum(jnp.where(own, row, 0.0), axis=1, keepdims=True)
    lonc = jnp.broadcast_to(column, (rows, cells))
    lonc_ref[...] = lonc
    first, second = both_halves(jnp.broadcast_to(dec_ref[1:], (8, cells)))
    latc_ref[0] = first
    latc_ref[1] = second
    lon_tables(lonc, rows, cells, False, table_ref)


def k_lon_fwd(rows, k, cells, d_ref, lon_ref, table_ref, inside_ref, carried_ref):
    d_ref = d_ref.reshape(k * rows, cells)
    lon_local_rows(
        lambda y: d_ref[pl.ds(y, k, stride=rows), :],
        lon_ref[...],
        table_ref,
        rows,
        cells,
        False,
        inside_ref,
        carried_ref,
    )


def k_prepare(m_ref, lon_ref, a_ref, b_ref, table_ref):
    half = a_ref.shape[0]
    lon_tables(lon_ref[...], *lon_ref.shape, True, table_ref)

    def step(i, carry):
        a, b = swap_halves(m_ref[i].astype(f32), m_ref[i + half].astype(f32))
        a_ref[i] = a
        b_ref[i] = b
        return carry

    lax.fori_loop(0, half, step, 0)


def k_lat_first(rows, k, cells, n, chunks, *refs):
    inside_ref, lon_ref, lat_ref, *rest = refs
    blocks = [r[...] for r in rest[:n]]
    f_refs, out_refs = rest[n : n + 2], rest[n + 2 :]
    lonc = lon_ref[...]
    states = lon_incoming_states(lonc, blocks, rows, cells).T
    c, leak, _ = lon_consts(lonc)
    entering = lon_entering(c, leak, cells, False)
    half = k // 2
    for y in range(rows):
        row = inside_ref[y] + lon_correction(states, entering, y)
        f_refs[0][y], f_refs[1][y] = swap_halves(row[:half], row[half:])
    zero = jnp.zeros((8, cells), f32)
    for part, f_ref in enumerate(f_refs):

        def store(y, ch, at, base, value, last, part=part):
            if last is not None:
                for s in range(4):
                    out_refs[part * chunks + ch][s, at, :] = last[s]

        sweep_chunks(
            lambda y, base: f_ref[y, pl.ds(pl.multiple_of(base, 8), 8), :],
            store,
            lambda ch, at: [zero] * 4,
            lat_ref[part, :1],
            rows,
            half,
            chunks,
            False,
        )


def k_pass_on(rows, part, carried_ref, got_ref, lat_ref, out_ref):
    t = lat_trans(lat_ref[part, :1], rows)
    got = [got_ref[s] for s in range(4)]
    for i in range(4):
        v = carried_ref[i]
        for j in range(i + 1):
            v = v + t[i - j] * got[j]
        out_ref[i] = v


def active_pair(eig_ref, m, pairs, e, cells):
    low = iota((1, cells), 1) < float(cells // 2)
    first = jnp.where(e < eig_ref[m], 1.0, 0.0).astype(f32)
    second = jnp.where(e < eig_ref[m + pairs], 1.0, 0.0).astype(f32)
    return jnp.where(low, first, second)


def k_increment(rows, k, part, chunks, count, pairs, modes, levels, *refs):
    f_ref, lat_ref, m_ref, v_ref, eig_ref, *rest = refs
    out_ref, s_ref, inc_ref = rest[count:]
    cells = lat_ref.shape[-1]

    def store(y, ch, at, base, value, last):
        s_ref[pl.ds(base * rows + y, 8, stride=rows), :] = value

    sweep_chunks(
        lambda y, base: f_ref[y, pl.ds(pl.multiple_of(base, 8), 8), :],
        store,
        entering_states(rest[:count], chunks),
        lat_ref[part, :1],
        rows,
        k,
        chunks,
        False,
    )
    per = member_blocks(pairs)
    for b in range(pairs // per):
        fields = []
        for m in range(per):
            for e in range(modes):
                scale = active_pair(eig_ref, b * per + m, pairs, e, cells)
                at = ((b * per + m) * modes + e) * rows
                fields.append(s_ref[at : at + rows, :] * scale)

        def level(l, carry, b=b, fields=fields):
            total = None
            for m in range(per):
                p = None
                for e in range(modes):
                    t = v_ref[e, l] * fields[m * modes + e]
                    p = t if p is None else p + t
                p = m_ref[b * per + m, l] * p
                total = p if total is None else total + p
            if b == 0:
                inc_ref[l] = total
            else:
                inc_ref[l] += total
            return carry

        lax.fori_loop(0, levels, level, 0, unroll=4)
    half = levels // 2
    low = iota((1, 1, cells), 2) < float(cells // 2)
    full = inc_ref[...]
    full = full + pltpu.roll(full, cells // 2, 2)
    out_ref[...] = jnp.where(low, full[:half], full[half:])


def k_gradient(rows, k, part, chunks, pairs, modes, levels, *refs):
    inc_ref, got_ref, obs_ref, m_ref, v_ref, eig_ref, lat_ref, g_ref, *carried_refs, w_ref = refs
    cells = lat_ref.shape[-1]
    half = levels // 2
    first, second = both_halves(inc_ref[...] + got_ref[...])
    obs = both_halves(obs_ref[...])[part]
    w_ref[:half] = first * obs[:half]
    w_ref[half:] = second * obs[half:]
    per = member_blocks(pairs)
    for b in range(pairs // per):

        def level(l, acc, b=b):
            w = w_ref[l]
            vs = [v_ref[e, l] for e in range(modes)]
            out = []
            for m in range(per):
                t = m_ref[b * per + m, l] * w
                for e in range(modes):
                    out.append(acc[m * modes + e] + vs[e] * t)
            return tuple(out)

        zero = jnp.zeros((rows, cells), f32)
        acc = lax.fori_loop(0, levels, level, (zero,) * (per * modes), unroll=4)
        for m in range(per):
            for e in range(modes):
                scale = active_pair(eig_ref, b * per + m, pairs, e, cells)
                at = ((b * per + m) * modes + e) * rows
                g_ref[at : at + rows, :] = acc[m * modes + e] * scale
    zero8 = jnp.zeros((8, cells), f32)

    def store(y, ch, at, base, value, last):
        if last is not None:
            for s in range(4):
                carried_refs[ch][s, at, :] = last[s]

    sweep_chunks(
        lambda y, base: g_ref[pl.ds(base * rows + y, 8, stride=rows), :],
        store,
        lambda ch, at: [zero8] * 4,
        lat_ref[part, :1],
        rows,
        k,
        chunks,
        True,
    )


def k_lon_bwd(rows, k, cells, chunks, count, *refs):
    g_refs, lat_ref, lon_ref, table_ref, rest = refs[:2], refs[2], refs[3], refs[4], refs[5:]
    inside_ref, carried_ref, p_ref = rest[2 * count :]
    half = k // 2
    for part in range(2):
        g_ref = g_refs[part]

        def store(y, ch, at, base, value, last, part=part):
            p_ref[part, y, pl.ds(pl.multiple_of(base, 8), 8), :] = value

        sweep_chunks(
            lambda y, base: g_ref[pl.ds(base * rows + y, 8, stride=rows), :],
            store,
            entering_states(rest[part * count : (part + 1) * count], chunks),
            lat_ref[part, :1],
            rows,
            half,
            chunks,
            True,
        )

    def load_row(y):
        return jnp.concatenate(swap_halves(p_ref[0, y], p_ref[1, y]), axis=0)

    lon_local_rows(load_row, lon_ref[...], table_ref, rows, cells, True, inside_ref, carried_ref)


def k_sums(rows, k, cells, n, *refs):
    inside_ref, lon_ref, d_ref, r_ref, *rest = refs
    d_ref = d_ref.reshape(k * rows, cells)
    r_ref = r_ref.reshape(k * rows, cells)
    blocks = [r[...] for r in rest[:n]]
    h_ref, sums_ref = rest[n:]
    lonc = lon_ref[...]
    states = lon_incoming_states(lonc, blocks, rows, cells).T
    c, leak, _ = lon_consts(lonc)
    entering = lon_entering(c, leak, cells, True)
    for y in range(rows):
        at = pl.ds(y, k, stride=rows)
        h_ref[at, :] = inside_ref[y] + lon_correction(states, entering, y)
    block = 64
    zero = jnp.zeros((8, cells), f32)

    def step(i, acc):
        at = pl.ds(pl.multiple_of(i * block, 8), block)
        d = d_ref[at, :]
        r = r_ref[at, :]
        h = h_ref[at, :] + d
        h_ref[at, :] = h
        fold = lambda v: v.reshape(block // 8, 8, cells).sum(axis=0)
        return (acc[0] + fold(r * r), acc[1] + fold(d * h), acc[2] + fold(r * h), acc[3] + fold(h * h))

    acc = lax.fori_loop(0, (k * rows) // block, step, (zero,) * 4)
    out = [a.sum(axis=0, keepdims=True) for a in acc]
    sums_ref[...] = jnp.concatenate(out + [jnp.zeros((4, cells), f32)], axis=0)


def k_update(sums_ref, control_ref, r_ref, d_ref, h_ref, nc_ref, nr_ref, nd_ref):
    sums = jnp.sum(sums_ref[...], axis=1, keepdims=True)
    rr, dh, rh, hh = (sums[i : i + 1].reshape(1, 1, 1) for i in range(4))
    step = rr / dh
    norm_new = rr - 2.0 * step * rh + step * step * hh
    beta = norm_new / rr
    d = d_ref[...]
    nr = r_ref[...] - step * h_ref[...]
    nc_ref[...] = control_ref[...] + step * d
    nr_ref[...] = nr
    nd_ref[...] = nr + beta * d


def call(body, outs, ins, specs=None, scratch=(), name=None, cost=None):
    return pl.pallas_call(
        body,
        out_shape=outs,
        in_specs=specs or [VM] * len(ins),
        out_specs=jax.tree.map(lambda _: VM, outs),
        scratch_shapes=scratch,
        name=name,
        cost_estimate=None if cost is None else pl.CostEstimate(flops=cost, bytes_accessed=1000, transcendentals=0),
        compiler_params=pltpu.CompilerParams(vmem_limit_bytes=16 * 1024 * 1024),
    )(*ins)


def sds(*shape):
    return jax.ShapeDtypeStruct(shape, f32)


def lon_exchange(carried, backward):
    n = lax.axis_size("lon")
    sign = -1 if backward else 1
    got = [
        lax.ppermute(carried, "lon", [(j, (j + sign * r) % n) for j in range(n)]) for r in range(1, n)
    ]
    return got + [carried]


def pass_on(part, got, latc, rows, c):
    return call(functools.partial(k_pass_on, rows, c), sds(*part.shape), [part, got, latc], name="pass_on")


def lat_carry(halves, latc, rows, backward):
    n = lax.axis_size("lat")
    at = (lambda i: n - 1 - i) if backward else (lambda i: i)
    got = [[[] for _ in chunks] for chunks in halves]
    for h in range(n - 1):
        for c, chunks in enumerate(halves):
            for i, part in enumerate(chunks):
                v = pass_on(part, got[c][i][-1], latc, rows, c) if h else part
                got[c][i].append(lax.ppermute(v, "lat", [(at(h), at(h + 1))]))
    return [[g for chunk in half for g in chunk] for half in got]


def all_sum(v, axes, steps):
    total = 1
    for a in axes:
        total *= lax.axis_size(a)
    masks = [0]
    for s in steps:
        masks = masks + [m ^ s for m in masks]
    got = [lax.ppermute(v, axes, [(i, i ^ m) for i in range(total)]) for m in masks[1:]]
    for g in got:
        v = v + g
    return v


def powers(n):
    out, d = [], 1
    while d < n:
        out.append(d)
        d *= 2
    return out


def reduce_everywhere(v):
    n_lon, n_lat, n_mem = (lax.axis_size(a) for a in ("lon", "lat", "mem"))
    for s in powers(n_mem):
        v = all_sum(v, ("mem",), [s])
    for s in powers(n_lon):
        v = all_sum(v, ("lon",), [s])
    lat = powers(n_lat)
    for i in range(0, len(lat), 2):
        v = all_sum(v, ("lat",), lat[i : i + 2])
    return v


def body(control, residual, direction, members, vert_modes, eig_count, lon_decay, lat_decay, obs_weight):
    k, rows, cells = direction.shape
    mcount, levels = members.shape[:2]
    modes = vert_modes.shape[0]
    n_lon, n_mem = lax.axis_size("lon"), lax.axis_size("mem")
    half = k // 2
    pairs = mcount // 2
    chunks = 2
    states = (sds(4, half // chunks, cells),) * chunks

    decays = jnp.stack([jnp.pad(lon_decay, (0, cells - rows)), lat_decay])
    lonc, latc, tables = call(
        functools.partial(k_tables, rows, cells),
        (sds(rows, cells), sds(2, 8, cells), sds(rows, cells, cells)),
        [decays],
        name="tables",
        cost=10**9,
    )
    inside, carried = call(
        functools.partial(k_lon_fwd, rows, k, cells),
        (sds(rows, k, cells), sds(4 * rows, k)),
        [direction, lonc, tables],
        name="lon_fwd",
    )
    *packed, back_tables = call(
        k_prepare,
        (sds(pairs, levels, rows, cells),) * 2 + (sds(rows, cells, cells),),
        [members, lonc],
        name="prepare",
        cost=10**9,
    )
    blocks = lon_exchange(carried, False)
    fa, fb, *parts = call(
        functools.partial(k_lat_first, rows, k, cells, n_lon, chunks),
        (sds(rows, half, cells),) * 2 + states * 2,
        [inside, lonc, latc, *blocks],
        name="lat_first",
    )
    got = lat_carry([parts[:chunks], parts[chunks:]], latc, rows, False)
    count = len(got[0])
    fields = (fa, fb)
    inc = [None, None]
    for part in range(2):
        inc[part] = call(
            functools.partial(k_increment, rows, half, part, chunks, count, pairs, modes, levels),
            sds(levels // 2, rows, cells),
            [fields[part], latc, packed[part], vert_modes, eig_count, *got[part]],
            specs=[VM, VM, VM, SM, SM] + [VM] * count,
            scratch=[pltpu.VMEM((half * rows, cells), f32), pltpu.VMEM((levels, rows, cells), f32)],
            name="increment",
        )
    grads, sends = [None, None], [None, None]
    for part in range(2):
        v = inc[part]
        step = 1
        while step * 2 < n_mem:
            v = v + lax.ppermute(v, "mem", [(i, i ^ step) for i in range(n_mem)])
            step *= 2
        other = lax.ppermute(v, "mem", [(i, i ^ step) for i in range(n_mem)])
        grads[part], *sends[part] = call(
            functools.partial(k_gradient, rows, half, part, chunks, pairs, modes, levels),
            (sds(half * rows, cells),) + states,
            [v, other, obs_weight, packed[part], vert_modes, eig_count, latc],
            specs=[VM, VM, VM, VM, SM, SM, VM],
            scratch=[pltpu.VMEM((levels, rows, cells), f32)],
            name="gradient",
        )
    got = lat_carry(sends, latc, rows, True)
    inside, carried = call(
        functools.partial(k_lon_bwd, rows, k, cells, chunks, count),
        (sds(rows, k, cells), sds(4 * rows, k)),
        [*grads, latc, lonc, back_tables, *got[0], *got[1]],
        scratch=[pltpu.VMEM((2, rows, half, cells), f32)],
        name="lon_bwd",
    )
    blocks = lon_exchange(carried, True)
    h, sums = call(
        functools.partial(k_sums, rows, k, cells, n_lon),
        (sds(k * rows, cells), sds(8, cells)),
        [inside, lonc, direction, residual, *blocks],
        name="sums",
    )
    sums = reduce_everywhere(sums)
    outs = call(
        k_update,
        (sds(k, rows, cells),) * 3,
        [sums, control, residual, direction, h.reshape(k, rows, cells)],
        name="update",
    )
    return tuple(outs)


def solution(mesh):
    field = P("mem", "lat", "lon")
    placed = (
        field,
        field,
        field,
        P("mem", None, "lat", "lon"),
        P(),
        P("mem"),
        P("lat"),
        P("lon"),
        P(None, "lat", "lon"),
    )
    return jax.shard_map(body, mesh=mesh, in_specs=placed, out_specs=(field,) * 3, check_vma=False)
```

```python
import functools
import jax
import jax.numpy as jnp
from jax import lax
from jax.experimental import pallas as pl
from jax.experimental.pallas import tpu as pltpu
from jax.sharding import PartitionSpec as P

f32 = jnp.float32
bf16 = jnp.bfloat16
VM = pl.BlockSpec(memory_space=pltpu.VMEM)
SM = pl.BlockSpec(memory_space=pltpu.SMEM)


def choose(length, i):
    r = 1.0
    for k in range(i):
        r = r * (length + k) / (k + 1)
    return r


def rising(v, degree):
    r = jnp.ones_like(v)
    for k in range(degree):
        r = r * (v + (k + 1.0)) * (1.0 / (k + 1.0))
    return r


def halves(v):
    high = v.astype(bf16)
    return high, (v - high.astype(f32)).astype(bf16)


def left3(v, axis):
    high, low = halves(v)
    return jnp.concatenate([high, low, high], axis=axis)


def right3(v, axis):
    high, low = halves(v)
    return jnp.concatenate([high, high, low], axis=axis)


def product3(a, b):
    return jnp.dot(a, b, preferred_element_type=f32)


def iota(shape, dim):
    return lax.broadcasted_iota(jnp.int32, shape, dim).astype(f32)


def lon_consts(lonc):
    c = lonc
    q = jnp.exp(-c)
    leak = 1.0 - q
    return c, leak, 2.5 / jnp.sqrt(leak)


def lon_kernel_matrix(c_row, gain_row, cells, backward):
    a = iota((cells, cells), 0)
    b = iota((cells, cells), 1)
    lag = a - b if backward else b - a
    pos = jnp.maximum(lag, 0.0)
    shaped = rising(pos, 3) * jnp.exp(-pos * c_row) * gain_row
    return jnp.where(lag >= 0.0, shaped, 0.0)


def masked_rows(parts, y):
    rows = iota(parts[0].shape, 0)
    return jnp.concatenate([jnp.where(rows == float(y), p, 0.0) for p in parts], axis=0)


def lon_finals(c, leak, scale, cells, backward):
    x = iota(c.shape, 1)
    remain = x if backward else (cells - 1.0) - x
    decay = jnp.exp(-remain * c)
    return [leak ** (s + 1) * scale * rising(remain, s) * decay for s in range(4)]


def lon_entering(c, leak, cells, backward):
    x = iota(c.shape, 1)
    place = (cells - 1.0) - x if backward else x
    decay = jnp.exp(-(place + 1.0) * c)
    return [leak ** (3 - s) * rising(place, 3 - s) * decay for s in range(4)]


def lon_tables(lonc, rows, cells, backward, table_ref):
    c, leak, scale = lon_consts(lonc)
    gain = leak**4 * scale
    finals = lon_finals(c, leak, scale, cells, backward)
    spare = jnp.zeros((cells - 4 * rows, cells), f32)
    finals = jnp.concatenate(finals + [spare], axis=0).T
    column = lax.broadcasted_iota(jnp.int32, (cells, cells), 1)
    for y in range(rows):
        inside = lon_kernel_matrix(c[y : y + 1], gain[y : y + 1], cells, backward)
        leaving = jnp.where(lax.rem(column, rows) == y, finals, 0.0)
        table_ref[y] = right3(jnp.concatenate([inside, leaving], axis=1), 0)


def lon_local_rows(load_row, table_ref, rows, cells, inside_ref, carried_ref):
    carried = None
    for y in range(rows):
        both = product3(left3(load_row(y), 1), table_ref[y])
        inside_ref[y] = both[:, :cells]
        carried = both[:, cells:] if carried is None else carried + both[:, cells:]
    carried_ref[...] = carried.T[: 4 * rows]


def lon_incoming_states(lonc, blocks, rows, cells):
    k = blocks[0].shape[1]
    n = len(blocks)
    c = jnp.broadcast_to(lonc[:, :1], (rows, k))
    leak = 1.0 - jnp.exp(-c)

    def trans(r):
        closing = jnp.exp(-float(r * cells) * c)
        return [choose(r * cells, i) * leak**i * closing for i in range(4)]

    total = [jnp.zeros((rows, k), f32) for _ in range(4)]
    for r in range(n):
        part = [blocks[r][s * rows : (s + 1) * rows] for s in range(4)]
        if r:
            t = trans(r)
            part = [sum(t[i - j] * part[j] for j in range(i + 1)) for i in range(4)]
        total = [a + b for a, b in zip(total, part)]
    t = trans(n)
    solved = []
    for i in range(4):
        v = total[i]
        for j in range(i):
            v = v + t[i - j] * solved[j]
        solved.append(v / (1.0 - t[0]))
    return jnp.concatenate(solved, axis=0)


def lon_correction(states, entering, rows, cells):
    high = states.astype(bf16).astype(f32)
    low = states - high
    spare = jnp.zeros((cells - 12 * rows, states.shape[1]), f32)
    left = jnp.concatenate([high, low, high, spare], axis=0).T.astype(bf16)
    spare = jnp.zeros((cells - 12 * rows, cells), bf16)
    return lambda y: product3(left, jnp.concatenate([right3(masked_rows(entering, y), 0), spare], axis=0))


def lat_consts(dec):
    q = jnp.exp(-dec)
    leak = 1.0 - q
    return q, leak, leak * (2.5 / jnp.sqrt(leak))


def lat_sweep(load, store, start, dec, rows, k, backward, block):
    q1, l1, g1 = lat_consts(dec)
    x = dec.shape[1]
    q = jnp.broadcast_to(q1, (block, x))
    leak = jnp.broadcast_to(l1, (block, x))
    gain = jnp.broadcast_to(g1, (block, x))
    order = range(rows - 1, -1, -1) if backward else range(rows)

    def step(i, carry):
        at = pl.ds(pl.multiple_of(i * block, 8), block)
        u = start(at)
        for y in order:
            feed = gain * load(y, at, i * block)
            u0 = q * u[0] + feed
            u1 = q * u[1] + leak * u0
            u2 = q * u[2] + leak * u1
            u3 = q * u[3] + leak * u2
            u = [u0, u1, u2, u3]
            store(y, at, i * block, u3, u if y == order[-1] else None)
        return carry

    lax.fori_loop(0, k // block, step, 0)


def swap_halves(a, b):
    half = a.shape[-1] // 2
    low = iota((1,) * (a.ndim - 1) + (a.shape[-1],), a.ndim - 1) < float(half)
    turn = lambda v: pltpu.roll(v, half, v.ndim - 1)
    return jnp.where(low, a, turn(b)), jnp.where(low, turn(a), b)


def both_halves(v):
    return swap_halves(v, v)


def lat_trans(dec, rows):
    leak = 1.0 - jnp.exp(-dec)
    closing = jnp.exp(-float(rows) * dec)
    return [choose(rows, i) * leak**i * closing for i in range(4)]


def entering_states(got, chunks):
    hops = len(got) // chunks

    def at(chunk, where):
        out = []
        for s in range(4):
            v = None
            for p in got[chunk * hops : (chunk + 1) * hops]:
                v = p[s, where, :] if v is None else v + p[s, where, :]
            out.append(v)
        return out

    return at


def sweep_chunks(load, store, start, dec, rows, k, chunks, backward):
    size = k // chunks
    for ch in range(chunks):
        lat_sweep(
            lambda y, at, base, ch=ch: load(y, ch * size + base),
            lambda y, at, base, value, last, ch=ch: store(y, ch, at, ch * size + base, value, last),
            lambda at, ch=ch: start(ch, at),
            dec,
            rows,
            size,
            backward,
            8,
        )


def member_blocks(members):
    for size in (5, 4, 2, 1):
        if members % size == 0:
            return size


def k_tables(rows, cells, dec_ref, lonc_ref, latc_ref, table_ref):
    row = jnp.broadcast_to(dec_ref[:, cells:], (rows, rows))
    own = iota((rows, rows), 0) == iota((rows, rows), 1)
    column = jnp.sum(jnp.where(own, row, 0.0), axis=1, keepdims=True)
    lonc = jnp.broadcast_to(column, (rows, cells))
    lonc_ref[...] = lonc
    first, second = both_halves(jnp.broadcast_to(dec_ref[:, :cells], (8, cells)))
    latc_ref[0] = first
    latc_ref[1] = second
    lon_tables(lonc, rows, cells, False, table_ref)


def k_lon_fwd(rows, k, cells, d_ref, table_ref, inside_ref, carried_ref):
    d_ref = d_ref.reshape(k * rows, cells)
    lon_local_rows(
        lambda y: d_ref[pl.ds(y, k, stride=rows), :], table_ref, rows, cells, inside_ref, carried_ref
    )


def k_prepare(m_ref, lon_ref, a_ref, b_ref, table_ref):
    half = a_ref.shape[0]
    lon_tables(lon_ref[...], *lon_ref.shape, True, table_ref)

    def step(i, carry):
        a, b = swap_halves(m_ref[i].astype(f32), m_ref[i + half].astype(f32))
        a_ref[i] = a
        b_ref[i] = b
        return carry

    lax.fori_loop(0, half, step, 0)


def k_lat_first(rows, k, cells, n, chunks, *refs):
    inside_ref, lon_ref, lat_ref, *rest = refs
    blocks = [r[...] for r in rest[:n]]
    f_refs, out_refs = rest[n : n + 2], rest[n + 2 :]
    lonc = lon_ref[...]
    states = lon_incoming_states(lonc, blocks, rows, cells)
    c, leak, _ = lon_consts(lonc)
    added = lon_correction(states, lon_entering(c, leak, cells, False), rows, cells)
    half = k // 2
    for y in range(rows):
        row = inside_ref[y] + added(y)
        f_refs[0][y], f_refs[1][y] = swap_halves(row[:half], row[half:])
    zero = jnp.zeros((8, cells), f32)
    for part, f_ref in enumerate(f_refs):

        def store(y, ch, at, base, value, last, part=part):
            if last is not None:
                for s in range(4):
                    out_refs[part * chunks + ch][s, at, :] = last[s]

        sweep_chunks(
            lambda y, base: f_ref[y, pl.ds(pl.multiple_of(base, 8), 8), :],
            store,
            lambda ch, at: [zero] * 4,
            lat_ref[part, :1],
            rows,
            half,
            chunks,
            False,
        )


def k_pass_on(rows, part, carried_ref, got_ref, lat_ref, out_ref):
    t = lat_trans(lat_ref[part, :1], rows)
    got = [got_ref[s] for s in range(4)]
    for i in range(4):
        v = carried_ref[i]
        for j in range(i + 1):
            v = v + t[i - j] * got[j]
        out_ref[i] = v


def active_pair(eig_ref, m, pairs, e, cells):
    low = iota((1, cells), 1) < float(cells // 2)
    first = jnp.where(e < eig_ref[m], 1.0, 0.0).astype(f32)
    second = jnp.where(e < eig_ref[m + pairs], 1.0, 0.0).astype(f32)
    return jnp.where(low, first, second)


def k_increment(rows, k, part, chunks, count, pairs, modes, levels, *refs):
    f_ref, lat_ref, m_ref, v_ref, eig_ref, *rest = refs
    out_ref, s_ref, inc_ref = rest[count:]
    cells = lat_ref.shape[-1]

    def store(y, ch, at, base, value, last):
        s_ref[pl.ds(base * rows + y, 8, stride=rows), :] = value

    sweep_chunks(
        lambda y, base: f_ref[y, pl.ds(pl.multiple_of(base, 8), 8), :],
        store,
        entering_states(rest[:count], chunks),
        lat_ref[part, :1],
        rows,
        k,
        chunks,
        False,
    )
    per = member_blocks(pairs)
    for b in range(pairs // per):
        fields = []
        for m in range(per):
            for e in range(modes):
                scale = active_pair(eig_ref, b * per + m, pairs, e, cells)
                at = ((b * per + m) * modes + e) * rows
                fields.append(s_ref[at : at + rows, :] * scale)

        def level(l, carry, b=b, fields=fields):
            total = None
            for m in range(per):
                p = None
                for e in range(modes):
                    t = v_ref[e, l] * fields[m * modes + e]
                    p = t if p is None else p + t
                p = m_ref[b * per + m, l] * p
                total = p if total is None else total + p
            if b == 0:
                inc_ref[l] = total
            else:
                inc_ref[l] += total
            return carry

        lax.fori_loop(0, levels, level, 0, unroll=4)
    half = levels // 2
    low = iota((1, 1, cells), 2) < float(cells // 2)
    full = inc_ref[...]
    full = full + pltpu.roll(full, cells // 2, 2)
    out_ref[...] = jnp.where(low, full[:half], full[half:])


def k_gradient(rows, k, part, chunks, pairs, modes, levels, *refs):
    inc_ref, got_ref, obs_ref, m_ref, v_ref, eig_ref, lat_ref, g_ref, *carried_refs, w_ref = refs
    cells = lat_ref.shape[-1]
    half = levels // 2
    first, second = both_halves(inc_ref[...] + got_ref[...])
    obs = both_halves(obs_ref[...])[part]
    w_ref[:half] = first * obs[:half]
    w_ref[half:] = second * obs[half:]
    per = member_blocks(pairs)
    for b in range(pairs // per):

        def level(l, acc, b=b):
            w = w_ref[l]
            vs = [v_ref[e, l] for e in range(modes)]
            out = []
            for m in range(per):
                t = m_ref[b * per + m, l] * w
                for e in range(modes):
                    out.append(acc[m * modes + e] + vs[e] * t)
            return tuple(out)

        zero = jnp.zeros((rows, cells), f32)
        acc = lax.fori_loop(0, levels, level, (zero,) * (per * modes), unroll=4)
        for m in range(per):
            for e in range(modes):
                scale = active_pair(eig_ref, b * per + m, pairs, e, cells)
                at = ((b * per + m) * modes + e) * rows
                g_ref[at : at + rows, :] = acc[m * modes + e] * scale
    zero8 = jnp.zeros((8, cells), f32)

    def store(y, ch, at, base, value, last):
        if last is not None:
            for s in range(4):
                carried_refs[ch][s, at, :] = last[s]

    sweep_chunks(
        lambda y, base: g_ref[pl.ds(base * rows + y, 8, stride=rows), :],
        store,
        lambda ch, at: [zero8] * 4,
        lat_ref[part, :1],
        rows,
        k,
        chunks,
        True,
    )


def k_lon_bwd(rows, k, cells, chunks, count, *refs):
    g_refs, lat_ref, table_ref, rest = refs[:2], refs[2], refs[3], refs[4:]
    inside_ref, carried_ref, p_ref = rest[2 * count :]
    half = k // 2
    for part in range(2):
        g_ref = g_refs[part]

        def store(y, ch, at, base, value, last, part=part):
            p_ref[part, y, pl.ds(pl.multiple_of(base, 8), 8), :] = value

        sweep_chunks(
            lambda y, base: g_ref[pl.ds(base * rows + y, 8, stride=rows), :],
            store,
            entering_states(rest[part * count : (part + 1) * count], chunks),
            lat_ref[part, :1],
            rows,
            half,
            chunks,
            True,
        )

    def load_row(y):
        return jnp.concatenate(swap_halves(p_ref[0, y], p_ref[1, y]), axis=0)

    lon_local_rows(load_row, table_ref, rows, cells, inside_ref, carried_ref)


def k_sums(rows, k, cells, n, *refs):
    inside_ref, lon_ref, d_ref, r_ref, *rest = refs
    d_ref = d_ref.reshape(k * rows, cells)
    r_ref = r_ref.reshape(k * rows, cells)
    blocks = [r[...] for r in rest[:n]]
    h_ref, sums_ref = rest[n:]
    lonc = lon_ref[...]
    states = lon_incoming_states(lonc, blocks, rows, cells)
    c, leak, _ = lon_consts(lonc)
    added = lon_correction(states, lon_entering(c, leak, cells, True), rows, cells)
    for y in range(rows):
        at = pl.ds(y, k, stride=rows)
        h_ref[at, :] = inside_ref[y] + added(y)
    block = 64
    zero = jnp.zeros((8, cells), f32)

    def step(i, acc):
        at = pl.ds(pl.multiple_of(i * block, 8), block)
        d = d_ref[at, :]
        r = r_ref[at, :]
        h = h_ref[at, :] + d
        h_ref[at, :] = h
        fold = lambda v: v.reshape(block // 8, 8, cells).sum(axis=0)
        return (acc[0] + fold(r * r), acc[1] + fold(d * h), acc[2] + fold(r * h), acc[3] + fold(h * h))

    acc = lax.fori_loop(0, (k * rows) // block, step, (zero,) * 4)
    out = [a.sum(axis=0, keepdims=True) for a in acc]
    sums_ref[...] = jnp.concatenate(out + [jnp.zeros((4, cells), f32)], axis=0)


def k_update(pieces, sums_ref, control_ref, r_ref, d_ref, h_ref, *rest):
    outs, news, sems = rest[:3], rest[3:6], rest[6]
    sums = jnp.sum(sums_ref[...], axis=1, keepdims=True)
    rr, dh, rh, hh = (sums[i : i + 1].reshape(1, 1, 1) for i in range(4))
    step = rr / dh
    norm_new = rr - 2.0 * step * rh + step * step * hh
    beta = norm_new / rr
    size = d_ref.shape[0] // pieces
    copies = []
    for i in range(pieces):
        at = pl.ds(i * size, size)
        d = d_ref[at]
        nr = r_ref[at] - step * h_ref[at]
        for j, v in enumerate((control_ref[at] + step * d, nr, nr + beta * d)):
            news[j][at] = v
            copy = pltpu.make_async_copy(news[j].at[at], outs[j].at[at], sems.at[j, i])
            copy.start()
            copies.append(copy)
    for copy in copies:
        copy.wait()


def call(body, outs, ins, specs=None, out_specs=None, scratch=(), name=None, cost=None):
    return pl.pallas_call(
        body,
        out_shape=outs,
        in_specs=specs or [VM] * len(ins),
        out_specs=out_specs or jax.tree.map(lambda _: VM, outs),
        scratch_shapes=scratch,
        name=name,
        cost_estimate=None if cost is None else pl.CostEstimate(flops=cost, bytes_accessed=1000, transcendentals=0),
        compiler_params=pltpu.CompilerParams(vmem_limit_bytes=16 * 1024 * 1024),
    )(*ins)


def sds(*shape):
    return jax.ShapeDtypeStruct(shape, f32)


def lon_exchange(carried, backward):
    n = lax.axis_size("lon")
    sign = -1 if backward else 1
    got = [
        lax.ppermute(carried, "lon", [(j, (j + sign * r) % n) for j in range(n)]) for r in range(1, n)
    ]
    return got + [carried]


def pass_on(part, got, latc, rows, c):
    return call(functools.partial(k_pass_on, rows, c), sds(*part.shape), [part, got, latc], name="pass_on")


def lat_carry(halves, latc, rows, backward):
    n = lax.axis_size("lat")
    at = (lambda i: n - 1 - i) if backward else (lambda i: i)
    got = [[[] for _ in chunks] for chunks in halves]
    for h in range(n - 1):
        for c, chunks in enumerate(halves):
            for i, part in enumerate(chunks):
                v = pass_on(part, got[c][i][-1], latc, rows, c) if h else part
                got[c][i].append(lax.ppermute(v, "lat", [(at(h), at(h + 1))]))
    return [[g for chunk in half for g in chunk] for half in got]


def all_sum(v, axes, steps):
    total = 1
    for a in axes:
        total *= lax.axis_size(a)
    masks = [0]
    for s in steps:
        masks = masks + [m ^ s for m in masks]
    got = [lax.ppermute(v, axes, [(i, i ^ m) for i in range(total)]) for m in masks[1:]]
    for g in got:
        v = v + g
    return v


def powers(n):
    out, d = [], 1
    while d < n:
        out.append(d)
        d *= 2
    return out


def reduce_everywhere(v):
    n_lon, n_lat, n_mem = (lax.axis_size(a) for a in ("lon", "lat", "mem"))
    for s in powers(n_mem):
        v = all_sum(v, ("mem",), [s])
    for s in powers(n_lon):
        v = all_sum(v, ("lon",), [s])
    lat = powers(n_lat)
    for i in range(0, len(lat), 2):
        v = all_sum(v, ("lat",), lat[i : i + 2])
    return v


def body(control, residual, direction, members, vert_modes, eig_count, lon_decay, lat_decay, obs_weight):
    k, rows, cells = direction.shape
    mcount, levels = members.shape[:2]
    modes = vert_modes.shape[0]
    n_lon, n_mem = lax.axis_size("lon"), lax.axis_size("mem")
    half = k // 2
    pairs = mcount // 2
    chunks = 2
    states = (sds(4, half // chunks, cells),) * chunks

    decays = jnp.concatenate([lat_decay, lon_decay]).reshape(1, cells + rows)
    lonc, latc, tables = call(
        functools.partial(k_tables, rows, cells),
        (sds(rows, cells), sds(2, 8, cells), jax.ShapeDtypeStruct((rows, 3 * cells, 2 * cells), bf16)),
        [decays],
        name="tables",
        cost=10**9,
    )
    inside, carried = call(
        functools.partial(k_lon_fwd, rows, k, cells),
        (sds(rows, k, cells), sds(4 * rows, k)),
        [direction, tables],
        name="lon_fwd",
    )
    *packed, back_tables = call(
        k_prepare,
        (sds(pairs, levels, rows, cells),) * 2 + (jax.ShapeDtypeStruct((rows, 3 * cells, 2 * cells), bf16),),
        [members, lonc],
        name="prepare",
        cost=10**9,
    )
    blocks = lon_exchange(carried, False)
    fa, fb, *parts = call(
        functools.partial(k_lat_first, rows, k, cells, n_lon, chunks),
        (sds(rows, half, cells),) * 2 + states * 2,
        [inside, lonc, latc, *blocks],
        name="lat_first",
    )
    got = lat_carry([parts[:chunks], parts[chunks:]], latc, rows, False)
    count = len(got[0])
    fields = (fa, fb)
    inc = [None, None]
    for part in range(2):
        inc[part] = call(
            functools.partial(k_increment, rows, half, part, chunks, count, pairs, modes, levels),
            sds(levels // 2, rows, cells),
            [fields[part], latc, packed[part], vert_modes, eig_count, *got[part]],
            specs=[VM, VM, VM, SM, SM] + [VM] * count,
            scratch=[pltpu.VMEM((half * rows, cells), f32), pltpu.VMEM((levels, rows, cells), f32)],
            name="increment",
        )
    grads, sends = [None, None], [None, None]
    for part in range(2):
        v = inc[part]
        step = 1
        while step * 2 < n_mem:
            v = v + lax.ppermute(v, "mem", [(i, i ^ step) for i in range(n_mem)])
            step *= 2
        other = lax.ppermute(v, "mem", [(i, i ^ step) for i in range(n_mem)])
        grads[part], *sends[part] = call(
            functools.partial(k_gradient, rows, half, part, chunks, pairs, modes, levels),
            (sds(half * rows, cells),) + states,
            [v, other, obs_weight, packed[part], vert_modes, eig_count, latc],
            specs=[VM, VM, VM, VM, SM, SM, VM],
            scratch=[pltpu.VMEM((levels, rows, cells), f32)],
            name="gradient",
        )
    got = lat_carry(sends, latc, rows, True)
    inside, carried = call(
        functools.partial(k_lon_bwd, rows, k, cells, chunks, count),
        (sds(rows, k, cells), sds(4 * rows, k)),
        [*grads, latc, back_tables, *got[0], *got[1]],
        scratch=[pltpu.VMEM((2, rows, half, cells), f32)],
        name="lon_bwd",
    )
    blocks = lon_exchange(carried, True)
    h, sums = call(
        functools.partial(k_sums, rows, k, cells, n_lon),
        (sds(k * rows, cells), sds(8, cells)),
        [inside, lonc, direction, residual, *blocks],
        name="sums",
    )
    sums = reduce_everywhere(sums)
    pieces = 4 if k % 4 == 0 else 1
    outs = call(
        functools.partial(k_update, pieces),
        (sds(k, rows, cells),) * 3,
        [sums, control, residual, direction, h.reshape(k, rows, cells)],
        out_specs=(pl.BlockSpec(memory_space=pl.ANY),) * 3,
        scratch=[pltpu.VMEM((k, rows, cells), f32)] * 3 + [pltpu.SemaphoreType.DMA((3, pieces))],
        name="update",
    )
    return tuple(outs)


def solution(mesh):
    field = P("mem", "lat", "lon")
    placed = (
        field,
        field,
        field,
        P("mem", None, "lat", "lon"),
        P(),
        P("mem"),
        P("lat"),
        P("lon"),
        P(None, "lat", "lon"),
    )
    return jax.shard_map(body, mesh=mesh, in_specs=placed, out_specs=(field,) * 3, check_vma=False)
```

```python
import functools
import jax
import jax.numpy as jnp
from jax import lax
from jax.experimental import pallas as pl
from jax.experimental.pallas import tpu as pltpu
from jax.sharding import PartitionSpec as P


f32 = jnp.float32
bf16 = jnp.bfloat16
VM = pl.BlockSpec(memory_space=pltpu.VMEM)
SM = pl.BlockSpec(memory_space=pltpu.SMEM)


def choose(length, i):
    r = 1.0
    for k in range(i):
        r = r * (length + k) / (k + 1)
    return r


def rising(v, degree):
    r = jnp.ones_like(v)
    for k in range(degree):
        r = r * (v + (k + 1.0)) * (1.0 / (k + 1.0))
    return r


def halves(v):
    high = v.astype(bf16)
    return high, (v - high.astype(f32)).astype(bf16)


def left3(v, axis):
    high, low = halves(v)
    return jnp.concatenate([high, low, high], axis=axis)


def right3(v, axis):
    high, low = halves(v)
    return jnp.concatenate([high, high, low], axis=axis)


def product3(a, b):
    return jnp.dot(a, b, preferred_element_type=f32)


def iota(shape, dim):
    return lax.broadcasted_iota(jnp.int32, shape, dim).astype(f32)


def lon_consts(lonc):
    c = lonc
    q = jnp.exp(-c)
    leak = 1.0 - q
    return c, leak, 2.5 / jnp.sqrt(leak)


def lon_kernel_matrix(c_row, gain_row, cells, backward):
    a = iota((cells, cells), 0)
    b = iota((cells, cells), 1)
    lag = a - b if backward else b - a
    pos = jnp.maximum(lag, 0.0)
    shaped = rising(pos, 3) * jnp.exp(-pos * c_row) * gain_row
    return jnp.where(lag >= 0.0, shaped, 0.0)


def masked_rows(parts, y):
    rows = iota(parts[0].shape, 0)
    return jnp.concatenate([jnp.where(rows == float(y), p, 0.0) for p in parts], axis=0)


def lon_finals(c, leak, scale, cells, backward):
    x = iota(c.shape, 1)
    remain = x if backward else (cells - 1.0) - x
    decay = jnp.exp(-remain * c)
    return [leak ** (s + 1) * scale * rising(remain, s) * decay for s in range(4)]


def lon_entering(c, leak, cells, backward):
    x = iota(c.shape, 1)
    place = (cells - 1.0) - x if backward else x
    decay = jnp.exp(-(place + 1.0) * c)
    return [leak ** (3 - s) * rising(place, 3 - s) * decay for s in range(4)]


def lon_tables(lonc, rows, cells, backward, table_ref):
    c, leak, scale = lon_consts(lonc)
    gain = leak**4 * scale
    finals = lon_finals(c, leak, scale, cells, backward)
    spare = jnp.zeros((cells - 4 * rows, cells), f32)
    finals = jnp.concatenate(finals + [spare], axis=0).T
    column = lax.broadcasted_iota(jnp.int32, (cells, cells), 1)
    for y in range(rows):
        inside = lon_kernel_matrix(c[y : y + 1], gain[y : y + 1], cells, backward)
        leaving = jnp.where(lax.rem(column, rows) == y, finals, 0.0)
        table_ref[y] = right3(jnp.concatenate([inside, leaving], axis=1), 0)


def lon_local_rows(load_row, table_ref, rows, cells, inside_ref, carried_ref):
    carried = None
    for y in range(rows):
        both = product3(left3(load_row(y), 1), table_ref[y])
        inside_ref[y] = both[:, :cells]
        carried = both[:, cells:] if carried is None else carried + both[:, cells:]
    carried_ref[...] = carried.T[: 4 * rows]


def lon_incoming_states(lonc, blocks, rows, cells):
    k = blocks[0].shape[1]
    n = len(blocks)
    c = jnp.broadcast_to(lonc[:, :1], (rows, k))
    leak = 1.0 - jnp.exp(-c)

    def trans(r):
        closing = jnp.exp(-float(r * cells) * c)
        return [choose(r * cells, i) * leak**i * closing for i in range(4)]

    total = [jnp.zeros((rows, k), f32) for _ in range(4)]
    for r in range(n):
        part = [blocks[r][s * rows : (s + 1) * rows] for s in range(4)]
        if r:
            t = trans(r)
            part = [sum(t[i - j] * part[j] for j in range(i + 1)) for i in range(4)]
        total = [a + b for a, b in zip(total, part)]
    t = trans(n)
    solved = []
    for i in range(4):
        v = total[i]
        for j in range(i):
            v = v + t[i - j] * solved[j]
        solved.append(v / (1.0 - t[0]))
    return jnp.concatenate(solved, axis=0)


def lon_correction(states, entering, rows, cells):
    high = states.astype(bf16).astype(f32)
    low = states - high
    spare = jnp.zeros((cells - 12 * rows, states.shape[1]), f32)
    left = jnp.concatenate([high, low, high, spare], axis=0).T.astype(bf16)
    spare = jnp.zeros((cells - 12 * rows, cells), bf16)
    return lambda y: product3(left, jnp.concatenate([right3(masked_rows(entering, y), 0), spare], axis=0))


def lat_consts(dec):
    q = jnp.exp(-dec)
    leak = 1.0 - q
    return q, leak, leak * (2.5 / jnp.sqrt(leak))


def lat_sweep(load, store, start, dec, rows, k, backward, block):
    q1, l1, g1 = lat_consts(dec)
    x = dec.shape[1]
    q = jnp.broadcast_to(q1, (block, x))
    leak = jnp.broadcast_to(l1, (block, x))
    gain = jnp.broadcast_to(g1, (block, x))
    order = range(rows - 1, -1, -1) if backward else range(rows)

    def step(i, carry):
        at = pl.ds(pl.multiple_of(i * block, 8), block)
        u = start(at)
        for y in order:
            feed = gain * load(y, at, i * block)
            u0 = q * u[0] + feed
            u1 = q * u[1] + leak * u0
            u2 = q * u[2] + leak * u1
            u3 = q * u[3] + leak * u2
            u = [u0, u1, u2, u3]
            store(y, at, i * block, u3, u if y == order[-1] else None)
        return carry

    lax.fori_loop(0, k // block, step, 0)


def swap_halves(a, b):
    half = a.shape[-1] // 2
    low = iota((1,) * (a.ndim - 1) + (a.shape[-1],), a.ndim - 1) < float(half)
    turn = lambda v: pltpu.roll(v, half, v.ndim - 1)
    return jnp.where(low, a, turn(b)), jnp.where(low, turn(a), b)


def both_halves(v):
    return swap_halves(v, v)


def lat_trans(dec, rows):
    leak = 1.0 - jnp.exp(-dec)
    closing = jnp.exp(-float(rows) * dec)
    return [choose(rows, i) * leak**i * closing for i in range(4)]


def entering_states(got, chunks):
    hops = len(got) // chunks

    def at(chunk, where):
        out = []
        for s in range(4):
            v = None
            for p in got[chunk * hops : (chunk + 1) * hops]:
                v = p[s, where, :] if v is None else v + p[s, where, :]
            out.append(v)
        return out

    return at


def sweep_chunks(load, store, start, dec, rows, k, chunks, backward):
    size = k // chunks
    for ch in range(chunks):
        lat_sweep(
            lambda y, at, base, ch=ch: load(y, ch * size + base),
            lambda y, at, base, value, last, ch=ch: store(y, ch, at, ch * size + base, value, last),
            lambda at, ch=ch: start(ch, at),
            dec,
            rows,
            size,
            backward,
            8,
        )


def k_tables(rows, cells, dec_ref, lonc_ref, latc_ref, table_ref):
    row = jnp.broadcast_to(dec_ref[:, cells:], (rows, rows))
    own = iota((rows, rows), 0) == iota((rows, rows), 1)
    column = jnp.sum(jnp.where(own, row, 0.0), axis=1, keepdims=True)
    lonc = jnp.broadcast_to(column, (rows, cells))
    lonc_ref[...] = lonc
    first, second = both_halves(jnp.broadcast_to(dec_ref[:, :cells], (8, cells)))
    latc_ref[0] = first
    latc_ref[1] = second
    lon_tables(lonc, rows, cells, False, table_ref)


def k_lon_fwd(rows, k, cells, d_ref, table_ref, inside_ref, carried_ref):
    d_ref = d_ref.reshape(k * rows, cells)
    lon_local_rows(
        lambda y: d_ref[pl.ds(y, k, stride=rows), :], table_ref, rows, cells, inside_ref, carried_ref
    )


def spread_modes(v, pairs, transposed):
    source = v.T if transposed else v
    r, c = source.shape
    shape = (pairs * r, 3 * pairs * c)
    num = lambda shape, dim: lax.broadcasted_iota(jnp.int32, shape, dim)
    exact = functools.partial(jnp.dot, precision=lax.Precision.HIGHEST, preferred_element_type=f32)
    pick_row = (lax.rem(num((shape[0], r), 0), r) == num((shape[0], r), 1)).astype(f32)
    pick_column = (num((c, shape[1]), 0) == lax.rem(num((c, shape[1]), 1), c)).astype(f32)
    everywhere = exact(exact(pick_row, source), pick_column)
    row, column = num(shape, 0), num(shape, 1)
    place = lax.rem(column, pairs * c)
    own = (place >= (row // r) * c) & (place < (row // r + 1) * c)
    full = jnp.where(own, everywhere, 0.0)
    high, low = halves(full)
    middle = (column >= pairs * c) & (column < 2 * pairs * c)
    return jnp.where(middle, low.astype(f32), high.astype(f32)).astype(bf16)


def k_prepare(m_ref, lon_ref, v_ref, eig_ref, a_ref, b_ref, mask_ref, out_modes_ref, in_modes_ref, table_ref):
    members, levels, rows, cells = m_ref.shape
    pairs = members // 2
    modes = v_ref.shape[0]
    lon_tables(lon_ref[...], *lon_ref.shape, True, table_ref)
    v = v_ref[...]
    out_modes_ref[...] = spread_modes(v, pairs, True)
    in_modes_ref[...] = spread_modes(v, pairs, False)
    e = lax.broadcasted_iota(jnp.int32, (modes, cells), 0)
    low = lax.broadcasted_iota(jnp.int32, (modes, cells), 1) < cells // 2
    for m in range(pairs):
        used = jnp.where(low, eig_ref[m], eig_ref[m + pairs])
        mask_ref[m * modes : (m + 1) * modes] = jnp.where(e < used, 1.0, 0.0)
    apart = pairs * levels

    def step(i, carry):
        for l in range(levels):
            a, b = swap_halves(m_ref[i, l].astype(f32), m_ref[i + pairs, l].astype(f32))
            at = pl.ds(i * levels + l, rows, stride=apart)
            a_ref[at, :] = a
            b_ref[at, :] = b
        return carry

    lax.fori_loop(0, pairs, step, 0)


def k_lat_first(rows, k, cells, n, chunks, *refs):
    inside_ref, lon_ref, lat_ref, *rest = refs
    blocks = [r[...] for r in rest[:n]]
    f_refs, out_refs = rest[n : n + 2], rest[n + 2 :]
    lonc = lon_ref[...]
    states = lon_incoming_states(lonc, blocks, rows, cells)
    c, leak, _ = lon_consts(lonc)
    added = lon_correction(states, lon_entering(c, leak, cells, False), rows, cells)
    half = k // 2
    for y in range(rows):
        row = inside_ref[y] + added(y)
        f_refs[0][y], f_refs[1][y] = swap_halves(row[:half], row[half:])
    zero = jnp.zeros((8, cells), f32)
    for part, f_ref in enumerate(f_refs):

        def store(y, ch, at, base, value, last, part=part):
            if last is not None:
                for s in range(4):
                    out_refs[part * chunks + ch][s, at, :] = last[s]

        sweep_chunks(
            lambda y, base: f_ref[y, pl.ds(pl.multiple_of(base, 8), 8), :],
            store,
            lambda ch, at: [zero] * 4,
            lat_ref[part, :1],
            rows,
            half,
            chunks,
            False,
        )


def k_pass_on(rows, part, carried_ref, got_ref, lat_ref, out_ref):
    t = lat_trans(lat_ref[part, :1], rows)
    got = [got_ref[s] for s in range(4)]
    for i in range(4):
        v = carried_ref[i]
        for j in range(i + 1):
            v = v + t[i - j] * got[j]
        out_ref[i] = v


def k_increment(rows, k, part, chunks, count, pairs, levels, *refs):
    f_ref, lat_ref, m_ref, mask_ref, modes_ref, *rest = refs
    out_ref, s_ref = rest[count:]
    cells = lat_ref.shape[-1]

    def store(y, ch, at, base, value, last):
        where = pl.ds(pl.multiple_of(base, 8), 8)
        s_ref[y, where, :] = value * mask_ref[where, :]

    sweep_chunks(
        lambda y, base: f_ref[y, pl.ds(pl.multiple_of(base, 8), 8), :],
        store,
        entering_states(rest[:count], chunks),
        lat_ref[part, :1],
        rows,
        k,
        chunks,
        False,
    )
    half = levels // 2
    low = iota((1, cells), 1) < float(cells // 2)
    size = pairs * levels
    for y in range(rows):
        profile = product3(modes_ref[...], right3(s_ref[y], 0))
        inc = None
        for m in range(pairs):
            p = m_ref[y * size + m * levels : y * size + (m + 1) * levels, :] * profile[m * levels : (m + 1) * levels]
            inc = p if inc is None else inc + p
        inc = inc + pltpu.roll(inc, cells // 2, 1)
        out_ref[y] = jnp.where(low, inc[:half], inc[half:])


def k_gradient(rows, k, part, chunks, pairs, levels, *refs):
    inc_ref, got_ref, obs_ref, m_ref, mask_ref, modes_ref, lat_ref, g_ref, *carried_refs = refs
    cells = lat_ref.shape[-1]
    obs_ref = obs_ref.reshape(levels * rows, cells)
    size = pairs * levels
    for y in range(rows):
        inc = jnp.concatenate(both_halves(inc_ref[y] + got_ref[y]), axis=0)
        w = inc * both_halves(obs_ref[pl.ds(y, levels, stride=rows), :])[part]
        m = m_ref[y * size : (y + 1) * size, :]
        weighted = (m.reshape(pairs, levels, cells) * w[None]).reshape(size, cells)
        g_ref[y] = product3(modes_ref[...], right3(weighted, 0)) * mask_ref[...]
    zero8 = jnp.zeros((8, cells), f32)

    def store(y, ch, at, base, value, last):
        if last is not None:
            for s in range(4):
                carried_refs[ch][s, at, :] = last[s]

    sweep_chunks(
        lambda y, base: g_ref[y, pl.ds(pl.multiple_of(base, 8), 8), :],
        store,
        lambda ch, at: [zero8] * 4,
        lat_ref[part, :1],
        rows,
        k,
        chunks,
        True,
    )


def k_lon_bwd(rows, k, cells, chunks, count, *refs):
    g_refs, lat_ref, table_ref, rest = refs[:2], refs[2], refs[3], refs[4:]
    inside_ref, carried_ref, p_ref = rest[2 * count :]
    half = k // 2
    for part in range(2):
        g_ref = g_refs[part]

        def store(y, ch, at, base, value, last, part=part):
            p_ref[part, y, pl.ds(pl.multiple_of(base, 8), 8), :] = value

        sweep_chunks(
            lambda y, base: g_ref[y, pl.ds(pl.multiple_of(base, 8), 8), :],
            store,
            entering_states(rest[part * count : (part + 1) * count], chunks),
            lat_ref[part, :1],
            rows,
            half,
            chunks,
            True,
        )

    def load_row(y):
        return jnp.concatenate(swap_halves(p_ref[0, y], p_ref[1, y]), axis=0)

    lon_local_rows(load_row, table_ref, rows, cells, inside_ref, carried_ref)


def k_sums(rows, k, cells, n, *refs):
    inside_ref, lon_ref, d_ref, r_ref, *rest = refs
    d_ref = d_ref.reshape(k * rows, cells)
    r_ref = r_ref.reshape(k * rows, cells)
    blocks = [r[...] for r in rest[:n]]
    h_ref, sums_ref = rest[n:]
    lonc = lon_ref[...]
    states = lon_incoming_states(lonc, blocks, rows, cells)
    c, leak, _ = lon_consts(lonc)
    added = lon_correction(states, lon_entering(c, leak, cells, True), rows, cells)
    for y in range(rows):
        at = pl.ds(y, k, stride=rows)
        h_ref[at, :] = inside_ref[y] + added(y)
    block = 64
    zero = jnp.zeros((8, cells), f32)

    def step(i, acc):
        at = pl.ds(pl.multiple_of(i * block, 8), block)
        d = d_ref[at, :]
        r = r_ref[at, :]
        h = h_ref[at, :] + d
        h_ref[at, :] = h
        fold = lambda v: v.reshape(block // 8, 8, cells).sum(axis=0)
        return (acc[0] + fold(r * r), acc[1] + fold(d * h), acc[2] + fold(r * h), acc[3] + fold(h * h))

    acc = lax.fori_loop(0, (k * rows) // block, step, (zero,) * 4)
    out = [a.sum(axis=0, keepdims=True) for a in acc]
    sums_ref[...] = jnp.concatenate(out + [jnp.zeros((4, cells), f32)], axis=0)


def k_update(pieces, sums_ref, control_ref, r_ref, d_ref, h_ref, *rest):
    outs, news, sems = rest[:3], rest[3:6], rest[6]
    sums = jnp.sum(sums_ref[...], axis=1, keepdims=True)
    rr, dh, rh, hh = (sums[i : i + 1].reshape(1, 1, 1) for i in range(4))
    step = rr / dh
    norm_new = rr - 2.0 * step * rh + step * step * hh
    beta = norm_new / rr
    size = d_ref.shape[0] // pieces
    copies = []
    for i in range(pieces):
        at = pl.ds(i * size, size)
        d = d_ref[at]
        nr = r_ref[at] - step * h_ref[at]
        for j, v in enumerate((control_ref[at] + step * d, nr, nr + beta * d)):
            news[j][at] = v
            copy = pltpu.make_async_copy(news[j].at[at], outs[j].at[at], sems.at[j, i])
            copy.start()
            copies.append(copy)
    for copy in copies:
        copy.wait()


def call(body, outs, ins, specs=None, out_specs=None, scratch=(), cost=None):
    return pl.pallas_call(
        body,
        out_shape=outs,
        in_specs=specs or [VM] * len(ins),
        out_specs=out_specs or jax.tree.map(lambda _: VM, outs),
        scratch_shapes=scratch,
        cost_estimate=None if cost is None else pl.CostEstimate(flops=cost, bytes_accessed=1000, transcendentals=0),
        compiler_params=pltpu.CompilerParams(vmem_limit_bytes=16 * 1024 * 1024),
    )(*ins)


def sds(*shape):
    return jax.ShapeDtypeStruct(shape, f32)


def lon_exchange(carried, backward):
    n = lax.axis_size("lon")
    sign = -1 if backward else 1
    got = [
        lax.ppermute(carried, "lon", [(j, (j + sign * r) % n) for j in range(n)]) for r in range(1, n)
    ]
    return got + [carried]


def pass_on(part, got, latc, rows, c):
    return call(functools.partial(k_pass_on, rows, c), sds(*part.shape), [part, got, latc])


def lat_carry(halves, latc, rows, backward):
    n = lax.axis_size("lat")
    at = (lambda i: n - 1 - i) if backward else (lambda i: i)
    got = [[[] for _ in chunks] for chunks in halves]
    for h in range(n - 1):
        for c, chunks in enumerate(halves):
            for i, part in enumerate(chunks):
                v = pass_on(part, got[c][i][-1], latc, rows, c) if h else part
                got[c][i].append(lax.ppermute(v, "lat", [(at(h), at(h + 1))]))
    return [[g for chunk in half for g in chunk] for half in got]


def all_sum(v, axes, steps):
    total = 1
    for a in axes:
        total *= lax.axis_size(a)
    masks = [0]
    for s in steps:
        masks = masks + [m ^ s for m in masks]
    got = [lax.ppermute(v, axes, [(i, i ^ m) for i in range(total)]) for m in masks[1:]]
    for g in got:
        v = v + g
    return v


def powers(n):
    out, d = [], 1
    while d < n:
        out.append(d)
        d *= 2
    return out


def reduce_everywhere(v):
    n_lon, n_lat, n_mem = (lax.axis_size(a) for a in ("lon", "lat", "mem"))
    for s in powers(n_mem):
        v = all_sum(v, ("mem",), [s])
    for s in powers(n_lon):
        v = all_sum(v, ("lon",), [s])
    lat = powers(n_lat)
    for i in range(0, len(lat), 2):
        v = all_sum(v, ("lat",), lat[i : i + 2])
    return v


def iteration(control, residual, direction, members, vert_modes, eig_count, lon_decay, lat_decay, obs_weight):
    k, rows, cells = direction.shape
    mcount, levels = members.shape[:2]
    n_lon, n_mem = lax.axis_size("lon"), lax.axis_size("mem")
    half = k // 2
    pairs = mcount // 2
    chunks, back_chunks = 2, 1
    states = lambda chunks: (sds(4, half // chunks, cells),) * chunks

    decays = jnp.concatenate([lat_decay, lon_decay]).reshape(1, cells + rows)
    lonc, latc, tables = call(
        functools.partial(k_tables, rows, cells),
        (sds(rows, cells), sds(2, 8, cells), jax.ShapeDtypeStruct((rows, 3 * cells, 2 * cells), bf16)),
        [decays],
        cost=10**9,
    )
    inside, carried = call(
        functools.partial(k_lon_fwd, rows, k, cells), (sds(rows, k, cells), sds(4 * rows, k)), [direction, tables]
    )
    *packed, mask, out_modes, in_modes, back_tables = call(
        k_prepare,
        (sds(rows * pairs * levels, cells),) * 2
        + (
            sds(half, cells),
            jax.ShapeDtypeStruct((pairs * levels, 3 * half), bf16),
            jax.ShapeDtypeStruct((half, 3 * pairs * levels), bf16),
            jax.ShapeDtypeStruct((rows, 3 * cells, 2 * cells), bf16),
        ),
        [members, lonc, vert_modes, eig_count],
        specs=[VM, VM, VM, SM],
        cost=10**9,
    )
    blocks = lon_exchange(carried, False)
    fa, fb, *parts = call(
        functools.partial(k_lat_first, rows, k, cells, n_lon, chunks),
        (sds(rows, half, cells),) * 2 + states(chunks) * 2,
        [inside, lonc, latc, *blocks],
    )
    got = lat_carry([parts[:chunks], parts[chunks:]], latc, rows, False)
    count = len(got[0])
    fields = (fa, fb)
    inc = [None, None]
    for part in range(2):
        inc[part] = call(
            functools.partial(k_increment, rows, half, part, chunks, count, pairs, levels),
            sds(rows, levels // 2, cells),
            [fields[part], latc, packed[part], mask, out_modes, *got[part]],
            scratch=[pltpu.VMEM((rows, half, cells), f32)],
        )
    grads, sends = [None, None], [None, None]
    for part in range(2):
        v = inc[part]
        step = 1
        while step * 2 < n_mem:
            v = v + lax.ppermute(v, "mem", [(i, i ^ step) for i in range(n_mem)])
            step *= 2
        other = lax.ppermute(v, "mem", [(i, i ^ step) for i in range(n_mem)])
        grads[part], *sends[part] = call(
            functools.partial(k_gradient, rows, half, part, back_chunks, pairs, levels),
            (sds(rows, half, cells),) + states(back_chunks),
            [v, other, obs_weight, packed[part], mask, in_modes, latc],
        )
    got = lat_carry(sends, latc, rows, True)
    count = len(got[0])
    inside, carried = call(
        functools.partial(k_lon_bwd, rows, k, cells, back_chunks, count),
        (sds(rows, k, cells), sds(4 * rows, k)),
        [*grads, latc, back_tables, *got[0], *got[1]],
        scratch=[pltpu.VMEM((2, rows, half, cells), f32)],
    )
    blocks = lon_exchange(carried, True)
    h, sums = call(
        functools.partial(k_sums, rows, k, cells, n_lon),
        (sds(k * rows, cells), sds(8, cells)),
        [inside, lonc, direction, residual, *blocks],
    )
    sums = reduce_everywhere(sums)
    pieces = 4 if k % 4 == 0 else 1
    outs = call(
        functools.partial(k_update, pieces),
        (sds(k, rows, cells),) * 3,
        [sums, control, residual, direction, h.reshape(k, rows, cells)],
        out_specs=(pl.BlockSpec(memory_space=pl.ANY),) * 3,
        scratch=[pltpu.VMEM((k, rows, cells), f32)] * 3 + [pltpu.SemaphoreType.DMA((3, pieces))],
    )
    return tuple(outs)


def solution(mesh):
    field = P("mem", "lat", "lon")
    placed = (
        field,
        field,
        field,
        P("mem", None, "lat", "lon"),
        P(),
        P("mem"),
        P("lat"),
        P("lon"),
        P(None, "lat", "lon"),
    )
    return jax.shard_map(iteration, mesh=mesh, in_specs=placed, out_specs=(field,) * 3, check_vma=False)
```

```python
import functools
import jax
import jax.numpy as jnp
from jax import lax
from jax.experimental import pallas as pl
from jax.experimental.pallas import tpu as pltpu
from jax.sharding import PartitionSpec as P


f32 = jnp.float32
bf16 = jnp.bfloat16
VM = pl.BlockSpec(memory_space=pltpu.VMEM)
SM = pl.BlockSpec(memory_space=pltpu.SMEM)


def choose(length, i):
    r = 1.0
    for k in range(i):
        r = r * (length + k) / (k + 1)
    return r


def rising(v, degree):
    r = jnp.ones_like(v)
    for k in range(degree):
        r = r * (v + (k + 1.0)) * (1.0 / (k + 1.0))
    return r


def halves(v):
    high = v.astype(bf16)
    return high, (v - high.astype(f32)).astype(bf16)


def left3(v, axis):
    high, low = halves(v)
    return jnp.concatenate([high, low, high], axis=axis)


def right3(v, axis):
    high, low = halves(v)
    return jnp.concatenate([high, high, low], axis=axis)


def product3(a, b):
    return jnp.dot(a, b, preferred_element_type=f32)


def iota(shape, dim):
    return lax.broadcasted_iota(jnp.int32, shape, dim).astype(f32)


def lon_consts(lonc):
    c = lonc
    q = jnp.exp(-c)
    leak = 1.0 - q
    return c, leak, 2.5 / jnp.sqrt(leak)


def lon_kernel_matrix(c_row, gain_row, cells, backward):
    a = iota((cells, cells), 0)
    b = iota((cells, cells), 1)
    lag = a - b if backward else b - a
    pos = jnp.maximum(lag, 0.0)
    shaped = rising(pos, 3) * jnp.exp(-pos * c_row) * gain_row
    return jnp.where(lag >= 0.0, shaped, 0.0)


def masked_rows(parts, y):
    rows = iota(parts[0].shape, 0)
    return jnp.concatenate([jnp.where(rows == float(y), p, 0.0) for p in parts], axis=0)


def lon_finals(c, leak, scale, cells, backward):
    x = iota(c.shape, 1)
    remain = x if backward else (cells - 1.0) - x
    decay = jnp.exp(-remain * c)
    return [leak ** (s + 1) * scale * rising(remain, s) * decay for s in range(4)]


def lon_entering(c, leak, cells, backward):
    x = iota(c.shape, 1)
    place = (cells - 1.0) - x if backward else x
    decay = jnp.exp(-(place + 1.0) * c)
    return [leak ** (3 - s) * rising(place, 3 - s) * decay for s in range(4)]


def lon_tables(lonc, rows, cells, backward, table_ref):
    c, leak, scale = lon_consts(lonc)
    gain = leak**4 * scale
    finals = lon_finals(c, leak, scale, cells, backward)
    spare = jnp.zeros((cells - 4 * rows, cells), f32)
    finals = jnp.concatenate(finals + [spare], axis=0).T
    column = lax.broadcasted_iota(jnp.int32, (cells, cells), 1)
    for y in range(rows):
        inside = lon_kernel_matrix(c[y : y + 1], gain[y : y + 1], cells, backward)
        leaving = jnp.where(lax.rem(column, rows) == y, finals, 0.0)
        table_ref[y] = right3(jnp.concatenate([inside, leaving], axis=1), 0)


def lon_local_rows(load_row, table_ref, rows, cells, inside_ref, carried_ref):
    carried = None
    for y in range(rows):
        both = product3(left3(load_row(y), 1), table_ref[y])
        inside_ref[y] = both[:, :cells]
        carried = both[:, cells:] if carried is None else carried + both[:, cells:]
    carried_ref[...] = carried.T[: 4 * rows]


def lon_incoming_states(lonc, blocks, rows, cells):
    k = blocks[0].shape[1]
    n = len(blocks)
    c = jnp.broadcast_to(lonc[:, :1], (rows, k))
    leak = 1.0 - jnp.exp(-c)

    def trans(r):
        closing = jnp.exp(-float(r * cells) * c)
        return [choose(r * cells, i) * leak**i * closing for i in range(4)]

    total = [jnp.zeros((rows, k), f32) for _ in range(4)]
    for r in range(n):
        part = [blocks[r][s * rows : (s + 1) * rows] for s in range(4)]
        if r:
            t = trans(r)
            part = [sum(t[i - j] * part[j] for j in range(i + 1)) for i in range(4)]
        total = [a + b for a, b in zip(total, part)]
    t = trans(n)
    solved = []
    for i in range(4):
        v = total[i]
        for j in range(i):
            v = v + t[i - j] * solved[j]
        solved.append(v / (1.0 - t[0]))
    return jnp.concatenate(solved, axis=0)


def lon_correction(states, entering, rows, cells):
    high = states.astype(bf16).astype(f32)
    low = states - high
    spare = jnp.zeros((cells - 12 * rows, states.shape[1]), f32)
    left = jnp.concatenate([high, low, high, spare], axis=0).T.astype(bf16)
    spare = jnp.zeros((cells - 12 * rows, cells), bf16)
    return lambda y: product3(left, jnp.concatenate([right3(masked_rows(entering, y), 0), spare], axis=0))


def lat_consts(dec):
    q = jnp.exp(-dec)
    leak = 1.0 - q
    return q, leak, leak * (2.5 / jnp.sqrt(leak))


def lat_sweep(load, store, start, dec, rows, k, backward, block):
    q1, l1, g1 = lat_consts(dec)
    x = dec.shape[1]
    q = jnp.broadcast_to(q1, (block, x))
    leak = jnp.broadcast_to(l1, (block, x))
    gain = jnp.broadcast_to(g1, (block, x))
    order = range(rows - 1, -1, -1) if backward else range(rows)

    def step(i, carry):
        at = pl.ds(pl.multiple_of(i * block, 8), block)
        u = start(at)
        for y in order:
            feed = gain * load(y, at, i * block)
            u0 = q * u[0] + feed
            u1 = q * u[1] + leak * u0
            u2 = q * u[2] + leak * u1
            u3 = q * u[3] + leak * u2
            u = [u0, u1, u2, u3]
            store(y, at, i * block, u3, u if y == order[-1] else None)
        return carry

    lax.fori_loop(0, k // block, step, 0)


def swap_halves(a, b):
    half = a.shape[-1] // 2
    low = iota((1,) * (a.ndim - 1) + (a.shape[-1],), a.ndim - 1) < float(half)
    turn = lambda v: pltpu.roll(v, half, v.ndim - 1)
    return jnp.where(low, a, turn(b)), jnp.where(low, turn(a), b)


def both_halves(v):
    return swap_halves(v, v)


def lat_trans(dec, rows):
    leak = 1.0 - jnp.exp(-dec)
    closing = jnp.exp(-float(rows) * dec)
    return [choose(rows, i) * leak**i * closing for i in range(4)]


def entering_states(got, chunks):
    hops = len(got) // chunks

    def at(chunk, where):
        out = []
        for s in range(4):
            v = None
            for p in got[chunk * hops : (chunk + 1) * hops]:
                v = p[s, where, :] if v is None else v + p[s, where, :]
            out.append(v)
        return out

    return at


def sweep_chunks(load, store, start, dec, rows, k, chunks, backward):
    size = k // chunks
    for ch in range(chunks):
        lat_sweep(
            lambda y, at, base, ch=ch: load(y, ch * size + base),
            lambda y, at, base, value, last, ch=ch: store(y, ch, at, ch * size + base, value, last),
            lambda at, ch=ch: start(ch, at),
            dec,
            rows,
            size,
            backward,
            8,
        )


def k_tables(rows, cells, dec_ref, lonc_ref, latc_ref, table_ref):
    row = jnp.broadcast_to(dec_ref[:, cells:], (rows, rows))
    own = iota((rows, rows), 0) == iota((rows, rows), 1)
    column = jnp.sum(jnp.where(own, row, 0.0), axis=1, keepdims=True)
    lonc = jnp.broadcast_to(column, (rows, cells))
    lonc_ref[...] = lonc
    first, second = both_halves(jnp.broadcast_to(dec_ref[:, :cells], (8, cells)))
    latc_ref[0] = first
    latc_ref[1] = second
    lon_tables(lonc, rows, cells, False, table_ref)


def k_lon_fwd(rows, k, cells, d_ref, table_ref, inside_ref, carried_ref):
    d_ref = d_ref.reshape(k * rows, cells)
    lon_local_rows(
        lambda y: d_ref[pl.ds(y, k, stride=rows), :], table_ref, rows, cells, inside_ref, carried_ref
    )


def spread_modes(v, pairs, transposed):
    source = v.T if transposed else v
    r, c = source.shape
    rows, columns = pairs * r, 3 * pairs * c
    exact = functools.partial(jnp.dot, precision=lax.Precision.HIGHEST, preferred_element_type=f32)
    block = lambda at, size: jnp.floor((at + 0.5) * (1.0 / size))
    at_row, at_column = iota((rows, r), 0), iota((c, columns), 1)
    pick_row = (at_row - block(at_row, r) * r == iota((rows, r), 1)).astype(f32)
    pick_column = (at_column - block(at_column, c) * c == iota((c, columns), 0)).astype(f32)
    everywhere = exact(exact(pick_row, source), pick_column)
    column = iota((1, columns), 1)
    part = block(column, pairs * c)
    own = block(iota((rows, 1), 0), r) == block(column - part * (pairs * c), c)
    full = jnp.where(own, everywhere, 0.0)
    high, low = halves(full)
    return jnp.where(part == 1.0, low.astype(f32), high.astype(f32)).astype(bf16)


def k_modes(pairs, v_ref, eig_ref, mask_ref, out_modes_ref, in_modes_ref):
    modes = v_ref.shape[0]
    cells = mask_ref.shape[1]
    v = v_ref[...]
    out_modes_ref[...] = spread_modes(v, pairs, True)
    in_modes_ref[...] = spread_modes(v, pairs, False)
    e = lax.broadcasted_iota(jnp.int32, (modes, cells), 0)
    low = lax.broadcasted_iota(jnp.int32, (modes, cells), 1) < cells // 2
    for m in range(pairs):
        used = jnp.where(low, eig_ref[m], eig_ref[m + pairs])
        mask_ref[m * modes : (m + 1) * modes] = jnp.where(e < used, 1.0, 0.0)


def k_prepare(m_ref, lon_ref, a_ref, b_ref, table_ref):
    members, levels, rows, _ = m_ref.shape
    pairs = members // 2
    lon_tables(lon_ref[...], *lon_ref.shape, True, table_ref)
    apart = pairs * levels

    def step(i, carry):
        for l in range(levels):
            a, b = swap_halves(m_ref[i, l].astype(f32), m_ref[i + pairs, l].astype(f32))
            at = pl.ds(i * levels + l, rows, stride=apart)
            a_ref[at, :] = a
            b_ref[at, :] = b
        return carry

    lax.fori_loop(0, pairs, step, 0)


def k_lat_first(rows, k, cells, n, chunks, *refs):
    inside_ref, lon_ref, lat_ref, *rest = refs
    blocks = [r[...] for r in rest[:n]]
    f_refs, out_refs = rest[n : n + 2], rest[n + 2 :]
    lonc = lon_ref[...]
    states = lon_incoming_states(lonc, blocks, rows, cells)
    c, leak, _ = lon_consts(lonc)
    added = lon_correction(states, lon_entering(c, leak, cells, False), rows, cells)
    half = k // 2
    for y in range(rows):
        row = inside_ref[y] + added(y)
        f_refs[0][y], f_refs[1][y] = swap_halves(row[:half], row[half:])
    zero = jnp.zeros((8, cells), f32)
    for part, f_ref in enumerate(f_refs):

        def store(y, ch, at, base, value, last, part=part):
            if last is not None:
                for s in range(4):
                    out_refs[part * chunks + ch][s, at, :] = last[s]

        sweep_chunks(
            lambda y, base: f_ref[y, pl.ds(pl.multiple_of(base, 8), 8), :],
            store,
            lambda ch, at: [zero] * 4,
            lat_ref[part, :1],
            rows,
            half,
            chunks,
            False,
        )


def k_pass_on(rows, part, carried_ref, got_ref, lat_ref, out_ref):
    t = lat_trans(lat_ref[part, :1], rows)
    got = [got_ref[s] for s in range(4)]
    for i in range(4):
        v = carried_ref[i]
        for j in range(i + 1):
            v = v + t[i - j] * got[j]
        out_ref[i] = v


def k_increment(rows, k, part, chunks, count, pairs, levels, *refs):
    f_ref, lat_ref, m_ref, mask_ref, modes_ref, *rest = refs
    out_ref, s_ref = rest[count:]
    cells = lat_ref.shape[-1]

    def store(y, ch, at, base, value, last):
        where = pl.ds(pl.multiple_of(base, 8), 8)
        s_ref[y, where, :] = value * mask_ref[where, :]

    sweep_chunks(
        lambda y, base: f_ref[y, pl.ds(pl.multiple_of(base, 8), 8), :],
        store,
        entering_states(rest[:count], chunks),
        lat_ref[part, :1],
        rows,
        k,
        chunks,
        False,
    )
    half = levels // 2
    low = iota((1, cells), 1) < float(cells // 2)
    size = pairs * levels
    for y in range(rows):
        profile = product3(modes_ref[...], right3(s_ref[y], 0))
        inc = None
        for m in range(pairs):
            p = m_ref[y * size + m * levels : y * size + (m + 1) * levels, :] * profile[m * levels : (m + 1) * levels]
            inc = p if inc is None else inc + p
        inc = inc + pltpu.roll(inc, cells // 2, 1)
        out_ref[y] = jnp.where(low, inc[:half], inc[half:])


def k_gradient(rows, k, part, chunks, pairs, levels, *refs):
    inc_ref, got_ref, obs_ref, m_ref, mask_ref, modes_ref, lat_ref, g_ref, *carried_refs = refs
    cells = lat_ref.shape[-1]
    obs_ref = obs_ref.reshape(levels * rows, cells)
    size = pairs * levels
    for y in range(rows):
        inc = jnp.concatenate(both_halves(inc_ref[y] + got_ref[y]), axis=0)
        w = inc * both_halves(obs_ref[pl.ds(y, levels, stride=rows), :])[part]
        m = m_ref[y * size : (y + 1) * size, :]
        weighted = (m.reshape(pairs, levels, cells) * w[None]).reshape(size, cells)
        g_ref[y] = product3(modes_ref[...], right3(weighted, 0)) * mask_ref[...]
    zero8 = jnp.zeros((8, cells), f32)

    def store(y, ch, at, base, value, last):
        if last is not None:
            for s in range(4):
                carried_refs[ch][s, at, :] = last[s]

    sweep_chunks(
        lambda y, base: g_ref[y, pl.ds(pl.multiple_of(base, 8), 8), :],
        store,
        lambda ch, at: [zero8] * 4,
        lat_ref[part, :1],
        rows,
        k,
        chunks,
        True,
    )


def k_lon_bwd(rows, k, cells, chunks, count, *refs):
    g_refs, lat_ref, table_ref, rest = refs[:2], refs[2], refs[3], refs[4:]
    inside_ref, carried_ref, p_ref = rest[2 * count :]
    half = k // 2
    for part in range(2):
        g_ref = g_refs[part]

        def store(y, ch, at, base, value, last, part=part):
            p_ref[part, y, pl.ds(pl.multiple_of(base, 8), 8), :] = value

        sweep_chunks(
            lambda y, base: g_ref[y, pl.ds(pl.multiple_of(base, 8), 8), :],
            store,
            entering_states(rest[part * count : (part + 1) * count], chunks),
            lat_ref[part, :1],
            rows,
            half,
            chunks,
            True,
        )

    def load_row(y):
        return jnp.concatenate(swap_halves(p_ref[0, y], p_ref[1, y]), axis=0)

    lon_local_rows(load_row, table_ref, rows, cells, inside_ref, carried_ref)


def k_sums(rows, k, cells, n, *refs):
    inside_ref, lon_ref, d_ref, r_ref, *rest = refs
    d_ref = d_ref.reshape(k * rows, cells)
    r_ref = r_ref.reshape(k * rows, cells)
    blocks = [r[...] for r in rest[:n]]
    h_ref, sums_ref = rest[n:]
    lonc = lon_ref[...]
    states = lon_incoming_states(lonc, blocks, rows, cells)
    c, leak, _ = lon_consts(lonc)
    added = lon_correction(states, lon_entering(c, leak, cells, True), rows, cells)
    for y in range(rows):
        at = pl.ds(y, k, stride=rows)
        h_ref[at, :] = inside_ref[y] + added(y)
    block = 64
    zero = jnp.zeros((8, cells), f32)

    def step(i, acc):
        at = pl.ds(pl.multiple_of(i * block, 8), block)
        d = d_ref[at, :]
        r = r_ref[at, :]
        h = h_ref[at, :] + d
        h_ref[at, :] = h
        fold = lambda v: v.reshape(block // 8, 8, cells).sum(axis=0)
        return (acc[0] + fold(r * r), acc[1] + fold(d * h), acc[2] + fold(r * h), acc[3] + fold(h * h))

    acc = lax.fori_loop(0, (k * rows) // block, step, (zero,) * 4)
    out = [a.sum(axis=0, keepdims=True) for a in acc]
    sums_ref[...] = jnp.concatenate(out + [jnp.zeros((4, cells), f32)], axis=0)


def k_update(pieces, sums_ref, control_ref, r_ref, d_ref, h_ref, *rest):
    outs, news, sems = rest[:3], rest[3:6], rest[6]
    sums = jnp.sum(sums_ref[...], axis=1, keepdims=True)
    rr, dh, rh, hh = (sums[i : i + 1].reshape(1, 1, 1) for i in range(4))
    step = rr / dh
    norm_new = rr - 2.0 * step * rh + step * step * hh
    beta = norm_new / rr
    size = d_ref.shape[0] // pieces
    copies = []
    for i in range(pieces):
        at = pl.ds(i * size, size)
        d = d_ref[at]
        nr = r_ref[at] - step * h_ref[at]
        for j, v in enumerate((control_ref[at] + step * d, nr, nr + beta * d)):
            news[j][at] = v
            copy = pltpu.make_async_copy(news[j].at[at], outs[j].at[at], sems.at[j, i])
            copy.start()
            copies.append(copy)
    for copy in copies:
        copy.wait()


def call(body, outs, ins, specs=None, out_specs=None, scratch=(), cost=None):
    return pl.pallas_call(
        body,
        out_shape=outs,
        in_specs=specs or [VM] * len(ins),
        out_specs=out_specs or jax.tree.map(lambda _: VM, outs),
        scratch_shapes=scratch,
        cost_estimate=None if cost is None else pl.CostEstimate(flops=cost, bytes_accessed=1000, transcendentals=0),
        compiler_params=pltpu.CompilerParams(vmem_limit_bytes=16 * 1024 * 1024),
    )(*ins)


def sds(*shape):
    return jax.ShapeDtypeStruct(shape, f32)


def lon_exchange(carried, backward):
    n = lax.axis_size("lon")
    sign = -1 if backward else 1
    got = [
        lax.ppermute(carried, "lon", [(j, (j + sign * r) % n) for j in range(n)]) for r in range(1, n)
    ]
    return got + [carried]


def pass_on(part, got, latc, rows, c):
    return call(functools.partial(k_pass_on, rows, c), sds(*part.shape), [part, got, latc])


def lat_carry(halves, latc, rows, backward):
    n = lax.axis_size("lat")
    at = (lambda i: n - 1 - i) if backward else (lambda i: i)
    got = [[[] for _ in chunks] for chunks in halves]
    for h in range(n - 1):
        for c, chunks in enumerate(halves):
            for i, part in enumerate(chunks):
                v = pass_on(part, got[c][i][-1], latc, rows, c) if h else part
                got[c][i].append(lax.ppermute(v, "lat", [(at(h), at(h + 1))]))
    return [[g for chunk in half for g in chunk] for half in got]


def all_sum(v, axes, steps):
    total = 1
    for a in axes:
        total *= lax.axis_size(a)
    masks = [0]
    for s in steps:
        masks = masks + [m ^ s for m in masks]
    got = [lax.ppermute(v, axes, [(i, i ^ m) for i in range(total)]) for m in masks[1:]]
    for g in got:
        v = v + g
    return v


def powers(n):
    out, d = [], 1
    while d < n:
        out.append(d)
        d *= 2
    return out


def reduce_everywhere(v):
    n_lon, n_lat, n_mem = (lax.axis_size(a) for a in ("lon", "lat", "mem"))
    for s in powers(n_mem):
        v = all_sum(v, ("mem",), [s])
    for s in powers(n_lon):
        v = all_sum(v, ("lon",), [s])
    lat = powers(n_lat)
    for i in range(0, len(lat), 2):
        v = all_sum(v, ("lat",), lat[i : i + 2])
    return v


def iteration(control, residual, direction, members, vert_modes, eig_count, lon_decay, lat_decay, obs_weight):
    k, rows, cells = direction.shape
    mcount, levels = members.shape[:2]
    n_lon, n_mem = lax.axis_size("lon"), lax.axis_size("mem")
    half = k // 2
    pairs = mcount // 2
    chunks, back_chunks = 2, 2
    states = lambda chunks: (sds(4, half // chunks, cells),) * chunks

    decays = jnp.concatenate([lat_decay, lon_decay]).reshape(1, cells + rows)
    lonc, latc, tables = call(
        functools.partial(k_tables, rows, cells),
        (sds(rows, cells), sds(2, 8, cells), jax.ShapeDtypeStruct((rows, 3 * cells, 2 * cells), bf16)),
        [decays],
        cost=10**9,
    )
    inside, carried = call(
        functools.partial(k_lon_fwd, rows, k, cells), (sds(rows, k, cells), sds(4 * rows, k)), [direction, tables]
    )
    *packed, back_tables = call(
        k_prepare,
        (sds(rows * pairs * levels, cells),) * 2
        + (jax.ShapeDtypeStruct((rows, 3 * cells, 2 * cells), bf16),),
        [members, lonc],
        cost=10**9,
    )
    mask, out_modes, in_modes = call(
        functools.partial(k_modes, pairs),
        (
            sds(half, cells),
            jax.ShapeDtypeStruct((pairs * levels, 3 * half), bf16),
            jax.ShapeDtypeStruct((half, 3 * pairs * levels), bf16),
        ),
        [vert_modes, eig_count],
        specs=[VM, SM],
        cost=10**9,
    )
    blocks = lon_exchange(carried, False)
    fa, fb, *parts = call(
        functools.partial(k_lat_first, rows, k, cells, n_lon, chunks),
        (sds(rows, half, cells),) * 2 + states(chunks) * 2,
        [inside, lonc, latc, *blocks],
    )
    got = lat_carry([parts[:chunks], parts[chunks:]], latc, rows, False)
    count = len(got[0])
    fields = (fa, fb)
    inc = [None, None]
    for part in range(2):
        inc[part] = call(
            functools.partial(k_increment, rows, half, part, chunks, count, pairs, levels),
            sds(rows, levels // 2, cells),
            [fields[part], latc, packed[part], mask, out_modes, *got[part]],
            scratch=[pltpu.VMEM((rows, half, cells), f32)],
        )
    grads, sends = [None, None], [None, None]
    for part in range(2):
        v = inc[part]
        step = 1
        while step * 2 < n_mem:
            v = v + lax.ppermute(v, "mem", [(i, i ^ step) for i in range(n_mem)])
            step *= 2
        other = lax.ppermute(v, "mem", [(i, i ^ step) for i in range(n_mem)])
        grads[part], *sends[part] = call(
            functools.partial(k_gradient, rows, half, part, back_chunks, pairs, levels),
            (sds(rows, half, cells),) + states(back_chunks),
            [v, other, obs_weight, packed[part], mask, in_modes, latc],
        )
    got = lat_carry(sends, latc, rows, True)
    count = len(got[0])
    inside, carried = call(
        functools.partial(k_lon_bwd, rows, k, cells, back_chunks, count),
        (sds(rows, k, cells), sds(4 * rows, k)),
        [*grads, latc, back_tables, *got[0], *got[1]],
        scratch=[pltpu.VMEM((2, rows, half, cells), f32)],
    )
    blocks = lon_exchange(carried, True)
    h, sums = call(
        functools.partial(k_sums, rows, k, cells, n_lon),
        (sds(k * rows, cells), sds(8, cells)),
        [inside, lonc, direction, residual, *blocks],
    )
    sums = reduce_everywhere(sums)
    pieces = 4 if k % 4 == 0 else 1
    outs = call(
        functools.partial(k_update, pieces),
        (sds(k, rows, cells),) * 3,
        [sums, control, residual, direction, h.reshape(k, rows, cells)],
        out_specs=(pl.BlockSpec(memory_space=pl.ANY),) * 3,
        scratch=[pltpu.VMEM((k, rows, cells), f32)] * 3 + [pltpu.SemaphoreType.DMA((3, pieces))],
    )
    return tuple(outs)


def solution(mesh):
    field = P("mem", "lat", "lon")
    placed = (
        field,
        field,
        field,
        P("mem", None, "lat", "lon"),
        P(),
        P("mem"),
        P("lat"),
        P("lon"),
        P(None, "lat", "lon"),
    )
    return jax.shard_map(iteration, mesh=mesh, in_specs=placed, out_specs=(field,) * 3, check_vma=False)
```

```python
import functools
import jax
import jax.numpy as jnp
from jax import lax
from jax.experimental import pallas as pl
from jax.experimental.pallas import tpu as pltpu
from jax.sharding import PartitionSpec as P


f32 = jnp.float32
bf16 = jnp.bfloat16
VM = pl.BlockSpec(memory_space=pltpu.VMEM)
SM = pl.BlockSpec(memory_space=pltpu.SMEM)


def choose(length, i):
    r = 1.0
    for k in range(i):
        r = r * (length + k) / (k + 1)
    return r


def rising(v, degree):
    r = jnp.ones_like(v)
    for k in range(degree):
        r = r * (v + (k + 1.0)) * (1.0 / (k + 1.0))
    return r


def halves(v):
    high = v.astype(bf16)
    return high, (v - high.astype(f32)).astype(bf16)


def left3(v, axis):
    high, low = halves(v)
    return jnp.concatenate([high, low, high], axis=axis)


def right3(v, axis):
    high, low = halves(v)
    return jnp.concatenate([high, high, low], axis=axis)


def product3(a, b):
    return jnp.dot(a, b, preferred_element_type=f32)


def iota(shape, dim):
    return lax.broadcasted_iota(jnp.int32, shape, dim).astype(f32)


def lon_consts(lonc):
    c = lonc
    q = jnp.exp(-c)
    leak = 1.0 - q
    return c, leak, 2.5 / jnp.sqrt(leak)


def lon_kernel_matrix(c_row, gain_row, cells, backward):
    a = iota((cells, cells), 0)
    b = iota((cells, cells), 1)
    lag = a - b if backward else b - a
    pos = jnp.maximum(lag, 0.0)
    shaped = rising(pos, 3) * jnp.exp(-pos * c_row) * gain_row
    return jnp.where(lag >= 0.0, shaped, 0.0)


def masked_rows(parts, y):
    rows = iota(parts[0].shape, 0)
    return jnp.concatenate([jnp.where(rows == float(y), p, 0.0) for p in parts], axis=0)


def lon_finals(c, leak, scale, cells, backward):
    x = iota(c.shape, 1)
    remain = x if backward else (cells - 1.0) - x
    decay = jnp.exp(-remain * c)
    return [leak ** (s + 1) * scale * rising(remain, s) * decay for s in range(4)]


def lon_entering(c, leak, cells, backward):
    x = iota(c.shape, 1)
    place = (cells - 1.0) - x if backward else x
    decay = jnp.exp(-(place + 1.0) * c)
    return [leak ** (3 - s) * rising(place, 3 - s) * decay for s in range(4)]


def lon_tables(lonc, rows, cells, backward, table_ref):
    c, leak, scale = lon_consts(lonc)
    gain = leak**4 * scale
    finals = lon_finals(c, leak, scale, cells, backward)
    spare = jnp.zeros((cells - 4 * rows, cells), f32)
    finals = jnp.concatenate(finals + [spare], axis=0).T
    column = lax.broadcasted_iota(jnp.int32, (cells, cells), 1)
    for y in range(rows):
        inside = lon_kernel_matrix(c[y : y + 1], gain[y : y + 1], cells, backward)
        leaving = jnp.where(lax.rem(column, rows) == y, finals, 0.0)
        table_ref[y] = right3(jnp.concatenate([inside, leaving], axis=1), 0)


def lon_local_rows(load_row, table_ref, rows, cells, inside_ref, carried_ref):
    carried = None
    for y in range(rows):
        both = product3(left3(load_row(y), 1), table_ref[y])
        inside_ref[y] = both[:, :cells]
        carried = both[:, cells:] if carried is None else carried + both[:, cells:]
    carried_ref[...] = carried.T[: 4 * rows]


def lon_incoming_states(lonc, blocks, rows, cells):
    k = blocks[0].shape[1]
    n = len(blocks)
    c = jnp.broadcast_to(lonc[:, :1], (rows, k))
    leak = 1.0 - jnp.exp(-c)

    def trans(r):
        closing = jnp.exp(-float(r * cells) * c)
        return [choose(r * cells, i) * leak**i * closing for i in range(4)]

    total = [jnp.zeros((rows, k), f32) for _ in range(4)]
    for r in range(n):
        part = [blocks[r][s * rows : (s + 1) * rows] for s in range(4)]
        if r:
            t = trans(r)
            part = [sum(t[i - j] * part[j] for j in range(i + 1)) for i in range(4)]
        total = [a + b for a, b in zip(total, part)]
    t = trans(n)
    solved = []
    for i in range(4):
        v = total[i]
        for j in range(i):
            v = v + t[i - j] * solved[j]
        solved.append(v / (1.0 - t[0]))
    return jnp.concatenate(solved, axis=0)


def lon_correction(states, entering, rows, cells):
    high = states.astype(bf16).astype(f32)
    low = states - high
    spare = jnp.zeros((cells - 12 * rows, states.shape[1]), f32)
    left = jnp.concatenate([high, low, high, spare], axis=0).T.astype(bf16)
    spare = jnp.zeros((cells - 12 * rows, cells), bf16)
    return lambda y: product3(left, jnp.concatenate([right3(masked_rows(entering, y), 0), spare], axis=0))


def lat_consts(dec):
    q = jnp.exp(-dec)
    leak = 1.0 - q
    return q, leak, leak * (2.5 / jnp.sqrt(leak))


def lat_sweep(load, store, start, dec, rows, k, backward, block):
    q1, l1, g1 = lat_consts(dec)
    x = dec.shape[1]
    q = jnp.broadcast_to(q1, (block, x))
    leak = jnp.broadcast_to(l1, (block, x))
    gain = jnp.broadcast_to(g1, (block, x))
    order = range(rows - 1, -1, -1) if backward else range(rows)

    def step(i, carry):
        at = pl.ds(pl.multiple_of(i * block, 8), block)
        u = start(at)
        for y in order:
            feed = gain * load(y, at, i * block)
            u0 = q * u[0] + feed
            u1 = q * u[1] + leak * u0
            u2 = q * u[2] + leak * u1
            u3 = q * u[3] + leak * u2
            u = [u0, u1, u2, u3]
            store(y, at, i * block, u3, u if y == order[-1] else None)
        return carry

    lax.fori_loop(0, k // block, step, 0)


def swap_halves(a, b):
    half = a.shape[-1] // 2
    low = iota((1,) * (a.ndim - 1) + (a.shape[-1],), a.ndim - 1) < float(half)
    turn = lambda v: pltpu.roll(v, half, v.ndim - 1)
    return jnp.where(low, a, turn(b)), jnp.where(low, turn(a), b)


def both_halves(v):
    return swap_halves(v, v)


def lat_trans(dec, rows):
    leak = 1.0 - jnp.exp(-dec)
    closing = jnp.exp(-float(rows) * dec)
    return [choose(rows, i) * leak**i * closing for i in range(4)]


def entering_states(got, chunks):
    hops = len(got) // chunks

    def at(chunk, where):
        out = []
        for s in range(4):
            v = None
            for p in got[chunk * hops : (chunk + 1) * hops]:
                v = p[s, where, :] if v is None else v + p[s, where, :]
            out.append(v)
        return out

    return at


def sweep_chunks(load, store, start, dec, rows, k, chunks, backward):
    size = k // chunks
    for ch in range(chunks):
        lat_sweep(
            lambda y, at, base, ch=ch: load(y, ch * size + base),
            lambda y, at, base, value, last, ch=ch: store(y, ch, at, ch * size + base, value, last),
            lambda at, ch=ch: start(ch, at),
            dec,
            rows,
            size,
            backward,
            8,
        )


def k_tables(rows, cells, dec_ref, lonc_ref, latc_ref, table_ref):
    row = jnp.broadcast_to(dec_ref[:, cells:], (rows, rows))
    own = iota((rows, rows), 0) == iota((rows, rows), 1)
    column = jnp.sum(jnp.where(own, row, 0.0), axis=1, keepdims=True)
    lonc = jnp.broadcast_to(column, (rows, cells))
    lonc_ref[...] = lonc
    first, second = both_halves(jnp.broadcast_to(dec_ref[:, :cells], (8, cells)))
    latc_ref[0] = first
    latc_ref[1] = second
    lon_tables(lonc, rows, cells, False, table_ref)


def k_lon_fwd(rows, k, cells, d_ref, table_ref, inside_ref, carried_ref):
    d_ref = d_ref.reshape(k * rows, cells)
    lon_local_rows(
        lambda y: d_ref[pl.ds(y, k, stride=rows), :], table_ref, rows, cells, inside_ref, carried_ref
    )


def spread_modes(v, pairs, transposed):
    source = v.T if transposed else v
    r, c = source.shape
    rows, columns = pairs * r, 3 * pairs * c
    exact = functools.partial(jnp.dot, precision=lax.Precision.HIGHEST, preferred_element_type=f32)
    block = lambda at, size: jnp.floor((at + 0.5) * (1.0 / size))
    at_row, at_column = iota((rows, r), 0), iota((c, columns), 1)
    pick_row = (at_row - block(at_row, r) * r == iota((rows, r), 1)).astype(f32)
    pick_column = (at_column - block(at_column, c) * c == iota((c, columns), 0)).astype(f32)
    everywhere = exact(exact(pick_row, source), pick_column)
    column = iota((1, columns), 1)
    part = block(column, pairs * c)
    own = block(iota((rows, 1), 0), r) == block(column - part * (pairs * c), c)
    full = jnp.where(own, everywhere, 0.0)
    high, low = halves(full)
    return jnp.where(part == 1.0, low.astype(f32), high.astype(f32)).astype(bf16)


def k_modes(pairs, v_ref, eig_ref, mask_ref, out_modes_ref, in_modes_ref):
    modes = v_ref.shape[0]
    cells = mask_ref.shape[1]
    v = v_ref[...]
    out_modes_ref[...] = spread_modes(v, pairs, True)
    in_modes_ref[...] = spread_modes(v, pairs, False)
    e = lax.broadcasted_iota(jnp.int32, (modes, cells), 0)
    low = lax.broadcasted_iota(jnp.int32, (modes, cells), 1) < cells // 2
    for m in range(pairs):
        used = jnp.where(low, eig_ref[m], eig_ref[m + pairs])
        mask_ref[m * modes : (m + 1) * modes] = jnp.where(e < used, 1.0, 0.0)


def row_spacing(size):
    return size + 8 if size // 8 % 2 == 0 else size


def k_back_tables(lon_ref, table_ref):
    lon_tables(lon_ref[...], *lon_ref.shape, True, table_ref)


def k_prepare(m_ref, a_ref, b_ref):
    members, levels, rows, _ = m_ref.shape
    pairs = members // 2
    apart = row_spacing(pairs * levels)

    def step(i, carry):
        for l in range(levels):
            a, b = swap_halves(m_ref[i, l].astype(f32), m_ref[i + pairs, l].astype(f32))
            at = pl.ds(i * levels + l, rows, stride=apart)
            a_ref[at, :] = a
            b_ref[at, :] = b
        return carry

    lax.fori_loop(0, pairs, step, 0)


def k_lat_first(rows, k, cells, n, chunks, *refs):
    inside_ref, lon_ref, lat_ref, *rest = refs
    blocks = [r[...] for r in rest[:n]]
    f_refs, out_refs = rest[n : n + 2], rest[n + 2 :]
    lonc = lon_ref[...]
    states = lon_incoming_states(lonc, blocks, rows, cells)
    c, leak, _ = lon_consts(lonc)
    added = lon_correction(states, lon_entering(c, leak, cells, False), rows, cells)
    half = k // 2
    for y in range(rows):
        row = inside_ref[y] + added(y)
        f_refs[0][y], f_refs[1][y] = swap_halves(row[:half], row[half:])
    zero = jnp.zeros((8, cells), f32)
    for part, f_ref in enumerate(f_refs):

        def store(y, ch, at, base, value, last, part=part):
            if last is not None:
                for s in range(4):
                    out_refs[part * chunks + ch][s, at, :] = last[s]

        sweep_chunks(
            lambda y, base: f_ref[y, pl.ds(pl.multiple_of(base, 8), 8), :],
            store,
            lambda ch, at: [zero] * 4,
            lat_ref[part, :1],
            rows,
            half,
            chunks,
            False,
        )


def k_pass_on(rows, part, carried_ref, got_ref, lat_ref, out_ref):
    t = lat_trans(lat_ref[part, :1], rows)
    got = [got_ref[s] for s in range(4)]
    for i in range(4):
        v = carried_ref[i]
        for j in range(i + 1):
            v = v + t[i - j] * got[j]
        out_ref[i] = v


def k_increment(rows, k, part, chunks, count, pairs, levels, *refs):
    f_ref, lat_ref, m_ref, mask_ref, modes_ref, *rest = refs
    out_ref, s_ref = rest[count:]
    cells = lat_ref.shape[-1]

    def store(y, ch, at, base, value, last):
        where = pl.ds(pl.multiple_of(base, 8), 8)
        s_ref[y, where, :] = value * mask_ref[where, :]

    sweep_chunks(
        lambda y, base: f_ref[y, pl.ds(pl.multiple_of(base, 8), 8), :],
        store,
        entering_states(rest[:count], chunks),
        lat_ref[part, :1],
        rows,
        k,
        chunks,
        False,
    )
    half = levels // 2
    low = iota((1, cells), 1) < float(cells // 2)
    apart = row_spacing(pairs * levels)
    for y in range(rows):
        profile = product3(modes_ref[...], right3(s_ref[y], 0))
        inc = None
        for m in range(pairs):
            at = y * apart + m * levels
            p = m_ref[at : at + levels, :] * profile[m * levels : (m + 1) * levels]
            inc = p if inc is None else inc + p
        inc = inc + pltpu.roll(inc, cells // 2, 1)
        out_ref[y] = jnp.where(low, inc[:half], inc[half:])


def k_gradient(rows, k, part, chunks, pairs, levels, *refs):
    inc_ref, got_ref, obs_ref, m_ref, mask_ref, modes_ref, lat_ref, g_ref, *carried_refs = refs
    cells = lat_ref.shape[-1]
    obs_ref = obs_ref.reshape(levels * rows, cells)
    size = pairs * levels
    apart = row_spacing(size)
    for y in range(rows):
        inc = jnp.concatenate(both_halves(inc_ref[y] + got_ref[y]), axis=0)
        w = inc * both_halves(obs_ref[pl.ds(y, levels, stride=rows), :])[part]
        m = m_ref[y * apart : y * apart + size, :]
        weighted = (m.reshape(pairs, levels, cells) * w[None]).reshape(size, cells)
        g_ref[y] = product3(modes_ref[...], right3(weighted, 0)) * mask_ref[...]
    zero8 = jnp.zeros((8, cells), f32)

    def store(y, ch, at, base, value, last):
        if last is not None:
            for s in range(4):
                carried_refs[ch][s, at, :] = last[s]

    sweep_chunks(
        lambda y, base: g_ref[y, pl.ds(pl.multiple_of(base, 8), 8), :],
        store,
        lambda ch, at: [zero8] * 4,
        lat_ref[part, :1],
        rows,
        k,
        chunks,
        True,
    )


def k_lon_bwd(rows, k, cells, chunks, count, *refs):
    g_refs, lat_ref, table_ref, rest = refs[:2], refs[2], refs[3], refs[4:]
    inside_ref, carried_ref, p_ref = rest[2 * count :]
    half = k // 2
    for part in range(2):
        g_ref = g_refs[part]

        def store(y, ch, at, base, value, last, part=part):
            p_ref[part, y, pl.ds(pl.multiple_of(base, 8), 8), :] = value

        sweep_chunks(
            lambda y, base: g_ref[y, pl.ds(pl.multiple_of(base, 8), 8), :],
            store,
            entering_states(rest[part * count : (part + 1) * count], chunks),
            lat_ref[part, :1],
            rows,
            half,
            chunks,
            True,
        )

    def load_row(y):
        return jnp.concatenate(swap_halves(p_ref[0, y], p_ref[1, y]), axis=0)

    lon_local_rows(load_row, table_ref, rows, cells, inside_ref, carried_ref)


def k_sums(rows, k, cells, n, *refs):
    inside_ref, lon_ref, d_ref, r_ref, *rest = refs
    d_ref = d_ref.reshape(k * rows, cells)
    r_ref = r_ref.reshape(k * rows, cells)
    blocks = [r[...] for r in rest[:n]]
    h_ref, sums_ref = rest[n:]
    lonc = lon_ref[...]
    states = lon_incoming_states(lonc, blocks, rows, cells)
    c, leak, _ = lon_consts(lonc)
    added = lon_correction(states, lon_entering(c, leak, cells, True), rows, cells)
    for y in range(rows):
        at = pl.ds(y, k, stride=rows)
        h_ref[at, :] = inside_ref[y] + added(y)
    block = 64
    zero = jnp.zeros((8, cells), f32)

    def step(i, acc):
        at = pl.ds(pl.multiple_of(i * block, 8), block)
        d = d_ref[at, :]
        r = r_ref[at, :]
        h = h_ref[at, :] + d
        h_ref[at, :] = h
        fold = lambda v: v.reshape(block // 8, 8, cells).sum(axis=0)
        return (acc[0] + fold(r * r), acc[1] + fold(d * h), acc[2] + fold(r * h), acc[3] + fold(h * h))

    acc = lax.fori_loop(0, (k * rows) // block, step, (zero,) * 4)
    out = [a.sum(axis=0, keepdims=True) for a in acc]
    sums_ref[...] = jnp.concatenate(out + [jnp.zeros((4, cells), f32)], axis=0)


def k_update(pieces, sums_ref, control_ref, r_ref, d_ref, h_ref, *rest):
    outs, news, sems = rest[:3], rest[3:6], rest[6]
    sums = jnp.sum(sums_ref[...], axis=1, keepdims=True)
    rr, dh, rh, hh = (sums[i : i + 1].reshape(1, 1, 1) for i in range(4))
    step = rr / dh
    norm_new = rr - 2.0 * step * rh + step * step * hh
    beta = norm_new / rr
    size = d_ref.shape[0] // pieces
    copies = []
    for i in range(pieces):
        at = pl.ds(i * size, size)
        d = d_ref[at]
        nr = r_ref[at] - step * h_ref[at]
        for j, v in enumerate((control_ref[at] + step * d, nr, nr + beta * d)):
            news[j][at] = v
            copy = pltpu.make_async_copy(news[j].at[at], outs[j].at[at], sems.at[j, i])
            copy.start()
            copies.append(copy)
    for copy in copies:
        copy.wait()


def call(body, outs, ins, specs=None, out_specs=None, scratch=(), cost=None):
    return pl.pallas_call(
        body,
        out_shape=outs,
        in_specs=specs or [VM] * len(ins),
        out_specs=out_specs or jax.tree.map(lambda _: VM, outs),
        scratch_shapes=scratch,
        cost_estimate=None if cost is None else pl.CostEstimate(flops=cost, bytes_accessed=1000, transcendentals=0),
        compiler_params=pltpu.CompilerParams(vmem_limit_bytes=16 * 1024 * 1024),
    )(*ins)


def sds(*shape):
    return jax.ShapeDtypeStruct(shape, f32)


def lon_exchange(carried, backward):
    n = lax.axis_size("lon")
    sign = -1 if backward else 1
    got = [
        lax.ppermute(carried, "lon", [(j, (j + sign * r) % n) for j in range(n)]) for r in range(1, n)
    ]
    return got + [carried]


def pass_on(part, got, latc, rows, c):
    return call(functools.partial(k_pass_on, rows, c), sds(*part.shape), [part, got, latc])


def lat_carry(halves, latc, rows, backward):
    n = lax.axis_size("lat")
    at = (lambda i: n - 1 - i) if backward else (lambda i: i)
    got = [[[] for _ in chunks] for chunks in halves]
    for h in range(n - 1):
        for c, chunks in enumerate(halves):
            for i, part in enumerate(chunks):
                v = pass_on(part, got[c][i][-1], latc, rows, c) if h else part
                got[c][i].append(lax.ppermute(v, "lat", [(at(h), at(h + 1))]))
    return [[g for chunk in half for g in chunk] for half in got]


def all_sum(v, axes, steps):
    total = 1
    for a in axes:
        total *= lax.axis_size(a)
    masks = [0]
    for s in steps:
        masks = masks + [m ^ s for m in masks]
    got = [lax.ppermute(v, axes, [(i, i ^ m) for i in range(total)]) for m in masks[1:]]
    for g in got:
        v = v + g
    return v


def powers(n):
    out, d = [], 1
    while d < n:
        out.append(d)
        d *= 2
    return out


def reduce_everywhere(v):
    n_lon, n_lat, n_mem = (lax.axis_size(a) for a in ("lon", "lat", "mem"))
    for s in powers(n_mem):
        v = all_sum(v, ("mem",), [s])
    for s in powers(n_lon):
        v = all_sum(v, ("lon",), [s])
    lat = powers(n_lat)
    for i in range(0, len(lat), 2):
        v = all_sum(v, ("lat",), lat[i : i + 2])
    return v


def iteration(control, residual, direction, members, vert_modes, eig_count, lon_decay, lat_decay, obs_weight):
    k, rows, cells = direction.shape
    mcount, levels = members.shape[:2]
    n_lon, n_mem = lax.axis_size("lon"), lax.axis_size("mem")
    half = k // 2
    pairs = mcount // 2
    chunks, back_chunks = 2, 2
    states = lambda chunks: (sds(4, half // chunks, cells),) * chunks

    decays = jnp.concatenate([lat_decay, lon_decay]).reshape(1, cells + rows)
    lonc, latc, tables = call(
        functools.partial(k_tables, rows, cells),
        (sds(rows, cells), sds(2, 8, cells), jax.ShapeDtypeStruct((rows, 3 * cells, 2 * cells), bf16)),
        [decays],
        cost=10**9,
    )
    inside, carried = call(
        functools.partial(k_lon_fwd, rows, k, cells),
        (sds(rows, k, cells), sds(4 * rows, k)),
        [direction, tables],
    )
    packed = call(
        k_prepare, (sds(rows * row_spacing(pairs * levels), cells),) * 2, [members], cost=10**9
    )
    back_tables = call(
        k_back_tables, jax.ShapeDtypeStruct((rows, 3 * cells, 2 * cells), bf16), [lonc], cost=10**9
    )
    mask, out_modes, in_modes = call(
        functools.partial(k_modes, pairs),
        (
            sds(half, cells),
            jax.ShapeDtypeStruct((pairs * levels, 3 * half), bf16),
            jax.ShapeDtypeStruct((half, 3 * pairs * levels), bf16),
        ),
        [vert_modes, eig_count],
        specs=[VM, SM],
        cost=10**9,
    )
    blocks = lon_exchange(carried, False)
    fa, fb, *parts = call(
        functools.partial(k_lat_first, rows, k, cells, n_lon, chunks),
        (sds(rows, half, cells),) * 2 + states(chunks) * 2,
        [inside, lonc, latc, *blocks],
    )
    got = lat_carry([parts[:chunks], parts[chunks:]], latc, rows, False)
    count = len(got[0])
    fields = (fa, fb)
    inc = [None, None]
    for part in range(2):
        inc[part] = call(
            functools.partial(k_increment, rows, half, part, chunks, count, pairs, levels),
            sds(rows, levels // 2, cells),
            [fields[part], latc, packed[part], mask, out_modes, *got[part]],
            scratch=[pltpu.VMEM((rows, half, cells), f32)],
        )
    grads, sends = [None, None], [None, None]
    for part in range(2):
        v = inc[part]
        step = 1
        while step * 2 < n_mem:
            v = v + lax.ppermute(v, "mem", [(i, i ^ step) for i in range(n_mem)])
            step *= 2
        other = lax.ppermute(v, "mem", [(i, i ^ step) for i in range(n_mem)])
        grads[part], *sends[part] = call(
            functools.partial(k_gradient, rows, half, part, back_chunks, pairs, levels),
            (sds(rows, half, cells),) + states(back_chunks),
            [v, other, obs_weight, packed[part], mask, in_modes, latc],
        )
    got = lat_carry(sends, latc, rows, True)
    count = len(got[0])
    inside, carried = call(
        functools.partial(k_lon_bwd, rows, k, cells, back_chunks, count),
        (sds(rows, k, cells), sds(4 * rows, k)),
        [*grads, latc, back_tables, *got[0], *got[1]],
        scratch=[pltpu.VMEM((2, rows, half, cells), f32)],
    )
    blocks = lon_exchange(carried, True)
    h, sums = call(
        functools.partial(k_sums, rows, k, cells, n_lon),
        (sds(k * rows, cells), sds(8, cells)),
        [inside, lonc, direction, residual, *blocks],
    )
    sums = reduce_everywhere(sums)
    pieces = 4 if k % 4 == 0 else 1
    outs = call(
        functools.partial(k_update, pieces),
        (sds(k, rows, cells),) * 3,
        [sums, control, residual, direction, h.reshape(k, rows, cells)],
        out_specs=(pl.BlockSpec(memory_space=pl.ANY),) * 3,
        scratch=[pltpu.VMEM((k, rows, cells), f32)] * 3 + [pltpu.SemaphoreType.DMA((3, pieces))],
    )
    return tuple(outs)


def solution(mesh):
    field = P("mem", "lat", "lon")
    placed = (
        field,
        field,
        field,
        P("mem", None, "lat", "lon"),
        P(),
        P("mem"),
        P("lat"),
        P("lon"),
        P(None, "lat", "lon"),
    )
    return jax.shard_map(iteration, mesh=mesh, in_specs=placed, out_specs=(field,) * 3, check_vma=False)
```

```python
import functools
import jax
import jax.numpy as jnp
from jax import lax
from jax.experimental import pallas as pl
from jax.experimental.pallas import tpu as pltpu
from jax.sharding import PartitionSpec as P


f32 = jnp.float32
bf16 = jnp.bfloat16
VM = pl.BlockSpec(memory_space=pltpu.VMEM)
SM = pl.BlockSpec(memory_space=pltpu.SMEM)


def choose(length, i):
    r = 1.0
    for k in range(i):
        r = r * (length + k) / (k + 1)
    return r


def rising(v, degree):
    r = jnp.ones_like(v)
    for k in range(degree):
        r = r * (v + (k + 1.0)) * (1.0 / (k + 1.0))
    return r


def halves(v):
    high = v.astype(bf16)
    return high, (v - high.astype(f32)).astype(bf16)


def left3(v, axis):
    high, low = halves(v)
    return jnp.concatenate([high, low, high], axis=axis)


def right3(v, axis):
    high, low = halves(v)
    return jnp.concatenate([high, high, low], axis=axis)


def product3(a, b):
    return jnp.dot(a, b, preferred_element_type=f32)


def iota(shape, dim):
    return lax.broadcasted_iota(jnp.int32, shape, dim).astype(f32)


def lon_consts(lonc):
    c = lonc
    q = jnp.exp(-c)
    leak = 1.0 - q
    return c, leak, 2.5 / jnp.sqrt(leak)


def lon_kernel_matrix(c_row, gain_row, cells, backward):
    a = iota((cells, cells), 0)
    b = iota((cells, cells), 1)
    lag = a - b if backward else b - a
    pos = jnp.maximum(lag, 0.0)
    shaped = rising(pos, 3) * jnp.exp(-pos * c_row) * gain_row
    return jnp.where(lag >= 0.0, shaped, 0.0)


def masked_rows(parts, y):
    rows = iota(parts[0].shape, 0)
    return jnp.concatenate([jnp.where(rows == float(y), p, 0.0) for p in parts], axis=0)


def lon_finals(c, leak, scale, cells, backward):
    x = iota(c.shape, 1)
    remain = x if backward else (cells - 1.0) - x
    decay = jnp.exp(-remain * c)
    return [leak ** (s + 1) * scale * rising(remain, s) * decay for s in range(4)]


def lon_entering(c, leak, cells, backward):
    x = iota(c.shape, 1)
    place = (cells - 1.0) - x if backward else x
    decay = jnp.exp(-(place + 1.0) * c)
    return [leak ** (3 - s) * rising(place, 3 - s) * decay for s in range(4)]


def lon_tables(lonc, rows, cells, backward, table_ref):
    c, leak, scale = lon_consts(lonc)
    gain = leak**4 * scale
    finals = lon_finals(c, leak, scale, cells, backward)
    spare = jnp.zeros((cells - 4 * rows, cells), f32)
    finals = jnp.concatenate(finals + [spare], axis=0).T
    column = lax.broadcasted_iota(jnp.int32, (cells, cells), 1)
    for y in range(rows):
        inside = lon_kernel_matrix(c[y : y + 1], gain[y : y + 1], cells, backward)
        leaving = jnp.where(lax.rem(column, rows) == y, finals, 0.0)
        table_ref[y] = right3(jnp.concatenate([inside, leaving], axis=1), 0)


def lon_local_rows(load_row, table_ref, rows, cells, inside_ref, carried_ref):
    carried = None
    for y in range(rows):
        both = product3(left3(load_row(y), 1), table_ref[y])
        inside_ref[y] = both[:, :cells]
        carried = both[:, cells:] if carried is None else carried + both[:, cells:]
    carried_ref[...] = carried.T[: 4 * rows]


def lon_incoming_states(lonc, blocks, rows, cells):
    k = blocks[0].shape[1]
    n = len(blocks)
    c = jnp.broadcast_to(lonc[:, :1], (rows, k))
    leak = 1.0 - jnp.exp(-c)

    def trans(r):
        closing = jnp.exp(-float(r * cells) * c)
        return [choose(r * cells, i) * leak**i * closing for i in range(4)]

    total = [jnp.zeros((rows, k), f32) for _ in range(4)]
    for r in range(n):
        part = [blocks[r][s * rows : (s + 1) * rows] for s in range(4)]
        if r:
            t = trans(r)
            part = [sum(t[i - j] * part[j] for j in range(i + 1)) for i in range(4)]
        total = [a + b for a, b in zip(total, part)]
    t = trans(n)
    solved = []
    for i in range(4):
        v = total[i]
        for j in range(i):
            v = v + t[i - j] * solved[j]
        solved.append(v / (1.0 - t[0]))
    return jnp.concatenate(solved, axis=0)


def lon_correction(states, entering, rows, cells):
    high = states.astype(bf16).astype(f32)
    low = states - high
    spare = jnp.zeros((cells - 12 * rows, states.shape[1]), f32)
    left = jnp.concatenate([high, low, high, spare], axis=0).T.astype(bf16)
    spare = jnp.zeros((cells - 12 * rows, cells), bf16)
    return lambda y: product3(left, jnp.concatenate([right3(masked_rows(entering, y), 0), spare], axis=0))


def lat_consts(dec):
    q = jnp.exp(-dec)
    leak = 1.0 - q
    return q, leak, leak * (2.5 / jnp.sqrt(leak))


def lat_sweep(load, store, start, dec, rows, k, backward, block):
    q1, l1, g1 = lat_consts(dec)
    x = dec.shape[1]
    q = jnp.broadcast_to(q1, (block, x))
    leak = jnp.broadcast_to(l1, (block, x))
    gain = jnp.broadcast_to(g1, (block, x))
    order = range(rows - 1, -1, -1) if backward else range(rows)

    def step(i, carry):
        at = pl.ds(pl.multiple_of(i * block, 8), block)
        u = start(at)
        for y in order:
            feed = gain * load(y, at, i * block)
            u0 = q * u[0] + feed
            u1 = q * u[1] + leak * u0
            u2 = q * u[2] + leak * u1
            u3 = q * u[3] + leak * u2
            u = [u0, u1, u2, u3]
            store(y, at, i * block, u3, u if y == order[-1] else None)
        return carry

    lax.fori_loop(0, k // block, step, 0)


def swap_halves(a, b):
    half = a.shape[-1] // 2
    low = iota((1,) * (a.ndim - 1) + (a.shape[-1],), a.ndim - 1) < float(half)
    turn = lambda v: pltpu.roll(v, half, v.ndim - 1)
    return jnp.where(low, a, turn(b)), jnp.where(low, turn(a), b)


def both_halves(v):
    return swap_halves(v, v)


def lat_trans(dec, rows):
    leak = 1.0 - jnp.exp(-dec)
    closing = jnp.exp(-float(rows) * dec)
    return [choose(rows, i) * leak**i * closing for i in range(4)]


def entering_states(got, chunks, block):
    hops = len(got) // chunks
    mine = [block == float(h + 1) for h in range(hops)]

    def at(chunk, where):
        out = []
        for s in range(4):
            v = jnp.zeros(block.shape, f32)
            for m, p in zip(mine, got[chunk * hops : (chunk + 1) * hops]):
                v = jnp.where(m, p[s, where, :], v)
            out.append(v)
        return out

    return at


def sweep_chunks(load, store, start, dec, rows, k, chunks, backward):
    size = k // chunks
    for ch in range(chunks):
        lat_sweep(
            lambda y, at, base, ch=ch: load(y, ch * size + base),
            lambda y, at, base, value, last, ch=ch: store(y, ch, at, ch * size + base, value, last),
            lambda at, ch=ch: start(ch, at),
            dec,
            rows,
            size,
            backward,
            8,
        )


def k_tables(rows, cells, dec_ref, lonc_ref, latc_ref, table_ref, block_ref):
    block_ref[...] = jnp.full((8, cells), lax.axis_index("lat").astype(f32))
    row = jnp.broadcast_to(dec_ref[:, cells:], (rows, rows))
    own = iota((rows, rows), 0) == iota((rows, rows), 1)
    column = jnp.sum(jnp.where(own, row, 0.0), axis=1, keepdims=True)
    lonc = jnp.broadcast_to(column, (rows, cells))
    lonc_ref[...] = lonc
    first, second = both_halves(jnp.broadcast_to(dec_ref[:, :cells], (8, cells)))
    latc_ref[0] = first
    latc_ref[1] = second
    lon_tables(lonc, rows, cells, False, table_ref)


def k_lon_fwd(rows, k, cells, d_ref, table_ref, inside_ref, carried_ref):
    d_ref = d_ref.reshape(k * rows, cells)
    lon_local_rows(
        lambda y: d_ref[pl.ds(y, k, stride=rows), :], table_ref, rows, cells, inside_ref, carried_ref
    )


def spread_modes(v, pairs, transposed):
    source = v.T if transposed else v
    r, c = source.shape
    rows, columns = pairs * r, 3 * pairs * c
    exact = functools.partial(jnp.dot, precision=lax.Precision.HIGHEST, preferred_element_type=f32)
    block = lambda at, size: jnp.floor((at + 0.5) * (1.0 / size))
    at_row, at_column = iota((rows, r), 0), iota((c, columns), 1)
    pick_row = (at_row - block(at_row, r) * r == iota((rows, r), 1)).astype(f32)
    pick_column = (at_column - block(at_column, c) * c == iota((c, columns), 0)).astype(f32)
    everywhere = exact(exact(pick_row, source), pick_column)
    column = iota((1, columns), 1)
    part = block(column, pairs * c)
    own = block(iota((rows, 1), 0), r) == block(column - part * (pairs * c), c)
    full = jnp.where(own, everywhere, 0.0)
    high, low = halves(full)
    return jnp.where(part == 1.0, low.astype(f32), high.astype(f32)).astype(bf16)


def k_out_modes(pairs, v_ref, eig_ref, mask_ref, modes_ref):
    modes = v_ref.shape[0]
    cells = mask_ref.shape[1]
    modes_ref[...] = spread_modes(v_ref[...], pairs, True)
    e = lax.broadcasted_iota(jnp.int32, (modes, cells), 0)
    low = lax.broadcasted_iota(jnp.int32, (modes, cells), 1) < cells // 2
    for m in range(pairs):
        used = jnp.where(low, eig_ref[m], eig_ref[m + pairs])
        mask_ref[m * modes : (m + 1) * modes] = jnp.where(e < used, 1.0, 0.0)


def k_in_modes(pairs, v_ref, modes_ref):
    modes_ref[...] = spread_modes(v_ref[...], pairs, False)


def row_spacing(size):
    return size + 8 if size // 8 % 2 == 0 else size


def k_back_tables(lon_ref, table_ref):
    lon_tables(lon_ref[...], *lon_ref.shape, True, table_ref)


def k_prepare(m_ref, a_ref, b_ref):
    members, levels, rows, _ = m_ref.shape
    pairs = members // 2
    apart = row_spacing(pairs * levels)

    def step(i, carry):
        for l in range(levels):
            a, b = swap_halves(m_ref[i, l].astype(f32), m_ref[i + pairs, l].astype(f32))
            at = pl.ds(i * levels + l, rows, stride=apart)
            a_ref[at, :] = a
            b_ref[at, :] = b
        return carry

    lax.fori_loop(0, pairs, step, 0)


def k_lat_first(rows, k, cells, n, chunks, *refs):
    inside_ref, lon_ref, lat_ref, *rest = refs
    blocks = [r[...] for r in rest[:n]]
    f_refs, out_refs = rest[n : n + 2], rest[n + 2 :]
    lonc = lon_ref[...]
    states = lon_incoming_states(lonc, blocks, rows, cells)
    c, leak, _ = lon_consts(lonc)
    added = lon_correction(states, lon_entering(c, leak, cells, False), rows, cells)
    half = k // 2
    for y in range(rows):
        row = inside_ref[y] + added(y)
        f_refs[0][y], f_refs[1][y] = swap_halves(row[:half], row[half:])
    zero = jnp.zeros((8, cells), f32)
    for part, f_ref in enumerate(f_refs):

        def store(y, ch, at, base, value, last, part=part):
            if last is not None:
                for s in range(4):
                    out_refs[part * chunks + ch][s, at, :] = last[s]

        sweep_chunks(
            lambda y, base: f_ref[y, pl.ds(pl.multiple_of(base, 8), 8), :],
            store,
            lambda ch, at: [zero] * 4,
            lat_ref[part, :1],
            rows,
            half,
            chunks,
            False,
        )


def k_pass_on(rows, part, carried_ref, got_ref, lat_ref, out_ref):
    t = lat_trans(lat_ref[part, :1], rows)
    got = [got_ref[s] for s in range(4)]
    for i in range(4):
        v = carried_ref[i]
        for j in range(i + 1):
            v = v + t[i - j] * got[j]
        out_ref[i] = v


def k_increment(rows, k, part, chunks, count, pairs, levels, *refs):
    f_ref, lat_ref, block_ref, m_ref, mask_ref, modes_ref, *rest = refs
    out_ref, s_ref = rest[count:]
    cells = lat_ref.shape[-1]

    def store(y, ch, at, base, value, last):
        where = pl.ds(pl.multiple_of(base, 8), 8)
        s_ref[y, where, :] = value * mask_ref[where, :]

    sweep_chunks(
        lambda y, base: f_ref[y, pl.ds(pl.multiple_of(base, 8), 8), :],
        store,
        entering_states(rest[:count], chunks, block_ref[...]),
        lat_ref[part, :1],
        rows,
        k,
        chunks,
        False,
    )
    half = levels // 2
    low = iota((1, cells), 1) < float(cells // 2)
    apart = row_spacing(pairs * levels)
    for y in range(rows):
        profile = product3(modes_ref[...], right3(s_ref[y], 0))
        inc = None
        for m in range(pairs):
            at = y * apart + m * levels
            p = m_ref[at : at + levels, :] * profile[m * levels : (m + 1) * levels]
            inc = p if inc is None else inc + p
        inc = inc + pltpu.roll(inc, cells // 2, 1)
        out_ref[y] = jnp.where(low, inc[:half], inc[half:])


def k_gradient(rows, k, part, chunks, pairs, levels, *refs):
    inc_ref, got_ref, obs_ref, m_ref, mask_ref, modes_ref, lat_ref, g_ref, *carried_refs = refs
    cells = lat_ref.shape[-1]
    obs_ref = obs_ref.reshape(levels * rows, cells)
    size = pairs * levels
    apart = row_spacing(size)
    for y in range(rows):
        inc = jnp.concatenate(both_halves(inc_ref[y] + got_ref[y]), axis=0)
        w = inc * both_halves(obs_ref[pl.ds(y, levels, stride=rows), :])[part]
        m = m_ref[y * apart : y * apart + size, :]
        weighted = (m.reshape(pairs, levels, cells) * w[None]).reshape(size, cells)
        g_ref[y] = product3(modes_ref[...], right3(weighted, 0)) * mask_ref[...]
    zero8 = jnp.zeros((8, cells), f32)

    def store(y, ch, at, base, value, last):
        if last is not None:
            for s in range(4):
                carried_refs[ch][s, at, :] = last[s]

    sweep_chunks(
        lambda y, base: g_ref[y, pl.ds(pl.multiple_of(base, 8), 8), :],
        store,
        lambda ch, at: [zero8] * 4,
        lat_ref[part, :1],
        rows,
        k,
        chunks,
        True,
    )


def k_lon_bwd(rows, k, cells, chunks, count, blocks, *refs):
    g_refs, lat_ref, block_ref, table_ref, rest = refs[:2], refs[2], refs[3], refs[4], refs[5:]
    block = (blocks - 1.0) - block_ref[...]
    inside_ref, carried_ref, p_ref = rest[2 * count :]
    half = k // 2
    for part in range(2):
        g_ref = g_refs[part]

        def store(y, ch, at, base, value, last, part=part):
            p_ref[part, y, pl.ds(pl.multiple_of(base, 8), 8), :] = value

        sweep_chunks(
            lambda y, base: g_ref[y, pl.ds(pl.multiple_of(base, 8), 8), :],
            store,
            entering_states(rest[part * count : (part + 1) * count], chunks, block),
            lat_ref[part, :1],
            rows,
            half,
            chunks,
            True,
        )

    def load_row(y):
        return jnp.concatenate(swap_halves(p_ref[0, y], p_ref[1, y]), axis=0)

    lon_local_rows(load_row, table_ref, rows, cells, inside_ref, carried_ref)


def k_sums(rows, k, cells, n, *refs):
    inside_ref, lon_ref, d_ref, r_ref, *rest = refs
    d_ref = d_ref.reshape(k * rows, cells)
    r_ref = r_ref.reshape(k * rows, cells)
    blocks = [r[...] for r in rest[:n]]
    h_ref, sums_ref = rest[n:]
    lonc = lon_ref[...]
    states = lon_incoming_states(lonc, blocks, rows, cells)
    c, leak, _ = lon_consts(lonc)
    added = lon_correction(states, lon_entering(c, leak, cells, True), rows, cells)
    for y in range(rows):
        at = pl.ds(y, k, stride=rows)
        h_ref[at, :] = inside_ref[y] + added(y)
    block = 64
    zero = jnp.zeros((8, cells), f32)

    def step(i, acc):
        at = pl.ds(pl.multiple_of(i * block, 8), block)
        d = d_ref[at, :]
        r = r_ref[at, :]
        h = h_ref[at, :] + d
        h_ref[at, :] = h
        fold = lambda v: v.reshape(block // 8, 8, cells).sum(axis=0)
        return (acc[0] + fold(r * r), acc[1] + fold(d * h), acc[2] + fold(r * h), acc[3] + fold(h * h))

    acc = lax.fori_loop(0, (k * rows) // block, step, (zero,) * 4)
    out = [a.sum(axis=0, keepdims=True) for a in acc]
    sums_ref[...] = jnp.concatenate(out + [jnp.zeros((4, cells), f32)], axis=0)


def k_update(pieces, sums_ref, control_ref, r_ref, d_ref, h_ref, *rest):
    outs, news, sems = rest[:3], rest[3:6], rest[6]
    sums = jnp.sum(sums_ref[...], axis=1, keepdims=True)
    rr, dh, rh, hh = (sums[i : i + 1].reshape(1, 1, 1) for i in range(4))
    step = rr / dh
    norm_new = rr - 2.0 * step * rh + step * step * hh
    beta = norm_new / rr
    size = d_ref.shape[0] // pieces
    copies = []
    for i in range(pieces):
        at = pl.ds(i * size, size)
        d = d_ref[at]
        nr = r_ref[at] - step * h_ref[at]
        for j, v in enumerate((control_ref[at] + step * d, nr, nr + beta * d)):
            news[j][at] = v
            copy = pltpu.make_async_copy(news[j].at[at], outs[j].at[at], sems.at[j, i])
            copy.start()
            copies.append(copy)
    for copy in copies:
        copy.wait()


def call(body, outs, ins, specs=None, out_specs=None, scratch=(), cost=None):
    return pl.pallas_call(
        body,
        out_shape=outs,
        in_specs=specs or [VM] * len(ins),
        out_specs=out_specs or jax.tree.map(lambda _: VM, outs),
        scratch_shapes=scratch,
        cost_estimate=None if cost is None else pl.CostEstimate(flops=cost, bytes_accessed=1000, transcendentals=0),
        compiler_params=pltpu.CompilerParams(vmem_limit_bytes=16 * 1024 * 1024),
    )(*ins)


def sds(*shape):
    return jax.ShapeDtypeStruct(shape, f32)


def lon_exchange(carried, backward):
    n = lax.axis_size("lon")
    sign = -1 if backward else 1
    got = [
        lax.ppermute(carried, "lon", [(j, (j + sign * r) % n) for j in range(n)]) for r in range(1, n)
    ]
    return got + [carried]


def pass_on(part, got, latc, rows, c):
    return call(functools.partial(k_pass_on, rows, c), sds(*part.shape), [part, got, latc])


def hop_pairs(a, b):
    n, n_mem = lax.axis_size("lat"), lax.axis_size("mem")
    if n_mem % 2:
        return [(a * n_mem + i, b * n_mem + i) for i in range(n_mem)]
    to = lambda z, i: (b, i) if z == a else (a, i) if z == b else (z, i ^ 1)
    flat = lambda z, i: z * n_mem + i
    return [(flat(z, i), flat(*to(z, i))) for z in range(n) for i in range(n_mem)]


def lat_carry(halves, latc, rows, backward):
    n = lax.axis_size("lat")
    at = (lambda i: n - 1 - i) if backward else (lambda i: i)
    got = [[[] for _ in chunks] for chunks in halves]
    for h in range(n - 1):
        pairs = hop_pairs(at(h), at(h + 1))
        for c, chunks in enumerate(halves):
            for i, part in enumerate(chunks):
                v = pass_on(part, got[c][i][-1], latc, rows, c) if h else part
                got[c][i].append(lax.ppermute(v, ("lat", "mem"), pairs))
    return [[g for chunk in half for g in chunk] for half in got]


def all_sum(v, axes, steps):
    total = 1
    for a in axes:
        total *= lax.axis_size(a)
    masks = [0]
    for s in steps:
        masks = masks + [m ^ s for m in masks]
    got = [lax.ppermute(v, axes, [(i, i ^ m) for i in range(total)]) for m in masks[1:]]
    for g in got:
        v = v + g
    return v


def powers(n):
    out, d = [], 1
    while d < n:
        out.append(d)
        d *= 2
    return out


def reduce_everywhere(v):
    n_lon, n_lat, n_mem = (lax.axis_size(a) for a in ("lon", "lat", "mem"))
    for s in powers(n_mem):
        v = all_sum(v, ("mem",), [s])
    for s in powers(n_lon):
        v = all_sum(v, ("lon",), [s])
    lat = powers(n_lat)
    for i in range(0, len(lat), 2):
        v = all_sum(v, ("lat",), lat[i : i + 2])
    return v


def iteration(control, residual, direction, members, vert_modes, eig_count, lon_decay, lat_decay, obs_weight):
    k, rows, cells = direction.shape
    mcount, levels = members.shape[:2]
    n_lon, n_mem = lax.axis_size("lon"), lax.axis_size("mem")
    half = k // 2
    pairs = mcount // 2
    chunks, back_chunks = 2, 2
    states = lambda chunks: (sds(4, half // chunks, cells),) * chunks

    decays = jnp.concatenate([lat_decay, lon_decay]).reshape(1, cells + rows)
    lonc, latc, tables, block = call(
        functools.partial(k_tables, rows, cells),
        (sds(rows, cells), sds(2, 8, cells), jax.ShapeDtypeStruct((rows, 3 * cells, 2 * cells), bf16), sds(8, cells)),
        [decays],
        cost=10**9,
    )
    inside, carried = call(
        functools.partial(k_lon_fwd, rows, k, cells), (sds(rows, k, cells), sds(4 * rows, k)), [direction, tables]
    )
    packed = call(k_prepare, (sds(rows * row_spacing(pairs * levels), cells),) * 2, [members], cost=10**9)
    back_tables = call(k_back_tables, jax.ShapeDtypeStruct((rows, 3 * cells, 2 * cells), bf16), [lonc], cost=10**9)
    mask, out_modes = call(
        functools.partial(k_out_modes, pairs),
        (sds(half, cells), jax.ShapeDtypeStruct((pairs * levels, 3 * half), bf16)),
        [vert_modes, eig_count],
        specs=[VM, SM],
        cost=10**9,
    )
    in_modes = call(
        functools.partial(k_in_modes, pairs),
        jax.ShapeDtypeStruct((half, 3 * pairs * levels), bf16),
        [vert_modes],
        cost=10**9,
    )
    blocks = lon_exchange(carried, False)
    fa, fb, *parts = call(
        functools.partial(k_lat_first, rows, k, cells, n_lon, chunks),
        (sds(rows, half, cells),) * 2 + states(chunks) * 2,
        [inside, lonc, latc, *blocks],
    )
    got = lat_carry([parts[:chunks], parts[chunks:]], latc, rows, False)
    count = len(got[0])
    fields = (fa, fb)
    inc = [None, None]
    for part in range(2):
        inc[part] = call(
            functools.partial(k_increment, rows, half, part, chunks, count, pairs, levels),
            sds(rows, levels // 2, cells),
            [fields[part], latc, block, packed[part], mask, out_modes, *got[part]],
            scratch=[pltpu.VMEM((rows, half, cells), f32)],
        )
    grads, sends = [None, None], [None, None]
    for part in range(2):
        v = inc[part]
        step = 1
        while step * 2 < n_mem:
            v = v + lax.ppermute(v, "mem", [(i, i ^ step) for i in range(n_mem)])
            step *= 2
        other = lax.ppermute(v, "mem", [(i, i ^ step) for i in range(n_mem)])
        grads[part], *sends[part] = call(
            functools.partial(k_gradient, rows, half, part, back_chunks, pairs, levels),
            (sds(rows, half, cells),) + states(back_chunks),
            [v, other, obs_weight, packed[part], mask, in_modes, latc],
        )
    got = lat_carry(sends, latc, rows, True)
    count = len(got[0])
    inside, carried = call(
        functools.partial(k_lon_bwd, rows, k, cells, back_chunks, count, lax.axis_size("lat")),
        (sds(rows, k, cells), sds(4 * rows, k)),
        [*grads, latc, block, back_tables, *got[0], *got[1]],
        scratch=[pltpu.VMEM((2, rows, half, cells), f32)],
    )
    blocks = lon_exchange(carried, True)
    h, sums = call(
        functools.partial(k_sums, rows, k, cells, n_lon),
        (sds(k * rows, cells), sds(8, cells)),
        [inside, lonc, direction, residual, *blocks],
    )
    sums = reduce_everywhere(sums)
    pieces = 4 if k % 4 == 0 else 1
    outs = call(
        functools.partial(k_update, pieces),
        (sds(k, rows, cells),) * 3,
        [sums, control, residual, direction, h.reshape(k, rows, cells)],
        out_specs=(pl.BlockSpec(memory_space=pl.ANY),) * 3,
        scratch=[pltpu.VMEM((k, rows, cells), f32)] * 3 + [pltpu.SemaphoreType.DMA((3, pieces))],
    )
    return tuple(outs)


def solution(mesh):
    field = P("mem", "lat", "lon")
    placed = (
        field,
        field,
        field,
        P("mem", None, "lat", "lon"),
        P(),
        P("mem"),
        P("lat"),
        P("lon"),
        P(None, "lat", "lon"),
    )
    return jax.shard_map(iteration, mesh=mesh, in_specs=placed, out_specs=(field,) * 3, check_vma=False)
```

```python
import functools
import jax
import jax.numpy as jnp
from jax import lax
from jax.experimental import pallas as pl
from jax.experimental.pallas import tpu as pltpu
from jax.sharding import PartitionSpec as P


f32 = jnp.float32
bf16 = jnp.bfloat16
VM = pl.BlockSpec(memory_space=pltpu.VMEM)
SM = pl.BlockSpec(memory_space=pltpu.SMEM)


def choose(length, i):
    r = 1.0
    for k in range(i):
        r = r * (length + k) / (k + 1)
    return r


def rising(v, degree):
    r = jnp.ones_like(v)
    for k in range(degree):
        r = r * (v + (k + 1.0)) * (1.0 / (k + 1.0))
    return r


def halves(v):
    high = v.astype(bf16)
    return high, (v - high.astype(f32)).astype(bf16)


def left3(v, axis):
    high, low = halves(v)
    return jnp.concatenate([high, low, high], axis=axis)


def right3(v, axis):
    high, low = halves(v)
    return jnp.concatenate([high, high, low], axis=axis)


def product3(a, b):
    return jnp.dot(a, b, preferred_element_type=f32)


def iota(shape, dim):
    return lax.broadcasted_iota(jnp.int32, shape, dim).astype(f32)


def lon_consts(lonc):
    c = lonc
    q = jnp.exp(-c)
    leak = 1.0 - q
    return c, leak, 2.5 / jnp.sqrt(leak)


def lon_kernel_matrix(c_row, gain_row, cells, backward):
    a = iota((cells, cells), 0)
    b = iota((cells, cells), 1)
    lag = a - b if backward else b - a
    pos = jnp.maximum(lag, 0.0)
    shaped = rising(pos, 3) * jnp.exp(-pos * c_row) * gain_row
    return jnp.where(lag >= 0.0, shaped, 0.0)


def masked_rows(parts, y):
    rows = iota(parts[0].shape, 0)
    return jnp.concatenate([jnp.where(rows == float(y), p, 0.0) for p in parts], axis=0)


def lon_finals(c, leak, scale, cells, backward):
    x = iota(c.shape, 1)
    remain = x if backward else (cells - 1.0) - x
    decay = jnp.exp(-remain * c)
    return [leak ** (s + 1) * scale * rising(remain, s) * decay for s in range(4)]


def lon_entering(c, leak, cells, backward):
    x = iota(c.shape, 1)
    place = (cells - 1.0) - x if backward else x
    decay = jnp.exp(-(place + 1.0) * c)
    return [leak ** (3 - s) * rising(place, 3 - s) * decay for s in range(4)]


def lon_tables(lonc, rows, cells, backward, table_ref):
    c, leak, scale = lon_consts(lonc)
    gain = leak**4 * scale
    finals = lon_finals(c, leak, scale, cells, backward)
    spare = jnp.zeros((cells - 4 * rows, cells), f32)
    finals = jnp.concatenate(finals + [spare], axis=0).T
    column = lax.broadcasted_iota(jnp.int32, (cells, cells), 1)
    for y in range(rows):
        inside = lon_kernel_matrix(c[y : y + 1], gain[y : y + 1], cells, backward)
        leaving = jnp.where(lax.rem(column, rows) == y, finals, 0.0)
        table_ref[y] = right3(jnp.concatenate([inside, leaving], axis=1), 0)


def lon_local_rows(load_row, table_ref, rows, cells, inside_ref, carried_ref):
    carried = None
    for y in range(rows):
        both = product3(left3(load_row(y), 1), table_ref[y])
        inside_ref[y] = both[:, :cells]
        carried = both[:, cells:] if carried is None else carried + both[:, cells:]
    carried_ref[...] = carried.T[: 4 * rows]


def lon_incoming_states(lonc, blocks, rows, cells):
    k = blocks[0].shape[1]
    n = len(blocks)
    c = jnp.broadcast_to(lonc[:, :1], (rows, k))
    leak = 1.0 - jnp.exp(-c)

    def trans(r):
        closing = jnp.exp(-float(r * cells) * c)
        return [choose(r * cells, i) * leak**i * closing for i in range(4)]

    total = [jnp.zeros((rows, k), f32) for _ in range(4)]
    for r in range(n):
        part = [blocks[r][s * rows : (s + 1) * rows] for s in range(4)]
        if r:
            t = trans(r)
            part = [sum(t[i - j] * part[j] for j in range(i + 1)) for i in range(4)]
        total = [a + b for a, b in zip(total, part)]
    t = trans(n)
    solved = []
    for i in range(4):
        v = total[i]
        for j in range(i):
            v = v + t[i - j] * solved[j]
        solved.append(v / (1.0 - t[0]))
    return jnp.concatenate(solved, axis=0)


def lon_correction(states, entering, rows, cells):
    high = states.astype(bf16).astype(f32)
    low = states - high
    spare = jnp.zeros((cells - 12 * rows, states.shape[1]), f32)
    left = jnp.concatenate([high, low, high, spare], axis=0).T.astype(bf16)
    spare = jnp.zeros((cells - 12 * rows, cells), bf16)
    return lambda y: product3(left, jnp.concatenate([right3(masked_rows(entering, y), 0), spare], axis=0))


def lat_consts(dec):
    q = jnp.exp(-dec)
    leak = 1.0 - q
    return q, leak, leak * (2.5 / jnp.sqrt(leak))


def lat_sweep(load, store, start, dec, rows, k, backward, block):
    q1, l1, g1 = lat_consts(dec)
    x = dec.shape[1]
    q = jnp.broadcast_to(q1, (block, x))
    leak = jnp.broadcast_to(l1, (block, x))
    gain = jnp.broadcast_to(g1, (block, x))
    order = range(rows - 1, -1, -1) if backward else range(rows)

    def step(i, carry):
        at = pl.ds(pl.multiple_of(i * block, 8), block)
        u = start(at)
        for y in order:
            feed = gain * load(y, at, i * block)
            u0 = q * u[0] + feed
            u1 = q * u[1] + leak * u0
            u2 = q * u[2] + leak * u1
            u3 = q * u[3] + leak * u2
            u = [u0, u1, u2, u3]
            store(y, at, i * block, u3, u if y == order[-1] else None)
        return carry

    if k == block:
        step(0, 0)
    else:
        lax.fori_loop(0, k // block, step, 0)


def swap_halves(a, b):
    half = a.shape[-1] // 2
    low = iota((1,) * (a.ndim - 1) + (a.shape[-1],), a.ndim - 1) < float(half)
    turn = lambda v: pltpu.roll(v, half, v.ndim - 1)
    return jnp.where(low, a, turn(b)), jnp.where(low, turn(a), b)


def both_halves(v):
    return swap_halves(v, v)


def lat_trans(dec, rows):
    leak = 1.0 - jnp.exp(-dec)
    closing = jnp.exp(-float(rows) * dec)
    return [choose(rows, i) * leak**i * closing for i in range(4)]


def entering_states(got, chunks, block):
    hops = len(got) // chunks
    mine = [block[:1] == float(h + 1) for h in range(hops)]

    def at(chunk, where):
        out = []
        for s in range(4):
            v = None
            for m, p in zip(mine, got[chunk * hops : (chunk + 1) * hops]):
                new = p[s, where, :]
                v = jnp.where(m, new, jnp.zeros_like(new) if v is None else v)
            out.append(v)
        return out

    return at


def rows_at_once(size):
    return 40 if size % 40 == 0 else 8


def sweep_chunks(load, store, start, dec, rows, k, chunks, backward):
    size = k // chunks
    block = rows_at_once(size)
    for ch in range(chunks):
        lat_sweep(
            lambda y, at, base, ch=ch: load(y, ch * size + base),
            lambda y, at, base, value, last, ch=ch: store(y, ch, at, ch * size + base, value, last),
            lambda at, ch=ch: start(ch, at),
            dec,
            rows,
            size,
            backward,
            block,
        )


def k_tables(rows, cells, dec_ref, lonc_ref, latc_ref, table_ref, block_ref):
    block_ref[...] = jnp.full((8, cells), lax.axis_index("lat").astype(f32))
    row = jnp.broadcast_to(dec_ref[:, cells:], (rows, rows))
    own = iota((rows, rows), 0) == iota((rows, rows), 1)
    column = jnp.sum(jnp.where(own, row, 0.0), axis=1, keepdims=True)
    lonc = jnp.broadcast_to(column, (rows, cells))
    lonc_ref[...] = lonc
    first, second = both_halves(jnp.broadcast_to(dec_ref[:, :cells], (8, cells)))
    latc_ref[0] = first
    latc_ref[1] = second
    lon_tables(lonc, rows, cells, False, table_ref)


def k_lon_fwd(rows, k, cells, d_ref, table_ref, inside_ref, carried_ref):
    d_ref = d_ref.reshape(k * rows, cells)
    lon_local_rows(
        lambda y: d_ref[pl.ds(y, k, stride=rows), :], table_ref, rows, cells, inside_ref, carried_ref
    )


def spread_modes(v, pairs, transposed):
    source = v.T if transposed else v
    r, c = source.shape
    rows, columns = pairs * r, 3 * pairs * c
    exact = functools.partial(jnp.dot, precision=lax.Precision.HIGHEST, preferred_element_type=f32)
    block = lambda at, size: jnp.floor((at + 0.5) * (1.0 / size))
    at_row, at_column = iota((rows, r), 0), iota((c, columns), 1)
    pick_row = (at_row - block(at_row, r) * r == iota((rows, r), 1)).astype(f32)
    pick_column = (at_column - block(at_column, c) * c == iota((c, columns), 0)).astype(f32)
    everywhere = exact(exact(pick_row, source), pick_column)
    column = iota((1, columns), 1)
    part = block(column, pairs * c)
    own = block(iota((rows, 1), 0), r) == block(column - part * (pairs * c), c)
    full = jnp.where(own, everywhere, 0.0)
    high, low = halves(full)
    return jnp.where(part == 1.0, low.astype(f32), high.astype(f32)).astype(bf16)


def k_out_modes(pairs, v_ref, eig_ref, mask_ref, modes_ref):
    modes = v_ref.shape[0]
    cells = mask_ref.shape[1]
    modes_ref[...] = spread_modes(v_ref[...], pairs, True)
    e = lax.broadcasted_iota(jnp.int32, (modes, cells), 0)
    low = lax.broadcasted_iota(jnp.int32, (modes, cells), 1) < cells // 2
    for m in range(pairs):
        used = jnp.where(low, eig_ref[m], eig_ref[m + pairs])
        mask_ref[m * modes : (m + 1) * modes] = jnp.where(e < used, 1.0, 0.0)


def k_in_modes(pairs, v_ref, modes_ref):
    modes_ref[...] = spread_modes(v_ref[...], pairs, False)


def row_spacing(size):
    return size + 8 if size // 8 % 2 == 0 else size


def k_back_tables(lon_ref, table_ref):
    lon_tables(lon_ref[...], *lon_ref.shape, True, table_ref)


def k_prepare(m_ref, a_ref, b_ref):
    members, levels, rows, _ = m_ref.shape
    pairs = members // 2
    apart = row_spacing(pairs * levels)

    def step(i, carry):
        for l in range(levels):
            a, b = swap_halves(m_ref[i, l].astype(f32), m_ref[i + pairs, l].astype(f32))
            at = pl.ds(i * levels + l, rows, stride=apart)
            a_ref[at, :] = a
            b_ref[at, :] = b
        return carry

    lax.fori_loop(0, pairs, step, 0)


def k_lat_first(rows, k, cells, n, chunks, *refs):
    inside_ref, lon_ref, lat_ref, *rest = refs
    blocks = [r[...] for r in rest[:n]]
    f_refs, out_refs = rest[n : n + 2], rest[n + 2 :]
    lonc = lon_ref[...]
    states = lon_incoming_states(lonc, blocks, rows, cells)
    c, leak, _ = lon_consts(lonc)
    added = lon_correction(states, lon_entering(c, leak, cells, False), rows, cells)
    half = k // 2
    for y in range(rows):
        row = inside_ref[y] + added(y)
        f_refs[0][y], f_refs[1][y] = swap_halves(row[:half], row[half:])
    for part, f_ref in enumerate(f_refs):

        def store(y, ch, at, base, value, last, part=part):
            if last is not None:
                for s in range(4):
                    out_refs[part * chunks + ch][s, at, :] = last[s]

        sweep_chunks(
            lambda y, base: f_ref[y, pl.ds(pl.multiple_of(base, 8), rows_at_once(half // chunks)), :],
            store,
            lambda ch, at: [jnp.zeros((1, cells), f32)] * 4,
            lat_ref[part, :1],
            rows,
            half,
            chunks,
            False,
        )


def k_pass_on(rows, part, carried_ref, got_ref, lat_ref, out_ref):
    t = lat_trans(lat_ref[part, :1], rows)
    got = [got_ref[s] for s in range(4)]
    for i in range(4):
        v = carried_ref[i]
        for j in range(i + 1):
            v = v + t[i - j] * got[j]
        out_ref[i] = v


def k_increment(rows, k, part, chunks, count, pairs, levels, *refs):
    f_ref, lat_ref, block_ref, m_ref, mask_ref, modes_ref, *rest = refs
    out_ref, s_ref = rest[count:]
    cells = lat_ref.shape[-1]

    def store(y, ch, at, base, value, last):
        where = pl.ds(pl.multiple_of(base, 8), rows_at_once(k // chunks))
        s_ref[y, where, :] = value * mask_ref[where, :]

    sweep_chunks(
        lambda y, base: f_ref[y, pl.ds(pl.multiple_of(base, 8), rows_at_once(k // chunks)), :],
        store,
        entering_states(rest[:count], chunks, block_ref[...]),
        lat_ref[part, :1],
        rows,
        k,
        chunks,
        False,
    )
    half = levels // 2
    low = iota((1, cells), 1) < float(cells // 2)
    apart = row_spacing(pairs * levels)
    for y in range(rows):
        profile = product3(modes_ref[...], right3(s_ref[y], 0))
        inc = None
        for m in range(pairs):
            at = y * apart + m * levels
            p = m_ref[at : at + levels, :] * profile[m * levels : (m + 1) * levels]
            inc = p if inc is None else inc + p
        inc = inc + pltpu.roll(inc, cells // 2, 1)
        out_ref[y] = jnp.where(low, inc[:half], inc[half:])


def k_gradient(rows, k, part, chunks, pairs, levels, *refs):
    inc_ref, got_ref, obs_ref, m_ref, mask_ref, modes_ref, lat_ref, g_ref, *carried_refs = refs
    cells = lat_ref.shape[-1]
    obs_ref = obs_ref.reshape(levels * rows, cells)
    size = pairs * levels
    apart = row_spacing(size)
    for y in range(rows):
        inc = jnp.concatenate(both_halves(inc_ref[y] + got_ref[y]), axis=0)
        w = inc * both_halves(obs_ref[pl.ds(y, levels, stride=rows), :])[part]
        m = m_ref[y * apart : y * apart + size, :]
        weighted = (m.reshape(pairs, levels, cells) * w[None]).reshape(size, cells)
        g_ref[y] = product3(modes_ref[...], right3(weighted, 0)) * mask_ref[...]

    def store(y, ch, at, base, value, last):
        if last is not None:
            for s in range(4):
                carried_refs[ch][s, at, :] = last[s]

    sweep_chunks(
        lambda y, base: g_ref[y, pl.ds(pl.multiple_of(base, 8), rows_at_once(k // chunks)), :],
        store,
        lambda ch, at: [jnp.zeros((1, cells), f32)] * 4,
        lat_ref[part, :1],
        rows,
        k,
        chunks,
        True,
    )


def k_lon_bwd(rows, k, cells, chunks, count, blocks, *refs):
    g_refs, lat_ref, block_ref, table_ref, rest = refs[:2], refs[2], refs[3], refs[4], refs[5:]
    block = (blocks - 1.0) - block_ref[...]
    inside_ref, carried_ref, p_ref = rest[2 * count :]
    half = k // 2
    for part in range(2):
        g_ref = g_refs[part]

        def store(y, ch, at, base, value, last, part=part):
            p_ref[part, y, pl.ds(pl.multiple_of(base, 8), rows_at_once(half // chunks)), :] = value

        sweep_chunks(
            lambda y, base: g_ref[y, pl.ds(pl.multiple_of(base, 8), rows_at_once(half // chunks)), :],
            store,
            entering_states(rest[part * count : (part + 1) * count], chunks, block),
            lat_ref[part, :1],
            rows,
            half,
            chunks,
            True,
        )

    def load_row(y):
        return jnp.concatenate(swap_halves(p_ref[0, y], p_ref[1, y]), axis=0)

    lon_local_rows(load_row, table_ref, rows, cells, inside_ref, carried_ref)


def k_sums(rows, k, cells, n, *refs):
    inside_ref, lon_ref, d_ref, r_ref, *rest = refs
    d_ref = d_ref.reshape(k * rows, cells)
    r_ref = r_ref.reshape(k * rows, cells)
    blocks = [r[...] for r in rest[:n]]
    h_ref, sums_ref = rest[n:]
    lonc = lon_ref[...]
    states = lon_incoming_states(lonc, blocks, rows, cells)
    c, leak, _ = lon_consts(lonc)
    added = lon_correction(states, lon_entering(c, leak, cells, True), rows, cells)
    for y in range(rows):
        at = pl.ds(y, k, stride=rows)
        h_ref[at, :] = inside_ref[y] + added(y)
    block = 64
    zero = jnp.zeros((8, cells), f32)

    def step(i, acc):
        at = pl.ds(pl.multiple_of(i * block, 8), block)
        d = d_ref[at, :]
        r = r_ref[at, :]
        h = h_ref[at, :] + d
        h_ref[at, :] = h
        fold = lambda v: v.reshape(block // 8, 8, cells).sum(axis=0)
        return (acc[0] + fold(r * r), acc[1] + fold(d * h), acc[2] + fold(r * h), acc[3] + fold(h * h))

    acc = lax.fori_loop(0, (k * rows) // block, step, (zero,) * 4)
    out = [a.sum(axis=0, keepdims=True) for a in acc]
    sums_ref[...] = jnp.concatenate(out + [jnp.zeros((4, cells), f32)], axis=0)


def k_update(pieces, sums_ref, control_ref, r_ref, d_ref, h_ref, *rest):
    outs, news, sems = rest[:3], rest[3:6], rest[6]
    sums = jnp.sum(sums_ref[...], axis=1, keepdims=True)
    rr, dh, rh, hh = (sums[i : i + 1].reshape(1, 1, 1) for i in range(4))
    step = rr / dh
    norm_new = rr - 2.0 * step * rh + step * step * hh
    beta = norm_new / rr
    size = d_ref.shape[0] // pieces
    copies = []
    for i in range(pieces):
        at = pl.ds(i * size, size)
        d = d_ref[at]
        nr = r_ref[at] - step * h_ref[at]
        for j, v in enumerate((control_ref[at] + step * d, nr, nr + beta * d)):
            news[j][at] = v
            copy = pltpu.make_async_copy(news[j].at[at], outs[j].at[at], sems.at[j, i])
            copy.start()
            copies.append(copy)
    for copy in copies:
        copy.wait()


def call(body, outs, ins, specs=None, out_specs=None, scratch=(), cost=None):
    return pl.pallas_call(
        body,
        out_shape=outs,
        in_specs=specs or [VM] * len(ins),
        out_specs=out_specs or jax.tree.map(lambda _: VM, outs),
        scratch_shapes=scratch,
        cost_estimate=None if cost is None else pl.CostEstimate(flops=cost, bytes_accessed=1000, transcendentals=0),
        compiler_params=pltpu.CompilerParams(vmem_limit_bytes=16 * 1024 * 1024),
    )(*ins)


def sds(*shape):
    return jax.ShapeDtypeStruct(shape, f32)


def lon_exchange(carried, backward):
    n = lax.axis_size("lon")
    sign = -1 if backward else 1
    got = [
        lax.ppermute(carried, "lon", [(j, (j + sign * r) % n) for j in range(n)]) for r in range(1, n)
    ]
    return got + [carried]


def pass_on(part, got, latc, rows, c):
    return call(functools.partial(k_pass_on, rows, c), sds(*part.shape), [part, got, latc])


def hop_pairs(a, b):
    n, n_mem = lax.axis_size("lat"), lax.axis_size("mem")
    if n_mem % 2:
        return [(a * n_mem + i, b * n_mem + i) for i in range(n_mem)]
    to = lambda z, i: (b, i) if z == a else (a, i) if z == b else (z, i ^ 1)
    flat = lambda z, i: z * n_mem + i
    return [(flat(z, i), flat(*to(z, i))) for z in range(n) for i in range(n_mem)]


def lat_carry(halves, latc, rows, backward):
    n = lax.axis_size("lat")
    at = (lambda i: n - 1 - i) if backward else (lambda i: i)
    got = [[[] for _ in chunks] for chunks in halves]
    for h in range(n - 1):
        pairs = hop_pairs(at(h), at(h + 1))
        for c, chunks in enumerate(halves):
            for i, part in enumerate(chunks):
                v = pass_on(part, got[c][i][-1], latc, rows, c) if h else part
                got[c][i].append(lax.ppermute(v, ("lat", "mem"), pairs))
    return [[g for chunk in half for g in chunk] for half in got]


def all_sum(v, axes, steps):
    total = 1
    for a in axes:
        total *= lax.axis_size(a)
    masks = [0]
    for s in steps:
        masks = masks + [m ^ s for m in masks]
    got = [lax.ppermute(v, axes, [(i, i ^ m) for i in range(total)]) for m in masks[1:]]
    for g in got:
        v = v + g
    return v


def powers(n):
    out, d = [], 1
    while d < n:
        out.append(d)
        d *= 2
    return out


def reduce_everywhere(v):
    n_lon, n_lat, n_mem = (lax.axis_size(a) for a in ("lon", "lat", "mem"))
    for s in powers(n_mem):
        v = all_sum(v, ("mem",), [s])
    for s in powers(n_lon):
        v = all_sum(v, ("lon",), [s])
    lat = powers(n_lat)
    for i in range(0, len(lat), 2):
        v = all_sum(v, ("lat",), lat[i : i + 2])
    return v


def iteration(control, residual, direction, members, vert_modes, eig_count, lon_decay, lat_decay, obs_weight):
    k, rows, cells = direction.shape
    mcount, levels = members.shape[:2]
    n_lon, n_mem = lax.axis_size("lon"), lax.axis_size("mem")
    half = k // 2
    pairs = mcount // 2
    chunks, back_chunks = 2, 2
    states = lambda chunks: (sds(4, half // chunks, cells),) * chunks

    decays = jnp.concatenate([lat_decay, lon_decay]).reshape(1, cells + rows)
    lonc, latc, tables, block = call(
        functools.partial(k_tables, rows, cells),
        (sds(rows, cells), sds(2, 8, cells), jax.ShapeDtypeStruct((rows, 3 * cells, 2 * cells), bf16), sds(8, cells)),
        [decays],
        cost=10**9,
    )
    inside, carried = call(
        functools.partial(k_lon_fwd, rows, k, cells), (sds(rows, k, cells), sds(4 * rows, k)), [direction, tables]
    )
    packed = call(k_prepare, (sds(rows * row_spacing(pairs * levels), cells),) * 2, [members], cost=10**9)
    back_tables = call(k_back_tables, jax.ShapeDtypeStruct((rows, 3 * cells, 2 * cells), bf16), [lonc], cost=10**9)
    mask, out_modes = call(
        functools.partial(k_out_modes, pairs),
        (sds(half, cells), jax.ShapeDtypeStruct((pairs * levels, 3 * half), bf16)),
        [vert_modes, eig_count],
        specs=[VM, SM],
        cost=10**9,
    )
    in_modes = call(
        functools.partial(k_in_modes, pairs),
        jax.ShapeDtypeStruct((half, 3 * pairs * levels), bf16),
        [vert_modes],
        cost=10**9,
    )
    blocks = lon_exchange(carried, False)
    fa, fb, *parts = call(
        functools.partial(k_lat_first, rows, k, cells, n_lon, chunks),
        (sds(rows, half, cells),) * 2 + states(chunks) * 2,
        [inside, lonc, latc, *blocks],
    )
    got = lat_carry([parts[:chunks], parts[chunks:]], latc, rows, False)
    count = len(got[0])
    fields = (fa, fb)
    inc = [None, None]
    for part in range(2):
        inc[part] = call(
            functools.partial(k_increment, rows, half, part, chunks, count, pairs, levels),
            sds(rows, levels // 2, cells),
            [fields[part], latc, block, packed[part], mask, out_modes, *got[part]],
            scratch=[pltpu.VMEM((rows, half, cells), f32)],
        )
    grads, sends = [None, None], [None, None]
    for part in range(2):
        v = inc[part]
        step = 1
        while step * 2 < n_mem:
            v = v + lax.ppermute(v, "mem", [(i, i ^ step) for i in range(n_mem)])
            step *= 2
        other = lax.ppermute(v, "mem", [(i, i ^ step) for i in range(n_mem)])
        grads[part], *sends[part] = call(
            functools.partial(k_gradient, rows, half, part, back_chunks, pairs, levels),
            (sds(rows, half, cells),) + states(back_chunks),
            [v, other, obs_weight, packed[part], mask, in_modes, latc],
        )
    got = lat_carry(sends, latc, rows, True)
    count = len(got[0])
    inside, carried = call(
        functools.partial(k_lon_bwd, rows, k, cells, back_chunks, count, lax.axis_size("lat")),
        (sds(rows, k, cells), sds(4 * rows, k)),
        [*grads, latc, block, back_tables, *got[0], *got[1]],
        scratch=[pltpu.VMEM((2, rows, half, cells), f32)],
    )
    blocks = lon_exchange(carried, True)
    h, sums = call(
        functools.partial(k_sums, rows, k, cells, n_lon),
        (sds(k * rows, cells), sds(8, cells)),
        [inside, lonc, direction, residual, *blocks],
    )
    sums = reduce_everywhere(sums)
    pieces = 4 if k % 4 == 0 else 1
    outs = call(
        functools.partial(k_update, pieces),
        (sds(k, rows, cells),) * 3,
        [sums, control, residual, direction, h.reshape(k, rows, cells)],
        out_specs=(pl.BlockSpec(memory_space=pl.ANY),) * 3,
        scratch=[pltpu.VMEM((k, rows, cells), f32)] * 3 + [pltpu.SemaphoreType.DMA((3, pieces))],
    )
    return tuple(outs)


def solution(mesh):
    field = P("mem", "lat", "lon")
    placed = (
        field,
        field,
        field,
        P("mem", None, "lat", "lon"),
        P(),
        P("mem"),
        P("lat"),
        P("lon"),
        P(None, "lat", "lon"),
    )
    return jax.shard_map(iteration, mesh=mesh, in_specs=placed, out_specs=(field,) * 3, check_vma=False)
```

```python
import functools
import jax
import jax.numpy as jnp
from jax import lax
from jax.experimental import pallas as pl
from jax.experimental.pallas import tpu as pltpu
from jax.sharding import PartitionSpec as P


f32 = jnp.float32
bf16 = jnp.bfloat16
VM = pl.BlockSpec(memory_space=pltpu.VMEM)
SM = pl.BlockSpec(memory_space=pltpu.SMEM)


def choose(length, i):
    r = 1.0
    for k in range(i):
        r = r * (length + k) / (k + 1)
    return r


def rising(v, degree):
    r = jnp.ones_like(v)
    for k in range(degree):
        r = r * (v + (k + 1.0)) * (1.0 / (k + 1.0))
    return r


def halves(v):
    high = v.astype(bf16)
    return high, (v - high.astype(f32)).astype(bf16)


def left3(v, axis):
    high, low = halves(v)
    return jnp.concatenate([high, low, high], axis=axis)


def right3(v, axis):
    high, low = halves(v)
    return jnp.concatenate([high, high, low], axis=axis)


def product3(a, b):
    return jnp.dot(a, b, preferred_element_type=f32)


def iota(shape, dim):
    return lax.broadcasted_iota(jnp.int32, shape, dim).astype(f32)


def lon_consts(lonc):
    c = lonc
    q = jnp.exp(-c)
    leak = 1.0 - q
    return c, leak, 2.5 / jnp.sqrt(leak)


def lon_kernel_matrix(c_row, gain_row, cells, backward):
    a = iota((cells, cells), 0)
    b = iota((cells, cells), 1)
    lag = a - b if backward else b - a
    pos = jnp.maximum(lag, 0.0)
    shaped = rising(pos, 3) * jnp.exp(-pos * c_row) * gain_row
    return jnp.where(lag >= 0.0, shaped, 0.0)


def masked_rows(parts, y):
    rows = iota(parts[0].shape, 0)
    return jnp.concatenate([jnp.where(rows == float(y), p, 0.0) for p in parts], axis=0)


def lon_finals(c, leak, scale, cells, backward):
    x = iota(c.shape, 1)
    remain = x if backward else (cells - 1.0) - x
    decay = jnp.exp(-remain * c)
    return [leak ** (s + 1) * scale * rising(remain, s) * decay for s in range(4)]


def lon_entering(c, leak, cells, backward):
    x = iota(c.shape, 1)
    place = (cells - 1.0) - x if backward else x
    decay = jnp.exp(-(place + 1.0) * c)
    return [leak ** (3 - s) * rising(place, 3 - s) * decay for s in range(4)]


def entering_columns(lonc, rows, cells, backward, first):
    c, leak, _ = lon_consts(lonc)
    before = [jnp.zeros((first, cells), f32)] if first else []
    after = cells - first - 4 * rows
    after = [jnp.zeros((after, cells), f32)] if after else []
    return jnp.concatenate(before + lon_entering(c, leak, cells, backward) + after, axis=0).T


def lon_tables(lonc, rows, cells, backward, table_ref):
    c, leak, scale = lon_consts(lonc)
    gain = leak**4 * scale
    finals = lon_finals(c, leak, scale, cells, backward)
    spare = jnp.zeros((cells - 4 * rows, cells), f32)
    finals = jnp.concatenate(finals + [spare], axis=0).T
    column = lax.broadcasted_iota(jnp.int32, (cells, cells), 1)
    if backward:
        products = entering_columns(lonc, rows, cells, backward, cells - 4 * rows)
    for y in range(rows):
        inside = lon_kernel_matrix(c[y : y + 1], gain[y : y + 1], cells, backward)
        leaving = jnp.where(lax.rem(column, rows) == y, finals, 0.0)
        if backward:
            mine = jnp.where(lax.rem(column, rows) == y, products, 0.0)
            leaving = leaving + jnp.dot(
                inside, mine, precision=lax.Precision.HIGHEST, preferred_element_type=f32
            )
        table_ref[y] = right3(jnp.concatenate([inside, leaving], axis=1), 0)


def lon_local_rows(load_row, table_ref, rows, cells, inside_ref, also=None):
    total = None
    for y in range(rows):
        both = product3(left3(load_row(y), 1), table_ref[y])
        inside_ref[y] = both[:, :cells]
        if also is not None:
            also(y, both[:, :cells])
        total = both[:, cells:] if total is None else total + both[:, cells:]
    return total


def lon_incoming_states(lonc, blocks, rows, cells):
    k = blocks[0].shape[1]
    n = len(blocks)
    c = jnp.broadcast_to(lonc[:, :1], (rows, k))
    leak = 1.0 - jnp.exp(-c)

    def trans(r):
        closing = jnp.exp(-float(r * cells) * c)
        return [choose(r * cells, i) * leak**i * closing for i in range(4)]

    total = [jnp.zeros((rows, k), f32) for _ in range(4)]
    for r in range(n):
        part = [blocks[r][s * rows : (s + 1) * rows] for s in range(4)]
        if r:
            t = trans(r)
            part = [sum(t[i - j] * part[j] for j in range(i + 1)) for i in range(4)]
        total = [a + b for a, b in zip(total, part)]
    t = trans(n)
    solved = []
    for i in range(4):
        v = total[i]
        for j in range(i):
            v = v + t[i - j] * solved[j]
        solved.append(v / (1.0 - t[0]))
    return jnp.concatenate(solved, axis=0)


def lon_correction(states, entering, rows, cells):
    high = states.astype(bf16).astype(f32)
    low = states - high
    spare = jnp.zeros((cells - 12 * rows, states.shape[1]), f32)
    left = jnp.concatenate([high, low, high, spare], axis=0).T.astype(bf16)
    spare = jnp.zeros((cells - 12 * rows, cells), bf16)
    return lambda y: product3(left, jnp.concatenate([right3(masked_rows(entering, y), 0), spare], axis=0))


def lat_consts(dec):
    q = jnp.exp(-dec)
    leak = 1.0 - q
    return q, leak, leak * (2.5 / jnp.sqrt(leak))


def lat_sweep(load, store, start, dec, rows, k, backward, block):
    q1, l1, g1 = lat_consts(dec)
    x = dec.shape[1]
    q = jnp.broadcast_to(q1, (block, x))
    leak = jnp.broadcast_to(l1, (block, x))
    gain = jnp.broadcast_to(g1, (block, x))
    order = range(rows - 1, -1, -1) if backward else range(rows)

    def step(i, carry):
        at = pl.ds(pl.multiple_of(i * block, 8), block)
        u = start(at)
        for y in order:
            feed = gain * load(y, at, i * block)
            u0 = q * u[0] + feed
            u1 = q * u[1] + leak * u0
            u2 = q * u[2] + leak * u1
            u3 = q * u[3] + leak * u2
            u = [u0, u1, u2, u3]
            store(y, at, i * block, u3, u if y == order[-1] else None)
        return carry

    if k == block:
        step(0, 0)
    else:
        lax.fori_loop(0, k // block, step, 0)


def swap_halves(a, b):
    half = a.shape[-1] // 2
    low = iota((1,) * (a.ndim - 1) + (a.shape[-1],), a.ndim - 1) < float(half)
    turn = lambda v: pltpu.roll(v, half, v.ndim - 1)
    return jnp.where(low, a, turn(b)), jnp.where(low, turn(a), b)


def both_halves(v):
    return swap_halves(v, v)


def lat_trans(dec, rows):
    leak = 1.0 - jnp.exp(-dec)
    closing = jnp.exp(-float(rows) * dec)
    return [choose(rows, i) * leak**i * closing for i in range(4)]


def entering_states(got, chunks, block):
    hops = len(got) // chunks
    mine = [block[:1] == float(h + 1) for h in range(hops)]

    def at(chunk, where):
        out = []
        for s in range(4):
            v = None
            for m, p in zip(mine, got[chunk * hops : (chunk + 1) * hops]):
                new = p[s, where, :]
                v = jnp.where(m, new, jnp.zeros_like(new) if v is None else v)
            out.append(v)
        return out

    return at


def rows_at_once(size):
    return 40 if size % 40 == 0 else 8


def sweep_chunks(load, store, start, dec, rows, k, chunks, backward):
    size = k // chunks
    block = rows_at_once(size)
    for ch in range(chunks):
        lat_sweep(
            lambda y, at, base, ch=ch: load(y, ch * size + base),
            lambda y, at, base, value, last, ch=ch: store(y, ch, at, ch * size + base, value, last),
            lambda at, ch=ch: start(ch, at),
            dec,
            rows,
            size,
            backward,
            block,
        )


def k_tables(rows, cells, dec_ref, lonc_ref, latc_ref, table_ref, block_ref):
    block_ref[...] = jnp.full((8, cells), lax.axis_index("lat").astype(f32))
    row = jnp.broadcast_to(dec_ref[:, cells:], (rows, rows))
    own = iota((rows, rows), 0) == iota((rows, rows), 1)
    column = jnp.sum(jnp.where(own, row, 0.0), axis=1, keepdims=True)
    lonc = jnp.broadcast_to(column, (rows, cells))
    lonc_ref[...] = lonc
    first, second = both_halves(jnp.broadcast_to(dec_ref[:, :cells], (8, cells)))
    latc_ref[0] = first
    latc_ref[1] = second
    lon_tables(lonc, rows, cells, False, table_ref)


def k_lon_fwd(rows, k, cells, d_ref, table_ref, inside_ref, carried_ref):
    d_ref = d_ref.reshape(k * rows, cells)
    total = lon_local_rows(lambda y: d_ref[pl.ds(y, k, stride=rows), :], table_ref, rows, cells, inside_ref)
    carried_ref[...] = total.T[: 4 * rows]


def spread_modes(v, pairs, transposed):
    source = v.T if transposed else v
    r, c = source.shape
    rows, columns = pairs * r, 3 * pairs * c
    exact = functools.partial(jnp.dot, precision=lax.Precision.HIGHEST, preferred_element_type=f32)
    block = lambda at, size: jnp.floor((at + 0.5) * (1.0 / size))
    at_row, at_column = iota((rows, r), 0), iota((c, columns), 1)
    pick_row = (at_row - block(at_row, r) * r == iota((rows, r), 1)).astype(f32)
    pick_column = (at_column - block(at_column, c) * c == iota((c, columns), 0)).astype(f32)
    everywhere = exact(exact(pick_row, source), pick_column)
    column = iota((1, columns), 1)
    part = block(column, pairs * c)
    own = block(iota((rows, 1), 0), r) == block(column - part * (pairs * c), c)
    full = jnp.where(own, everywhere, 0.0)
    high, low = halves(full)
    return jnp.where(part == 1.0, low.astype(f32), high.astype(f32)).astype(bf16)


def k_out_modes(pairs, v_ref, eig_ref, mask_ref, modes_ref):
    modes = v_ref.shape[0]
    cells = mask_ref.shape[1]
    modes_ref[...] = spread_modes(v_ref[...], pairs, True)
    e = lax.broadcasted_iota(jnp.int32, (modes, cells), 0)
    low = lax.broadcasted_iota(jnp.int32, (modes, cells), 1) < cells // 2
    for m in range(pairs):
        used = jnp.where(low, eig_ref[m], eig_ref[m + pairs])
        mask_ref[m * modes : (m + 1) * modes] = jnp.where(e < used, 1.0, 0.0)


def k_in_modes(pairs, v_ref, modes_ref):
    modes_ref[...] = spread_modes(v_ref[...], pairs, False)


def row_spacing(size):
    return size + 8 if size // 8 % 2 == 0 else size


def k_back_tables(lon_ref, table_ref):
    lon_tables(lon_ref[...], *lon_ref.shape, True, table_ref)


def k_prepare(m_ref, a_ref, b_ref):
    members, levels, rows, _ = m_ref.shape
    pairs = members // 2
    apart = row_spacing(pairs * levels)

    def step(i, carry):
        for l in range(levels):
            a, b = swap_halves(m_ref[i, l].astype(f32), m_ref[i + pairs, l].astype(f32))
            at = pl.ds(i * levels + l, rows, stride=apart)
            a_ref[at, :] = a
            b_ref[at, :] = b
        return carry

    lax.fori_loop(0, pairs, step, 0)


def k_lat_first(rows, k, cells, n, chunks, *refs):
    inside_ref, lon_ref, lat_ref, *rest = refs
    blocks = [r[...] for r in rest[:n]]
    f_refs, out_refs = rest[n : n + 2], rest[n + 2 :]
    lonc = lon_ref[...]
    states = lon_incoming_states(lonc, blocks, rows, cells)
    c, leak, _ = lon_consts(lonc)
    added = lon_correction(states, lon_entering(c, leak, cells, False), rows, cells)
    half = k // 2
    for y in range(rows):
        row = inside_ref[y] + added(y)
        f_refs[0][y], f_refs[1][y] = swap_halves(row[:half], row[half:])
    for part, f_ref in enumerate(f_refs):

        def store(y, ch, at, base, value, last, part=part):
            if last is not None:
                for s in range(4):
                    out_refs[part * chunks + ch][s, at, :] = last[s]

        sweep_chunks(
            lambda y, base: f_ref[y, pl.ds(pl.multiple_of(base, 8), rows_at_once(half // chunks)), :],
            store,
            lambda ch, at: [jnp.zeros((1, cells), f32)] * 4,
            lat_ref[part, :1],
            rows,
            half,
            chunks,
            False,
        )


def k_pass_on(rows, part, carried_ref, got_ref, lat_ref, out_ref):
    t = lat_trans(lat_ref[part, :1], rows)
    got = [got_ref[s] for s in range(4)]
    for i in range(4):
        v = carried_ref[i]
        for j in range(i + 1):
            v = v + t[i - j] * got[j]
        out_ref[i] = v


def k_increment(rows, k, part, chunks, count, pairs, levels, *refs):
    f_ref, lat_ref, block_ref, m_ref, mask_ref, modes_ref, *rest = refs
    out_ref, s_ref = rest[count:]
    cells = lat_ref.shape[-1]

    def store(y, ch, at, base, value, last):
        where = pl.ds(pl.multiple_of(base, 8), rows_at_once(k // chunks))
        s_ref[y, where, :] = value * mask_ref[where, :]

    sweep_chunks(
        lambda y, base: f_ref[y, pl.ds(pl.multiple_of(base, 8), rows_at_once(k // chunks)), :],
        store,
        entering_states(rest[:count], chunks, block_ref[...]),
        lat_ref[part, :1],
        rows,
        k,
        chunks,
        False,
    )
    half = levels // 2
    low = iota((1, cells), 1) < float(cells // 2)
    apart = row_spacing(pairs * levels)
    for y in range(rows):
        profile = product3(modes_ref[...], right3(s_ref[y], 0))
        inc = None
        for m in range(pairs):
            at = y * apart + m * levels
            p = m_ref[at : at + levels, :] * profile[m * levels : (m + 1) * levels]
            inc = p if inc is None else inc + p
        inc = inc + pltpu.roll(inc, cells // 2, 1)
        out_ref[y] = jnp.where(low, inc[:half], inc[half:])


def k_gradient(rows, k, part, chunks, pairs, levels, *refs):
    inc_ref, got_ref, obs_ref, m_ref, mask_ref, modes_ref, lat_ref, g_ref, *carried_refs = refs
    cells = lat_ref.shape[-1]
    obs_ref = obs_ref.reshape(levels * rows, cells)
    size = pairs * levels
    apart = row_spacing(size)
    for y in range(rows):
        inc = jnp.concatenate(both_halves(inc_ref[y] + got_ref[y]), axis=0)
        w = inc * both_halves(obs_ref[pl.ds(y, levels, stride=rows), :])[part]
        m = m_ref[y * apart : y * apart + size, :]
        weighted = (m.reshape(pairs, levels, cells) * w[None]).reshape(size, cells)
        g_ref[y] = product3(modes_ref[...], right3(weighted, 0)) * mask_ref[...]

    def store(y, ch, at, base, value, last):
        if last is not None:
            for s in range(4):
                carried_refs[ch][s, at, :] = last[s]

    sweep_chunks(
        lambda y, base: g_ref[y, pl.ds(pl.multiple_of(base, 8), rows_at_once(k // chunks)), :],
        store,
        lambda ch, at: [jnp.zeros((1, cells), f32)] * 4,
        lat_ref[part, :1],
        rows,
        k,
        chunks,
        True,
    )


def k_lon_bwd(rows, k, cells, chunks, count, blocks, *refs):
    g_refs, lat_ref, block_ref, table_ref, rest = refs[:2], refs[2], refs[3], refs[4], refs[5:]
    block = (blocks - 1.0) - block_ref[...]
    d_ref, r_ref, known_ref, inside_ref, sent_ref, p_ref = rest[2 * count :]
    d_ref = d_ref.reshape(k * rows, cells)
    r_ref = r_ref.reshape(k * rows, cells)
    half = k // 2
    for part in range(2):
        g_ref = g_refs[part]

        def store(y, ch, at, base, value, last, part=part):
            p_ref[part, y, pl.ds(pl.multiple_of(base, 8), rows_at_once(half // chunks)), :] = value

        sweep_chunks(
            lambda y, base: g_ref[y, pl.ds(pl.multiple_of(base, 8), rows_at_once(half // chunks)), :],
            store,
            entering_states(rest[part * count : (part + 1) * count], chunks, block),
            lat_ref[part, :1],
            rows,
            half,
            chunks,
            True,
        )

    def load_row(y):
        return jnp.concatenate(swap_halves(p_ref[0, y], p_ref[1, y]), axis=0)

    acc = [jnp.zeros((8, cells), f32)] * 4

    def also(y, q):
        at = pl.ds(y, k, stride=rows)
        d, r = d_ref[at, :], r_ref[at, :]
        h = d + q
        fold = lambda v: v.reshape(k // 8, 8, cells).sum(axis=0)
        acc[:] = [a + fold(v) for a, v in zip(acc, (r * r, d * h, r * h, h * h))]

    total = lon_local_rows(load_row, table_ref, rows, cells, inside_ref, also)
    sent_ref[:k] = total + known_ref[...]
    out = [a.sum(axis=0, keepdims=True) for a in acc]
    sent_ref[k:] = jnp.concatenate(out + [jnp.zeros((4, cells), f32)], axis=0)


def k_known(rows, k, cells, d_ref, r_ref, lon_ref, out_ref):
    d_ref = d_ref.reshape(k * rows, cells)
    r_ref = r_ref.reshape(k * rows, cells)
    columns = entering_columns(lon_ref[...], rows, cells, True, 0)
    column = lax.broadcasted_iota(jnp.int32, (cells, cells), 1)
    total = [None, None]
    for y in range(rows):
        table = right3(jnp.where(lax.rem(column, rows) == y, columns, 0.0), 0)
        for i, ref in enumerate((d_ref, r_ref)):
            part = product3(left3(ref[pl.ds(y, k, stride=rows), :], 1), table)
            total[i] = part if total[i] is None else total[i] + part
    group = 4 * rows
    d, r = total
    out_ref[...] = pltpu.roll(d, group, 1) + pltpu.roll(r, 2 * group, 1) + pltpu.roll(d, cells - group, 1)


def k_sums(rows, k, cells, lon_ref, own_ref, other_ref, sums_ref, states_ref):
    lonc = lon_ref[...]
    group = 4 * rows
    own, other = own_ref[:k].T, other_ref[:k].T
    c, leak, _ = lon_consts(lonc)
    entering = lon_entering(c, leak, cells, True)
    sums = own_ref[k:] + other_ref[k:]
    extra = [jnp.zeros((rows, k), f32)] * 3
    for here, there in ((own, other), (other, own)):
        states = lon_incoming_states(lonc, [there[:group], here[:group]], rows, cells)
        if here is own:
            states_ref[...] = states
        v = [states[s * rows : (s + 1) * rows] for s in range(4)]
        for s in range(4):
            d, r, h = (here[g * group + s * rows : g * group + (s + 1) * rows] for g in (1, 2, 3))
            both = 2.0 * h
            for t in range(4):
                both = both + jnp.sum(entering[s] * entering[t], axis=1, keepdims=True) * v[t]
            extra = [extra[0] + v[s] * d, extra[1] + v[s] * r, extra[2] + v[s] * both]
    lane, row = iota(sums.shape, 1), iota(sums.shape, 0)
    for i, e in enumerate(extra):
        e = jnp.sum(jnp.sum(e, axis=1, keepdims=True), axis=0, keepdims=True)
        sums = sums + jnp.where((lane == 0.0) & (row == float(i + 1)), e, 0.0)
    sums_ref[...] = sums


def k_finish(rows, k, cells, inside_ref, lon_ref, d_ref, states_ref, h_ref):
    d_ref = d_ref.reshape(k * rows, cells)
    c, leak, _ = lon_consts(lon_ref[...])
    added = lon_correction(states_ref[...], lon_entering(c, leak, cells, True), rows, cells)
    for y in range(rows):
        at = pl.ds(y, k, stride=rows)
        h_ref[at, :] = inside_ref[y] + added(y) + d_ref[at, :]


def k_sums_any(rows, k, cells, n, *refs):
    inside_ref, lon_ref, d_ref, r_ref, *rest = refs
    d_ref = d_ref.reshape(k * rows, cells)
    r_ref = r_ref.reshape(k * rows, cells)
    blocks = [r[:k].T[: 4 * rows] for r in rest[:n]]
    h_ref, sums_ref = rest[n:]
    lonc = lon_ref[...]
    states = lon_incoming_states(lonc, blocks, rows, cells)
    c, leak, _ = lon_consts(lonc)
    added = lon_correction(states, lon_entering(c, leak, cells, True), rows, cells)
    acc = [jnp.zeros((8, cells), f32)] * 4
    fold = lambda v: v.reshape(k // 8, 8, cells).sum(axis=0)
    for y in range(rows):
        at = pl.ds(y, k, stride=rows)
        d, r = d_ref[at, :], r_ref[at, :]
        h = inside_ref[y] + added(y) + d
        h_ref[at, :] = h
        acc = [a + fold(v) for a, v in zip(acc, (r * r, d * h, r * h, h * h))]
    out = [a.sum(axis=0, keepdims=True) for a in acc]
    sums_ref[...] = jnp.concatenate(out + [jnp.zeros((4, cells), f32)], axis=0)


def k_update(pieces, sums_ref, control_ref, r_ref, d_ref, h_ref, *rest):
    outs, news, sems = rest[:3], rest[3:6], rest[6]
    sums = jnp.sum(sums_ref[...], axis=1, keepdims=True)
    rr, dh, rh, hh = (sums[i : i + 1].reshape(1, 1, 1) for i in range(4))
    step = rr / dh
    norm_new = rr - 2.0 * step * rh + step * step * hh
    beta = norm_new / rr
    size = d_ref.shape[0] // pieces
    copies = []
    for i in range(pieces):
        at = pl.ds(i * size, size)
        d = d_ref[at]
        nr = r_ref[at] - step * h_ref[at]
        for j, v in enumerate((control_ref[at] + step * d, nr, nr + beta * d)):
            news[j][at] = v
            copy = pltpu.make_async_copy(news[j].at[at], outs[j].at[at], sems.at[j, i])
            copy.start()
            copies.append(copy)
    for copy in copies:
        copy.wait()


def call(body, outs, ins, specs=None, out_specs=None, scratch=(), cost=None):
    return pl.pallas_call(
        body,
        out_shape=outs,
        in_specs=specs or [VM] * len(ins),
        out_specs=out_specs or jax.tree.map(lambda _: VM, outs),
        scratch_shapes=scratch,
        cost_estimate=None if cost is None else pl.CostEstimate(flops=cost, bytes_accessed=1000, transcendentals=0),
        compiler_params=pltpu.CompilerParams(vmem_limit_bytes=16 * 1024 * 1024),
    )(*ins)


def sds(*shape):
    return jax.ShapeDtypeStruct(shape, f32)


def lon_exchange(carried, backward):
    n = lax.axis_size("lon")
    sign = -1 if backward else 1
    got = [
        lax.ppermute(carried, "lon", [(j, (j + sign * r) % n) for j in range(n)]) for r in range(1, n)
    ]
    return got + [carried]


def pass_on(part, got, latc, rows, c):
    return call(functools.partial(k_pass_on, rows, c), sds(*part.shape), [part, got, latc])


def hop_pairs(a, b):
    n, n_mem = lax.axis_size("lat"), lax.axis_size("mem")
    if n_mem % 2:
        return [(a * n_mem + i, b * n_mem + i) for i in range(n_mem)]
    to = lambda z, i: (b, i) if z == a else (a, i) if z == b else (z, i ^ 1)
    flat = lambda z, i: z * n_mem + i
    return [(flat(z, i), flat(*to(z, i))) for z in range(n) for i in range(n_mem)]


def lat_carry(halves, latc, rows, backward):
    n = lax.axis_size("lat")
    at = (lambda i: n - 1 - i) if backward else (lambda i: i)
    got = [[[] for _ in chunks] for chunks in halves]
    for h in range(n - 1):
        pairs = hop_pairs(at(h), at(h + 1))
        for c, chunks in enumerate(halves):
            for i, part in enumerate(chunks):
                v = pass_on(part, got[c][i][-1], latc, rows, c) if h else part
                got[c][i].append(lax.ppermute(v, ("lat", "mem"), pairs))
    return [[g for chunk in half for g in chunk] for half in got]


def all_sum(v, axes, steps):
    total = 1
    for a in axes:
        total *= lax.axis_size(a)
    masks = [0]
    for s in steps:
        masks = masks + [m ^ s for m in masks]
    got = [lax.ppermute(v, axes, [(i, i ^ m) for i in range(total)]) for m in masks[1:]]
    for g in got:
        v = v + g
    return v


def powers(n):
    out, d = [], 1
    while d < n:
        out.append(d)
        d *= 2
    return out


def reduce_everywhere(v, over_lon):
    n_lon, n_lat, n_mem = (lax.axis_size(a) for a in ("lon", "lat", "mem"))
    for s in powers(n_mem):
        v = all_sum(v, ("mem",), [s])
    for s in powers(n_lon) if over_lon else ():
        v = all_sum(v, ("lon",), [s])
    lat = powers(n_lat)
    for i in range(0, len(lat), 2):
        v = all_sum(v, ("lat",), lat[i : i + 2])
    return v


def iteration(control, residual, direction, members, vert_modes, eig_count, lon_decay, lat_decay, obs_weight):
    k, rows, cells = direction.shape
    mcount, levels = members.shape[:2]
    n_lon, n_mem = lax.axis_size("lon"), lax.axis_size("mem")
    half = k // 2
    pairs = mcount // 2
    chunks, back_chunks = 2, 2
    states = lambda chunks: (sds(4, half // chunks, cells),) * chunks

    decays = jnp.concatenate([lat_decay, lon_decay]).reshape(1, cells + rows)
    lonc, latc, tables, block = call(
        functools.partial(k_tables, rows, cells),
        (sds(rows, cells), sds(2, 8, cells), jax.ShapeDtypeStruct((rows, 3 * cells, 2 * cells), bf16), sds(8, cells)),
        [decays],
        cost=10**9,
    )
    inside, carried = call(
        functools.partial(k_lon_fwd, rows, k, cells), (sds(rows, k, cells), sds(4 * rows, k)), [direction, tables]
    )
    packed = call(k_prepare, (sds(rows * row_spacing(pairs * levels), cells),) * 2, [members], cost=10**9)
    back_tables = call(k_back_tables, jax.ShapeDtypeStruct((rows, 3 * cells, 2 * cells), bf16), [lonc], cost=10**9)
    mask, out_modes = call(
        functools.partial(k_out_modes, pairs),
        (sds(half, cells), jax.ShapeDtypeStruct((pairs * levels, 3 * half), bf16)),
        [vert_modes, eig_count],
        specs=[VM, SM],
        cost=10**9,
    )
    in_modes = call(
        functools.partial(k_in_modes, pairs),
        jax.ShapeDtypeStruct((half, 3 * pairs * levels), bf16),
        [vert_modes],
        cost=10**9,
    )
    blocks = lon_exchange(carried, False)
    fa, fb, *parts = call(
        functools.partial(k_lat_first, rows, k, cells, n_lon, chunks),
        (sds(rows, half, cells),) * 2 + states(chunks) * 2,
        [inside, lonc, latc, *blocks],
    )
    got = lat_carry([parts[:chunks], parts[chunks:]], latc, rows, False)
    count = len(got[0])
    fields = (fa, fb)
    inc = [None, None]
    for part in range(2):
        inc[part] = call(
            functools.partial(k_increment, rows, half, part, chunks, count, pairs, levels),
            sds(rows, levels // 2, cells),
            [fields[part], latc, block, packed[part], mask, out_modes, *got[part]],
            scratch=[pltpu.VMEM((rows, half, cells), f32)],
        )
    grads, sends = [None, None], [None, None]
    for part in range(2):
        v = inc[part]
        step = 1
        while step * 2 < n_mem:
            v = v + lax.ppermute(v, "mem", [(i, i ^ step) for i in range(n_mem)])
            step *= 2
        other = lax.ppermute(v, "mem", [(i, i ^ step) for i in range(n_mem)])
        grads[part], *sends[part] = call(
            functools.partial(k_gradient, rows, half, part, back_chunks, pairs, levels),
            (sds(rows, half, cells),) + states(back_chunks),
            [v, other, obs_weight, packed[part], mask, in_modes, latc],
        )
    got = lat_carry(sends, latc, rows, True)
    count = len(got[0])
    known = call(functools.partial(k_known, rows, k, cells), sds(k, cells), [direction, residual, lonc], cost=10**9)
    inside, sent = call(
        functools.partial(k_lon_bwd, rows, k, cells, back_chunks, count, lax.axis_size("lat")),
        (sds(rows, k, cells), sds(k + 8, cells)),
        [*grads, latc, block, back_tables, *got[0], *got[1], direction, residual, known],
        scratch=[pltpu.VMEM((2, rows, half, cells), f32)],
    )
    blocks = lon_exchange(sent, True)
    if n_lon == 2:
        sums, states = call(
            functools.partial(k_sums, rows, k, cells), (sds(8, cells), sds(4 * rows, k)), [lonc, sent, blocks[0]]
        )
        sums = reduce_everywhere(sums, False)
        h = call(
            functools.partial(k_finish, rows, k, cells),
            sds(k * rows, cells),
            [inside, lonc, direction, states],
            cost=10**9,
        )
    else:
        h, sums = call(
            functools.partial(k_sums_any, rows, k, cells, n_lon),
            (sds(k * rows, cells), sds(8, cells)),
            [inside, lonc, direction, residual, *blocks],
        )
        sums = reduce_everywhere(sums, True)
    pieces = 4 if k % 4 == 0 else 1
    outs = call(
        functools.partial(k_update, pieces),
        (sds(k, rows, cells),) * 3,
        [sums, control, residual, direction, h.reshape(k, rows, cells)],
        out_specs=(pl.BlockSpec(memory_space=pl.ANY),) * 3,
        scratch=[pltpu.VMEM((k, rows, cells), f32)] * 3 + [pltpu.SemaphoreType.DMA((3, pieces))],
    )
    return tuple(outs)


def solution(mesh):
    field = P("mem", "lat", "lon")
    placed = (
        field,
        field,
        field,
        P("mem", None, "lat", "lon"),
        P(),
        P("mem"),
        P("lat"),
        P("lon"),
        P(None, "lat", "lon"),
    )
    return jax.shard_map(iteration, mesh=mesh, in_specs=placed, out_specs=(field,) * 3, check_vma=False)
```

```python
import functools
import jax
import jax.numpy as jnp
from jax import lax
from jax.experimental import pallas as pl
from jax.experimental.pallas import tpu as pltpu
from jax.sharding import PartitionSpec as P


f32 = jnp.float32
bf16 = jnp.bfloat16
VM = pl.BlockSpec(memory_space=pltpu.VMEM)
SM = pl.BlockSpec(memory_space=pltpu.SMEM)


def choose(length, i):
    r = 1.0
    for k in range(i):
        r = r * (length + k) / (k + 1)
    return r


def rising(v, degree):
    r = jnp.ones_like(v)
    for k in range(degree):
        r = r * (v + (k + 1.0)) * (1.0 / (k + 1.0))
    return r


def halves(v):
    high = v.astype(bf16)
    return high, (v - high.astype(f32)).astype(bf16)


def left3(v, axis):
    high, low = halves(v)
    return jnp.concatenate([high, low, high], axis=axis)


def right3(v, axis):
    high, low = halves(v)
    return jnp.concatenate([high, high, low], axis=axis)


def product3(a, b):
    return jnp.dot(a, b, preferred_element_type=f32)


def iota(shape, dim):
    return lax.broadcasted_iota(jnp.int32, shape, dim).astype(f32)


def lon_consts(lonc):
    c = lonc
    q = jnp.exp(-c)
    leak = 1.0 - q
    return c, leak, 2.5 / jnp.sqrt(leak)


def lon_kernel_matrix(c_row, gain_row, cells, backward):
    a = iota((cells, cells), 0)
    b = iota((cells, cells), 1)
    lag = a - b if backward else b - a
    pos = jnp.maximum(lag, 0.0)
    shaped = rising(pos, 3) * jnp.exp(-pos * c_row) * gain_row
    return jnp.where(lag >= 0.0, shaped, 0.0)


def masked_rows(parts, y):
    rows = iota(parts[0].shape, 0)
    return jnp.concatenate([jnp.where(rows == float(y), p, 0.0) for p in parts], axis=0)


def lon_finals(c, leak, scale, cells, backward):
    x = iota(c.shape, 1)
    remain = x if backward else (cells - 1.0) - x
    decay = jnp.exp(-remain * c)
    return [leak ** (s + 1) * scale * rising(remain, s) * decay for s in range(4)]


def lon_entering(c, leak, cells, backward):
    x = iota(c.shape, 1)
    place = (cells - 1.0) - x if backward else x
    decay = jnp.exp(-(place + 1.0) * c)
    return [leak ** (3 - s) * rising(place, 3 - s) * decay for s in range(4)]


def entering_columns(lonc, rows, cells, backward, first):
    c, leak, _ = lon_consts(lonc)
    before = [jnp.zeros((first, cells), f32)] if first else []
    after = cells - first - 4 * rows
    after = [jnp.zeros((after, cells), f32)] if after else []
    return jnp.concatenate(before + lon_entering(c, leak, cells, backward) + after, axis=0).T


def lon_tables(lonc, rows, cells, backward, table_ref):
    c, leak, scale = lon_consts(lonc)
    gain = leak**4 * scale
    finals = lon_finals(c, leak, scale, cells, backward)
    spare = jnp.zeros((cells - 4 * rows, cells), f32)
    finals = jnp.concatenate(finals + [spare], axis=0).T
    column = lax.broadcasted_iota(jnp.int32, (cells, cells), 1)
    if backward:
        products = entering_columns(lonc, rows, cells, backward, cells - 4 * rows)
    for y in range(rows):
        inside = lon_kernel_matrix(c[y : y + 1], gain[y : y + 1], cells, backward)
        leaving = jnp.where(lax.rem(column, rows) == y, finals, 0.0)
        if backward:
            mine = jnp.where(lax.rem(column, rows) == y, products, 0.0)
            leaving = leaving + jnp.dot(
                inside, mine, precision=lax.Precision.HIGHEST, preferred_element_type=f32
            )
        table_ref[y] = right3(jnp.concatenate([inside, leaving], axis=1), 0)


def lon_local_rows(load_row, table_ref, rows, cells, inside_ref, also=None):
    total = None
    for y in range(rows):
        both = product3(left3(load_row(y), 1), table_ref[y])
        inside_ref[y] = both[:, :cells]
        if also is not None:
            also(y, both[:, :cells])
        total = both[:, cells:] if total is None else total + both[:, cells:]
    return total


def lon_incoming_states(lonc, blocks, rows, cells):
    k = blocks[0].shape[1]
    n = len(blocks)
    c = jnp.broadcast_to(lonc[:, :1], (rows, k))
    leak = 1.0 - jnp.exp(-c)

    def trans(r):
        closing = jnp.exp(-float(r * cells) * c)
        return [choose(r * cells, i) * leak**i * closing for i in range(4)]

    total = [jnp.zeros((rows, k), f32) for _ in range(4)]
    for r in range(n):
        part = [blocks[r][s * rows : (s + 1) * rows] for s in range(4)]
        if r:
            t = trans(r)
            part = [sum(t[i - j] * part[j] for j in range(i + 1)) for i in range(4)]
        total = [a + b for a, b in zip(total, part)]
    t = trans(n)
    solved = []
    for i in range(4):
        v = total[i]
        for j in range(i):
            v = v + t[i - j] * solved[j]
        solved.append(v / (1.0 - t[0]))
    return jnp.concatenate(solved, axis=0)


def lon_correction(states, entering, rows, cells):
    high = states.astype(bf16).astype(f32)
    low = states - high
    spare = jnp.zeros((cells - 12 * rows, states.shape[1]), f32)
    left = jnp.concatenate([high, low, high, spare], axis=0).T.astype(bf16)
    spare = jnp.zeros((cells - 12 * rows, cells), bf16)
    return lambda y: product3(left, jnp.concatenate([right3(masked_rows(entering, y), 0), spare], axis=0))


def lat_consts(dec):
    q = jnp.exp(-dec)
    leak = 1.0 - q
    return q, leak, leak * (2.5 / jnp.sqrt(leak))


def lat_sweep(load, store, start, dec, rows, k, backward, block):
    q1, l1, g1 = lat_consts(dec)
    x = dec.shape[1]
    q = jnp.broadcast_to(q1, (block, x))
    leak = jnp.broadcast_to(l1, (block, x))
    gain = jnp.broadcast_to(g1, (block, x))
    order = range(rows - 1, -1, -1) if backward else range(rows)

    def step(i, carry):
        at = pl.ds(pl.multiple_of(i * block, 8), block)
        u = start(at)
        for y in order:
            feed = gain * load(y, at, i * block)
            u0 = q * u[0] + feed
            u1 = q * u[1] + leak * u0
            u2 = q * u[2] + leak * u1
            u3 = q * u[3] + leak * u2
            u = [u0, u1, u2, u3]
            store(y, at, i * block, u3, u if y == order[-1] else None)
        return carry

    if k == block:
        step(0, 0)
    else:
        lax.fori_loop(0, k // block, step, 0)


def swap_halves(a, b):
    half = a.shape[-1] // 2
    low = iota((1,) * (a.ndim - 1) + (a.shape[-1],), a.ndim - 1) < float(half)
    turn = lambda v: pltpu.roll(v, half, v.ndim - 1)
    return jnp.where(low, a, turn(b)), jnp.where(low, turn(a), b)


def both_halves(v):
    return swap_halves(v, v)


def lat_trans(dec, rows):
    leak = 1.0 - jnp.exp(-dec)
    closing = jnp.exp(-float(rows) * dec)
    return [choose(rows, i) * leak**i * closing for i in range(4)]


def entering_states(got, chunks, block):
    hops = len(got) // chunks
    mine = [block[:1] == float(h + 1) for h in range(hops)]

    def at(chunk, where):
        out = []
        for s in range(4):
            v = None
            for m, p in zip(mine, got[chunk * hops : (chunk + 1) * hops]):
                new = p[s, where, :]
                v = jnp.where(m, new, jnp.zeros_like(new) if v is None else v)
            out.append(v)
        return out

    return at


def rows_at_once(size):
    return 40 if size % 40 == 0 else 8


def sweep_chunks(load, store, start, dec, rows, k, chunks, backward):
    size = k // chunks
    block = rows_at_once(size)
    for ch in range(chunks):
        lat_sweep(
            lambda y, at, base, ch=ch: load(y, ch * size + base),
            lambda y, at, base, value, last, ch=ch: store(y, ch, at, ch * size + base, value, last),
            lambda at, ch=ch: start(ch, at),
            dec,
            rows,
            size,
            backward,
            block,
        )


def k_tables(rows, cells, dec_ref, lonc_ref, latc_ref, table_ref, block_ref):
    block_ref[...] = jnp.full((8, cells), lax.axis_index("lat").astype(f32))
    row = jnp.broadcast_to(dec_ref[:, cells:], (rows, rows))
    own = iota((rows, rows), 0) == iota((rows, rows), 1)
    column = jnp.sum(jnp.where(own, row, 0.0), axis=1, keepdims=True)
    lonc = jnp.broadcast_to(column, (rows, cells))
    lonc_ref[...] = lonc
    first, second = both_halves(jnp.broadcast_to(dec_ref[:, :cells], (8, cells)))
    latc_ref[0] = first
    latc_ref[1] = second
    lon_tables(lonc, rows, cells, False, table_ref)


def k_lon_fwd(rows, k, cells, d_ref, table_ref, inside_ref, carried_ref):
    d_ref = d_ref.reshape(k * rows, cells)
    total = lon_local_rows(lambda y: d_ref[pl.ds(y, k, stride=rows), :], table_ref, rows, cells, inside_ref)
    carried_ref[...] = total.T[: 4 * rows]


def spread_modes(v, pairs, transposed):
    source = v.T if transposed else v
    r, c = source.shape
    rows, columns = pairs * r, 3 * pairs * c
    exact = functools.partial(jnp.dot, precision=lax.Precision.HIGHEST, preferred_element_type=f32)
    block = lambda at, size: jnp.floor((at + 0.5) * (1.0 / size))
    at_column = iota((c, columns), 1)
    pick_column = (at_column - block(at_column, c) * c == iota((c, columns), 0)).astype(f32)
    everywhere = jnp.concatenate([exact(source, pick_column)] * pairs, axis=0)
    column = iota((1, columns), 1)
    part = block(column, pairs * c)
    own = block(iota((rows, 1), 0), r) == block(column - part * (pairs * c), c)
    full = jnp.where(own, everywhere, 0.0)
    high, low = halves(full)
    return jnp.where(part == 1.0, low.astype(f32), high.astype(f32)).astype(bf16)


def k_out_modes(pairs, v_ref, eig_ref, mask_ref, modes_ref):
    modes = v_ref.shape[0]
    cells = mask_ref.shape[1]
    modes_ref[...] = spread_modes(v_ref[...], pairs, True)
    e = lax.broadcasted_iota(jnp.int32, (modes, cells), 0)
    low = lax.broadcasted_iota(jnp.int32, (modes, cells), 1) < cells // 2
    for m in range(pairs):
        used = jnp.where(low, eig_ref[m], eig_ref[m + pairs])
        mask_ref[m * modes : (m + 1) * modes] = jnp.where(e < used, 1.0, 0.0)


def k_in_modes(pairs, v_ref, modes_ref):
    modes_ref[...] = spread_modes(v_ref[...], pairs, False)


def row_spacing(size):
    return size + 8 if size // 8 % 2 == 0 else size


def k_back_tables(lon_ref, table_ref):
    lon_tables(lon_ref[...], *lon_ref.shape, True, table_ref)


def k_prepare(m_ref, a_ref, b_ref):
    members, levels, rows, _ = m_ref.shape
    pairs = members // 2
    apart = row_spacing(pairs * levels)

    def step(i, carry):
        for l in range(levels):
            a, b = swap_halves(m_ref[i, l].astype(f32), m_ref[i + pairs, l].astype(f32))
            at = pl.ds(i * levels + l, rows, stride=apart)
            a_ref[at, :] = a
            b_ref[at, :] = b
        return carry

    lax.fori_loop(0, pairs, step, 0)


def k_lat_first(rows, k, cells, n, chunks, *refs):
    inside_ref, lon_ref, lat_ref, *rest = refs
    blocks = [r[...] for r in rest[:n]]
    f_refs, out_refs = rest[n : n + 2], rest[n + 2 :]
    lonc = lon_ref[...]
    states = lon_incoming_states(lonc, blocks, rows, cells)
    c, leak, _ = lon_consts(lonc)
    added = lon_correction(states, lon_entering(c, leak, cells, False), rows, cells)
    half = k // 2
    for y in range(rows):
        row = inside_ref[y] + added(y)
        f_refs[0][y], f_refs[1][y] = swap_halves(row[:half], row[half:])
    for part, f_ref in enumerate(f_refs):

        def store(y, ch, at, base, value, last, part=part):
            if last is not None:
                for s in range(4):
                    out_refs[sum(chunks[:part]) + ch][s, at, :] = last[s]

        sweep_chunks(
            lambda y, base, part=part: f_ref[y, pl.ds(pl.multiple_of(base, 8), rows_at_once(half // chunks[part])), :],
            store,
            lambda ch, at: [jnp.zeros((1, cells), f32)] * 4,
            lat_ref[part, :1],
            rows,
            half,
            chunks[part],
            False,
        )


def k_pass_on(rows, part, carried_ref, got_ref, lat_ref, out_ref):
    t = lat_trans(lat_ref[part, :1], rows)
    got = [got_ref[s] for s in range(4)]
    for i in range(4):
        v = carried_ref[i]
        for j in range(i + 1):
            v = v + t[i - j] * got[j]
        out_ref[i] = v


def k_increment(rows, k, part, chunks, count, pairs, levels, *refs):
    f_ref, lat_ref, block_ref, m_ref, mask_ref, modes_ref, *rest = refs
    out_ref, s_ref = rest[count:]
    cells = lat_ref.shape[-1]

    def store(y, ch, at, base, value, last):
        where = pl.ds(pl.multiple_of(base, 8), rows_at_once(k // chunks))
        s_ref[y, where, :] = value * mask_ref[where, :]

    sweep_chunks(
        lambda y, base: f_ref[y, pl.ds(pl.multiple_of(base, 8), rows_at_once(k // chunks)), :],
        store,
        entering_states(rest[:count], chunks, block_ref[...]),
        lat_ref[part, :1],
        rows,
        k,
        chunks,
        False,
    )
    half = levels // 2
    low = iota((1, cells), 1) < float(cells // 2)
    apart = row_spacing(pairs * levels)
    for y in range(rows):
        profile = product3(modes_ref[...], right3(s_ref[y], 0))
        inc = None
        for m in range(pairs):
            at = y * apart + m * levels
            p = m_ref[at : at + levels, :] * profile[m * levels : (m + 1) * levels]
            inc = p if inc is None else inc + p
        inc = inc + pltpu.roll(inc, cells // 2, 1)
        out_ref[y] = jnp.where(low, inc[:half], inc[half:])


def k_gradient(rows, k, part, chunks, pairs, levels, *refs):
    inc_ref, got_ref, obs_ref, m_ref, mask_ref, modes_ref, lat_ref, g_ref, *carried_refs = refs
    cells = lat_ref.shape[-1]
    obs_ref = obs_ref.reshape(levels * rows, cells)
    size = pairs * levels
    apart = row_spacing(size)
    for y in range(rows):
        inc = jnp.concatenate(both_halves(inc_ref[y] + got_ref[y]), axis=0)
        w = inc * both_halves(obs_ref[pl.ds(y, levels, stride=rows), :])[part]
        m = m_ref[y * apart : y * apart + size, :]
        weighted = (m.reshape(pairs, levels, cells) * w[None]).reshape(size, cells)
        g_ref[y] = product3(modes_ref[...], right3(weighted, 0)) * mask_ref[...]

    def store(y, ch, at, base, value, last):
        if last is not None:
            for s in range(4):
                carried_refs[ch][s, at, :] = last[s]

    sweep_chunks(
        lambda y, base: g_ref[y, pl.ds(pl.multiple_of(base, 8), rows_at_once(k // chunks)), :],
        store,
        lambda ch, at: [jnp.zeros((1, cells), f32)] * 4,
        lat_ref[part, :1],
        rows,
        k,
        chunks,
        True,
    )


def k_lon_bwd(rows, k, cells, chunks, count, blocks, *refs):
    g_refs, lat_ref, block_ref, table_ref, rest = refs[:2], refs[2], refs[3], refs[4], refs[5:]
    block = (blocks - 1.0) - block_ref[...]
    d_ref, r_ref, known_ref, inside_ref, sent_ref, p_ref = rest[sum(count) :]
    d_ref = d_ref.reshape(k * rows, cells)
    r_ref = r_ref.reshape(k * rows, cells)
    half = k // 2
    for part in range(2):
        g_ref = g_refs[part]

        def store(y, ch, at, base, value, last, part=part):
            p_ref[part, y, pl.ds(pl.multiple_of(base, 8), rows_at_once(half // chunks[part])), :] = value

        sweep_chunks(
            lambda y, base: g_ref[y, pl.ds(pl.multiple_of(base, 8), rows_at_once(half // chunks[part])), :],
            store,
            entering_states(rest[sum(count[:part]) : sum(count[: part + 1])], chunks[part], block),
            lat_ref[part, :1],
            rows,
            half,
            chunks[part],
            True,
        )

    def load_row(y):
        return jnp.concatenate(swap_halves(p_ref[0, y], p_ref[1, y]), axis=0)

    acc = [jnp.zeros((8, cells), f32)] * 4

    def also(y, q):
        at = pl.ds(y, k, stride=rows)
        d, r = d_ref[at, :], r_ref[at, :]
        h = d + q
        fold = lambda v: v.reshape(k // 8, 8, cells).sum(axis=0)
        acc[:] = [a + fold(v) for a, v in zip(acc, (r * r, d * h, r * h, h * h))]

    total = lon_local_rows(load_row, table_ref, rows, cells, inside_ref, also)
    sent_ref[:k] = total + known_ref[...]
    out = [a.sum(axis=0, keepdims=True) for a in acc]
    sent_ref[k:] = jnp.concatenate(out + [jnp.zeros((4, cells), f32)], axis=0)


def k_known(rows, k, cells, d_ref, r_ref, lon_ref, out_ref):
    d_ref = d_ref.reshape(k * rows, cells)
    r_ref = r_ref.reshape(k * rows, cells)
    columns = entering_columns(lon_ref[...], rows, cells, True, 0)
    column = lax.broadcasted_iota(jnp.int32, (cells, cells), 1)
    total = [None, None]
    for y in range(rows):
        table = right3(jnp.where(lax.rem(column, rows) == y, columns, 0.0), 0)
        for i, ref in enumerate((d_ref, r_ref)):
            part = product3(left3(ref[pl.ds(y, k, stride=rows), :], 1), table)
            total[i] = part if total[i] is None else total[i] + part
    group = 4 * rows
    d, r = total
    out_ref[...] = pltpu.roll(d, group, 1) + pltpu.roll(r, 2 * group, 1) + pltpu.roll(d, cells - group, 1)


def k_sums(rows, k, cells, lon_ref, own_ref, other_ref, sums_ref, states_ref):
    lonc = lon_ref[...]
    group = 4 * rows
    own, other = own_ref[:k].T, other_ref[:k].T
    c, leak, _ = lon_consts(lonc)
    entering = lon_entering(c, leak, cells, True)
    sums = own_ref[k:] + other_ref[k:]
    extra = [jnp.zeros((rows, k), f32)] * 3
    for here, there in ((own, other), (other, own)):
        states = lon_incoming_states(lonc, [there[:group], here[:group]], rows, cells)
        if here is own:
            states_ref[...] = states
        v = [states[s * rows : (s + 1) * rows] for s in range(4)]
        for s in range(4):
            d, r, h = (here[g * group + s * rows : g * group + (s + 1) * rows] for g in (1, 2, 3))
            both = 2.0 * h
            for t in range(4):
                both = both + jnp.sum(entering[s] * entering[t], axis=1, keepdims=True) * v[t]
            extra = [extra[0] + v[s] * d, extra[1] + v[s] * r, extra[2] + v[s] * both]
    lane, row = iota(sums.shape, 1), iota(sums.shape, 0)
    for i, e in enumerate(extra):
        e = jnp.sum(jnp.sum(e, axis=1, keepdims=True), axis=0, keepdims=True)
        sums = sums + jnp.where((lane == 0.0) & (row == float(i + 1)), e, 0.0)
    sums_ref[...] = sums


def k_finish(rows, k, cells, inside_ref, lon_ref, d_ref, states_ref, h_ref):
    d_ref = d_ref.reshape(k * rows, cells)
    c, leak, _ = lon_consts(lon_ref[...])
    added = lon_correction(states_ref[...], lon_entering(c, leak, cells, True), rows, cells)
    for y in range(rows):
        at = pl.ds(y, k, stride=rows)
        h_ref[at, :] = inside_ref[y] + added(y) + d_ref[at, :]


def k_sums_any(rows, k, cells, n, *refs):
    inside_ref, lon_ref, d_ref, r_ref, *rest = refs
    d_ref = d_ref.reshape(k * rows, cells)
    r_ref = r_ref.reshape(k * rows, cells)
    blocks = [r[:k].T[: 4 * rows] for r in rest[:n]]
    h_ref, sums_ref = rest[n:]
    lonc = lon_ref[...]
    states = lon_incoming_states(lonc, blocks, rows, cells)
    c, leak, _ = lon_consts(lonc)
    added = lon_correction(states, lon_entering(c, leak, cells, True), rows, cells)
    acc = [jnp.zeros((8, cells), f32)] * 4
    fold = lambda v: v.reshape(k // 8, 8, cells).sum(axis=0)
    for y in range(rows):
        at = pl.ds(y, k, stride=rows)
        d, r = d_ref[at, :], r_ref[at, :]
        h = inside_ref[y] + added(y) + d
        h_ref[at, :] = h
        acc = [a + fold(v) for a, v in zip(acc, (r * r, d * h, r * h, h * h))]
    out = [a.sum(axis=0, keepdims=True) for a in acc]
    sums_ref[...] = jnp.concatenate(out + [jnp.zeros((4, cells), f32)], axis=0)


def k_update(pieces, sums_ref, control_ref, r_ref, d_ref, h_ref, *rest):
    outs, news, sems = rest[:3], rest[3:6], rest[6]
    sums = jnp.sum(sums_ref[...], axis=1, keepdims=True)
    rr, dh, rh, hh = (sums[i : i + 1].reshape(1, 1, 1) for i in range(4))
    step = rr / dh
    norm_new = rr - 2.0 * step * rh + step * step * hh
    beta = norm_new / rr
    size = d_ref.shape[0] // pieces
    copies = []
    for i in range(pieces):
        at = pl.ds(i * size, size)
        d = d_ref[at]
        nr = r_ref[at] - step * h_ref[at]
        for j, v in enumerate((control_ref[at] + step * d, nr, nr + beta * d)):
            news[j][at] = v
            copy = pltpu.make_async_copy(news[j].at[at], outs[j].at[at], sems.at[j, i])
            copy.start()
            copies.append(copy)
    for copy in copies:
        copy.wait()


def call(body, outs, ins, specs=None, out_specs=None, scratch=(), cost=None):
    return pl.pallas_call(
        body,
        out_shape=outs,
        in_specs=specs or [VM] * len(ins),
        out_specs=out_specs or jax.tree.map(lambda _: VM, outs),
        scratch_shapes=scratch,
        cost_estimate=None if cost is None else pl.CostEstimate(flops=cost, bytes_accessed=1000, transcendentals=0),
        compiler_params=pltpu.CompilerParams(vmem_limit_bytes=16 * 1024 * 1024),
    )(*ins)


def sds(*shape):
    return jax.ShapeDtypeStruct(shape, f32)


def lon_exchange(carried, backward):
    n = lax.axis_size("lon")
    sign = -1 if backward else 1
    got = [
        lax.ppermute(carried, "lon", [(j, (j + sign * r) % n) for j in range(n)]) for r in range(1, n)
    ]
    return got + [carried]


def pass_on(part, got, latc, rows, c):
    return call(functools.partial(k_pass_on, rows, c), sds(*part.shape), [part, got, latc])


def hop_pairs(a, b):
    n, n_mem = lax.axis_size("lat"), lax.axis_size("mem")
    if n_mem % 2:
        return [(a * n_mem + i, b * n_mem + i) for i in range(n_mem)]
    to = lambda z, i: (b, i) if z == a else (a, i) if z == b else (z, i ^ 1)
    flat = lambda z, i: z * n_mem + i
    return [(flat(z, i), flat(*to(z, i))) for z in range(n) for i in range(n_mem)]


def lat_carry(halves, latc, rows, backward):
    n = lax.axis_size("lat")
    at = (lambda i: n - 1 - i) if backward else (lambda i: i)
    got = [[[] for _ in chunks] for chunks in halves]
    for h in range(n - 1):
        pairs = hop_pairs(at(h), at(h + 1))
        for c, chunks in enumerate(halves):
            for i, part in enumerate(chunks):
                v = pass_on(part, got[c][i][-1], latc, rows, c) if h else part
                got[c][i].append(lax.ppermute(v, ("lat", "mem"), pairs))
    return [[g for chunk in half for g in chunk] for half in got]


def all_sum(v, axes, steps):
    total = 1
    for a in axes:
        total *= lax.axis_size(a)
    masks = [0]
    for s in steps:
        masks = masks + [m ^ s for m in masks]
    got = [lax.ppermute(v, axes, [(i, i ^ m) for i in range(total)]) for m in masks[1:]]
    for g in got:
        v = v + g
    return v


def powers(n):
    out, d = [], 1
    while d < n:
        out.append(d)
        d *= 2
    return out


def reduce_everywhere(v, over_lon):
    n_lon, n_lat, n_mem = (lax.axis_size(a) for a in ("lon", "lat", "mem"))
    for s in powers(n_mem):
        v = all_sum(v, ("mem",), [s])
    for s in powers(n_lon) if over_lon else ():
        v = all_sum(v, ("lon",), [s])
    lat = powers(n_lat)
    for i in range(0, len(lat), 2):
        v = all_sum(v, ("lat",), lat[i : i + 2])
    return v


def iteration(control, residual, direction, members, vert_modes, eig_count, lon_decay, lat_decay, obs_weight):
    k, rows, cells = direction.shape
    mcount, levels = members.shape[:2]
    n_lon, n_mem = lax.axis_size("lon"), lax.axis_size("mem")
    half = k // 2
    pairs = mcount // 2
    chunks, back_chunks = (2, 1), (2, 1)
    states = lambda chunks: (sds(4, half // chunks, cells),) * chunks

    decays = jnp.concatenate([lat_decay, lon_decay]).reshape(1, cells + rows)
    lonc, latc, tables, block = call(
        functools.partial(k_tables, rows, cells),
        (sds(rows, cells), sds(2, 8, cells), jax.ShapeDtypeStruct((rows, 3 * cells, 2 * cells), bf16), sds(8, cells)),
        [decays],
        cost=4 * 10**8,
    )
    inside, carried = call(
        functools.partial(k_lon_fwd, rows, k, cells), (sds(rows, k, cells), sds(4 * rows, k)), [direction, tables]
    )
    packed = call(k_prepare, (sds(rows * row_spacing(pairs * levels), cells),) * 2, [members], cost=10**9)
    back_tables = call(k_back_tables, jax.ShapeDtypeStruct((rows, 3 * cells, 2 * cells), bf16), [lonc], cost=10**9)
    mask, out_modes = call(
        functools.partial(k_out_modes, pairs),
        (sds(half, cells), jax.ShapeDtypeStruct((pairs * levels, 3 * half), bf16)),
        [vert_modes, eig_count],
        specs=[VM, SM],
        cost=10**9,
    )
    in_modes = call(
        functools.partial(k_in_modes, pairs),
        jax.ShapeDtypeStruct((half, 3 * pairs * levels), bf16),
        [vert_modes],
        cost=10**9,
    )
    blocks = lon_exchange(carried, False)
    fa, fb, *parts = call(
        functools.partial(k_lat_first, rows, k, cells, n_lon, chunks),
        (sds(rows, half, cells),) * 2 + states(chunks[0]) + states(chunks[1]),
        [inside, lonc, latc, *blocks],
    )
    got = lat_carry([parts[: chunks[0]], parts[chunks[0] :]], latc, rows, False)
    count = tuple(len(g) for g in got)
    fields = (fa, fb)
    inc = [None, None]
    for part in range(2):
        inc[part] = call(
            functools.partial(k_increment, rows, half, part, chunks[part], count[part], pairs, levels),
            sds(rows, levels // 2, cells),
            [fields[part], latc, block, packed[part], mask, out_modes, *got[part]],
            scratch=[pltpu.VMEM((rows, half, cells), f32)],
        )
    grads, sends = [None, None], [None, None]
    for part in range(2):
        v = inc[part]
        step = 1
        while step * 2 < n_mem:
            v = v + lax.ppermute(v, "mem", [(i, i ^ step) for i in range(n_mem)])
            step *= 2
        other = lax.ppermute(v, "mem", [(i, i ^ step) for i in range(n_mem)])
        grads[part], *sends[part] = call(
            functools.partial(k_gradient, rows, half, part, back_chunks[part], pairs, levels),
            (sds(rows, half, cells),) + states(back_chunks[part]),
            [v, other, obs_weight, packed[part], mask, in_modes, latc],
        )
    got = lat_carry(sends, latc, rows, True)
    count = tuple(len(g) for g in got)
    known = call(functools.partial(k_known, rows, k, cells), sds(k, cells), [direction, residual, lonc], cost=10**9)
    inside, sent = call(
        functools.partial(k_lon_bwd, rows, k, cells, back_chunks, count, lax.axis_size("lat")),
        (sds(rows, k, cells), sds(k + 8, cells)),
        [*grads, latc, block, back_tables, *got[0], *got[1], direction, residual, known],
        scratch=[pltpu.VMEM((2, rows, half, cells), f32)],
    )
    blocks = lon_exchange(sent, True)
    if n_lon == 2:
        sums, states = call(
            functools.partial(k_sums, rows, k, cells), (sds(8, cells), sds(4 * rows, k)), [lonc, sent, blocks[0]]
        )
        sums = reduce_everywhere(sums, False)
        h = call(
            functools.partial(k_finish, rows, k, cells),
            sds(k * rows, cells),
            [inside, lonc, direction, states],
            cost=10**9,
        )
    else:
        h, sums = call(
            functools.partial(k_sums_any, rows, k, cells, n_lon),
            (sds(k * rows, cells), sds(8, cells)),
            [inside, lonc, direction, residual, *blocks],
        )
        sums = reduce_everywhere(sums, True)
    pieces = 4 if k % 4 == 0 else 1
    outs = call(
        functools.partial(k_update, pieces),
        (sds(k, rows, cells),) * 3,
        [sums, control, residual, direction, h.reshape(k, rows, cells)],
        out_specs=(pl.BlockSpec(memory_space=pl.ANY),) * 3,
        scratch=[pltpu.VMEM((k, rows, cells), f32)] * 3 + [pltpu.SemaphoreType.DMA((3, pieces))],
    )
    return tuple(outs)


def solution(mesh):
    field = P("mem", "lat", "lon")
    placed = (
        field,
        field,
        field,
        P("mem", None, "lat", "lon"),
        P(),
        P("mem"),
        P("lat"),
        P("lon"),
        P(None, "lat", "lon"),
    )
    return jax.shard_map(iteration, mesh=mesh, in_specs=placed, out_specs=(field,) * 3, check_vma=False)
```

```python
import functools
import jax
import jax.numpy as jnp
from jax import lax
from jax.experimental import pallas as pl
from jax.experimental.pallas import tpu as pltpu
from jax.sharding import PartitionSpec as P


f32 = jnp.float32
bf16 = jnp.bfloat16
VM = pl.BlockSpec(memory_space=pltpu.VMEM)
SM = pl.BlockSpec(memory_space=pltpu.SMEM)


def choose(length, i):
    r = 1.0
    for k in range(i):
        r = r * (length + k) / (k + 1)
    return r


def rising(v, degree):
    r = jnp.ones_like(v)
    for k in range(degree):
        r = r * (v + (k + 1.0)) * (1.0 / (k + 1.0))
    return r


def halves(v):
    high = v.astype(bf16)
    return high, (v - high.astype(f32)).astype(bf16)


def left3(v, axis):
    high, low = halves(v)
    return jnp.concatenate([high, low, high], axis=axis)


def right3(v, axis):
    high, low = halves(v)
    return jnp.concatenate([high, high, low], axis=axis)


def product3(a, b):
    return jnp.dot(a, b, preferred_element_type=f32)


def iota(shape, dim):
    return lax.broadcasted_iota(jnp.int32, shape, dim).astype(f32)


def lon_consts(lonc):
    c = lonc
    q = jnp.exp(-c)
    leak = 1.0 - q
    return c, leak, 2.5 / jnp.sqrt(leak)


def lon_kernel_matrix(c_row, gain_row, cells, backward):
    a = iota((cells, cells), 0)
    b = iota((cells, cells), 1)
    lag = a - b if backward else b - a
    pos = jnp.maximum(lag, 0.0)
    shaped = rising(pos, 3) * jnp.exp(-pos * c_row) * gain_row
    return jnp.where(lag >= 0.0, shaped, 0.0)


def masked_rows(parts, y):
    rows = iota(parts[0].shape, 0)
    return jnp.concatenate([jnp.where(rows == float(y), p, 0.0) for p in parts], axis=0)


def lon_finals(c, leak, scale, cells, backward):
    x = iota(c.shape, 1)
    remain = x if backward else (cells - 1.0) - x
    decay = jnp.exp(-remain * c)
    return [leak ** (s + 1) * scale * rising(remain, s) * decay for s in range(4)]


def lon_entering(c, leak, cells, backward):
    x = iota(c.shape, 1)
    place = (cells - 1.0) - x if backward else x
    decay = jnp.exp(-(place + 1.0) * c)
    return [leak ** (3 - s) * rising(place, 3 - s) * decay for s in range(4)]


def entering_columns(lonc, rows, cells, backward, first):
    c, leak, _ = lon_consts(lonc)
    before = [jnp.zeros((first, cells), f32)] if first else []
    after = cells - first - 4 * rows
    after = [jnp.zeros((after, cells), f32)] if after else []
    return jnp.concatenate(before + lon_entering(c, leak, cells, backward) + after, axis=0).T


def lon_tables(lonc, rows, cells, backward, table_ref):
    c, leak, scale = lon_consts(lonc)
    gain = leak**4 * scale
    finals = lon_finals(c, leak, scale, cells, backward)
    spare = jnp.zeros((cells - 4 * rows, cells), f32)
    finals = jnp.concatenate(finals + [spare], axis=0).T
    column = lax.broadcasted_iota(jnp.int32, (cells, cells), 1)
    if backward:
        products = entering_columns(lonc, rows, cells, backward, cells - 4 * rows)
    for y in range(rows):
        inside = lon_kernel_matrix(c[y : y + 1], gain[y : y + 1], cells, backward)
        leaving = jnp.where(lax.rem(column, rows) == y, finals, 0.0)
        if backward:
            mine = jnp.where(lax.rem(column, rows) == y, products, 0.0)
            leaving = leaving + jnp.dot(
                inside, mine, precision=lax.Precision.HIGHEST, preferred_element_type=f32
            )
        table_ref[y] = right3(jnp.concatenate([inside, leaving], axis=1), 0)


def lon_local_rows(load_row, table_ref, rows, cells, inside_ref, also=None):
    total = None
    for y in range(rows):
        both = product3(left3(load_row(y), 1), table_ref[y])
        inside_ref[y] = both[:, :cells]
        if also is not None:
            also(y, both[:, :cells])
        total = both[:, cells:] if total is None else total + both[:, cells:]
    return total


def lon_incoming_states(lonc, blocks, rows, cells):
    k = blocks[0].shape[1]
    n = len(blocks)
    c = jnp.broadcast_to(lonc[:, :1], (rows, k))
    leak = 1.0 - jnp.exp(-c)

    def trans(r):
        closing = jnp.exp(-float(r * cells) * c)
        return [choose(r * cells, i) * leak**i * closing for i in range(4)]

    total = [jnp.zeros((rows, k), f32) for _ in range(4)]
    for r in range(n):
        part = [blocks[r][s * rows : (s + 1) * rows] for s in range(4)]
        if r:
            t = trans(r)
            part = [sum(t[i - j] * part[j] for j in range(i + 1)) for i in range(4)]
        total = [a + b for a, b in zip(total, part)]
    t = trans(n)
    solved = []
    for i in range(4):
        v = total[i]
        for j in range(i):
            v = v + t[i - j] * solved[j]
        solved.append(v / (1.0 - t[0]))
    return jnp.concatenate(solved, axis=0)


def lon_correction(states, entering, rows, cells):
    high = states.astype(bf16).astype(f32)
    low = states - high
    spare = jnp.zeros((cells - 12 * rows, states.shape[1]), f32)
    left = jnp.concatenate([high, low, high, spare], axis=0).T.astype(bf16)
    spare = jnp.zeros((cells - 12 * rows, cells), bf16)
    return lambda y: product3(left, jnp.concatenate([right3(masked_rows(entering, y), 0), spare], axis=0))


def lat_consts(dec):
    q = jnp.exp(-dec)
    leak = 1.0 - q
    return q, leak, leak * (2.5 / jnp.sqrt(leak))


def lat_sweep(load, store, start, dec, rows, k, backward, block):
    q1, l1, g1 = lat_consts(dec)
    x = dec.shape[1]
    q = jnp.broadcast_to(q1, (block, x))
    leak = jnp.broadcast_to(l1, (block, x))
    gain = jnp.broadcast_to(g1, (block, x))
    order = range(rows - 1, -1, -1) if backward else range(rows)

    def step(i, carry):
        at = pl.ds(pl.multiple_of(i * block, 8), block)
        u = start(at)
        for y in order:
            feed = gain * load(y, at, i * block)
            u0 = q * u[0] + feed
            u1 = q * u[1] + leak * u0
            u2 = q * u[2] + leak * u1
            u3 = q * u[3] + leak * u2
            u = [u0, u1, u2, u3]
            store(y, at, i * block, u3, u if y == order[-1] else None)
        return carry

    if k == block:
        step(0, 0)
    else:
        lax.fori_loop(0, k // block, step, 0)


def swap_halves(a, b):
    half = a.shape[-1] // 2
    low = iota((1,) * (a.ndim - 1) + (a.shape[-1],), a.ndim - 1) < float(half)
    turn = lambda v: pltpu.roll(v, half, v.ndim - 1)
    return jnp.where(low, a, turn(b)), jnp.where(low, turn(a), b)


def both_halves(v):
    return swap_halves(v, v)


def lat_trans(dec, rows):
    leak = 1.0 - jnp.exp(-dec)
    closing = jnp.exp(-float(rows) * dec)
    return [choose(rows, i) * leak**i * closing for i in range(4)]


def entering_states(got, chunks, block):
    hops = len(got) // chunks
    mine = [block[:1] == float(h + 1) for h in range(hops)]

    def at(chunk, where):
        out = []
        for s in range(4):
            v = None
            for m, p in zip(mine, got[chunk * hops : (chunk + 1) * hops]):
                new = p[s, where, :]
                v = jnp.where(m, new, jnp.zeros_like(new) if v is None else v)
            out.append(v)
        return out

    return at


def rows_at_once(size):
    return 40 if size % 40 == 0 else 8


def sweep_chunks(load, store, start, dec, rows, k, chunks, backward):
    size = k // chunks
    block = rows_at_once(size)
    for ch in range(chunks):
        lat_sweep(
            lambda y, at, base, ch=ch: load(y, ch * size + base),
            lambda y, at, base, value, last, ch=ch: store(y, ch, at, ch * size + base, value, last),
            lambda at, ch=ch: start(ch, at),
            dec,
            rows,
            size,
            backward,
            block,
        )


def k_tables(rows, cells, dec_ref, lonc_ref, latc_ref, table_ref, block_ref):
    block_ref[...] = jnp.full((8, cells), lax.axis_index("lat").astype(f32))
    row = jnp.broadcast_to(dec_ref[:, cells:], (rows, rows))
    own = iota((rows, rows), 0) == iota((rows, rows), 1)
    column = jnp.sum(jnp.where(own, row, 0.0), axis=1, keepdims=True)
    lonc = jnp.broadcast_to(column, (rows, cells))
    lonc_ref[...] = lonc
    first, second = both_halves(jnp.broadcast_to(dec_ref[:, :cells], (8, cells)))
    latc_ref[0] = first
    latc_ref[1] = second
    lon_tables(lonc, rows, cells, False, table_ref)


def k_lon_fwd(rows, k, cells, d_ref, table_ref, inside_ref, carried_ref):
    d_ref = d_ref.reshape(k * rows, cells)
    total = lon_local_rows(lambda y: d_ref[pl.ds(y, k, stride=rows), :], table_ref, rows, cells, inside_ref)
    carried_ref[...] = total.T[: 4 * rows]


def spread_modes(v, pairs, transposed):
    source = v.T if transposed else v
    r, c = source.shape
    rows, columns = pairs * r, 3 * pairs * c
    exact = functools.partial(jnp.dot, precision=lax.Precision.HIGHEST, preferred_element_type=f32)
    block = lambda at, size: jnp.floor((at + 0.5) * (1.0 / size))
    at_column = iota((c, columns), 1)
    pick_column = (at_column - block(at_column, c) * c == iota((c, columns), 0)).astype(f32)
    everywhere = jnp.concatenate([exact(source, pick_column)] * pairs, axis=0)
    column = iota((1, columns), 1)
    part = block(column, pairs * c)
    own = block(iota((rows, 1), 0), r) == block(column - part * (pairs * c), c)
    full = jnp.where(own, everywhere, 0.0)
    high, low = halves(full)
    return jnp.where(part == 1.0, low.astype(f32), high.astype(f32)).astype(bf16)


def k_out_modes(pairs, v_ref, eig_ref, mask_ref, modes_ref):
    modes = v_ref.shape[0]
    cells = mask_ref.shape[1]
    modes_ref[...] = spread_modes(v_ref[...], pairs, True)
    e = lax.broadcasted_iota(jnp.int32, (modes, cells), 0)
    low = lax.broadcasted_iota(jnp.int32, (modes, cells), 1) < cells // 2
    for m in range(pairs):
        used = jnp.where(low, eig_ref[m], eig_ref[m + pairs])
        mask_ref[m * modes : (m + 1) * modes] = jnp.where(e < used, 1.0, 0.0)


def k_in_modes(pairs, v_ref, modes_ref):
    modes_ref[...] = spread_modes(v_ref[...], pairs, False)


def row_spacing(size):
    return size + 8 if size // 8 % 2 == 0 else size


def k_back_tables(lon_ref, table_ref):
    lon_tables(lon_ref[...], *lon_ref.shape, True, table_ref)


def k_prepare(m_ref, a_ref, b_ref):
    members, levels, rows, _ = m_ref.shape
    pairs = members // 2
    apart = row_spacing(pairs * levels)

    def step(i, carry):
        for l in range(levels):
            a, b = swap_halves(m_ref[i, l].astype(f32), m_ref[i + pairs, l].astype(f32))
            at = pl.ds(i * levels + l, rows, stride=apart)
            a_ref[at, :] = a
            b_ref[at, :] = b
        return carry

    lax.fori_loop(0, pairs, step, 0)


def k_lat_first(rows, k, cells, n, chunks, *refs):
    inside_ref, lon_ref, lat_ref, *rest = refs
    blocks = [r[...] for r in rest[:n]]
    f_refs, out_refs = rest[n : n + 2], rest[n + 2 :]
    lonc = lon_ref[...]
    states = lon_incoming_states(lonc, blocks, rows, cells)
    c, leak, _ = lon_consts(lonc)
    added = lon_correction(states, lon_entering(c, leak, cells, False), rows, cells)
    half = k // 2
    for y in range(rows):
        row = inside_ref[y] + added(y)
        f_refs[0][y], f_refs[1][y] = swap_halves(row[:half], row[half:])
    for part, f_ref in enumerate(f_refs):

        def store(y, ch, at, base, value, last, part=part):
            if last is not None:
                for s in range(4):
                    out_refs[part * chunks + ch][s, at, :] = last[s]

        sweep_chunks(
            lambda y, base: f_ref[y, pl.ds(pl.multiple_of(base, 8), rows_at_once(half // chunks)), :],
            store,
            lambda ch, at: [jnp.zeros((1, cells), f32)] * 4,
            lat_ref[part, :1],
            rows,
            half,
            chunks,
            False,
        )


def k_pass_on(rows, part, carried_ref, got_ref, lat_ref, out_ref):
    t = lat_trans(lat_ref[part, :1], rows)
    got = [got_ref[s] for s in range(4)]
    for i in range(4):
        v = carried_ref[i]
        for j in range(i + 1):
            v = v + t[i - j] * got[j]
        out_ref[i] = v


def k_increment(rows, k, part, chunks, count, pairs, levels, *refs):
    f_ref, lat_ref, block_ref, m_ref, mask_ref, modes_ref, *rest = refs
    out_ref, s_ref = rest[count:]
    cells = lat_ref.shape[-1]

    def store(y, ch, at, base, value, last):
        where = pl.ds(pl.multiple_of(base, 8), rows_at_once(k // chunks))
        s_ref[y, where, :] = value * mask_ref[where, :]

    sweep_chunks(
        lambda y, base: f_ref[y, pl.ds(pl.multiple_of(base, 8), rows_at_once(k // chunks)), :],
        store,
        entering_states(rest[:count], chunks, block_ref[...]),
        lat_ref[part, :1],
        rows,
        k,
        chunks,
        False,
    )
    half = levels // 2
    low = iota((1, cells), 1) < float(cells // 2)
    apart = row_spacing(pairs * levels)
    for y in range(rows):
        profile = product3(modes_ref[...], right3(s_ref[y], 0))
        inc = None
        for m in range(pairs):
            at = y * apart + m * levels
            p = m_ref[at : at + levels, :] * profile[m * levels : (m + 1) * levels]
            inc = p if inc is None else inc + p
        inc = inc + pltpu.roll(inc, cells // 2, 1)
        out_ref[y] = jnp.where(low, inc[:half], inc[half:])


def k_gradient(rows, k, part, chunks, pairs, levels, *refs):
    inc_ref, got_ref, obs_ref, m_ref, mask_ref, modes_ref, lat_ref, g_ref, *carried_refs = refs
    cells = lat_ref.shape[-1]
    obs_ref = obs_ref.reshape(levels * rows, cells)
    size = pairs * levels
    apart = row_spacing(size)
    for y in range(rows):
        inc = jnp.concatenate(both_halves(inc_ref[y] + got_ref[y]), axis=0)
        w = inc * both_halves(obs_ref[pl.ds(y, levels, stride=rows), :])[part]
        m = m_ref[y * apart : y * apart + size, :]
        weighted = (m.reshape(pairs, levels, cells) * w[None]).reshape(size, cells)
        g_ref[y] = product3(modes_ref[...], right3(weighted, 0)) * mask_ref[...]

    def store(y, ch, at, base, value, last):
        if last is not None:
            for s in range(4):
                carried_refs[ch][s, at, :] = last[s]

    sweep_chunks(
        lambda y, base: g_ref[y, pl.ds(pl.multiple_of(base, 8), rows_at_once(k // chunks)), :],
        store,
        lambda ch, at: [jnp.zeros((1, cells), f32)] * 4,
        lat_ref[part, :1],
        rows,
        k,
        chunks,
        True,
    )


def k_lon_bwd(rows, k, cells, chunks, count, blocks, *refs):
    g_refs, lat_ref, block_ref, table_ref, rest = refs[:2], refs[2], refs[3], refs[4], refs[5:]
    block = (blocks - 1.0) - block_ref[...]
    d_ref, r_ref, known_ref, inside_ref, sent_ref, p_ref = rest[2 * count :]
    d_ref = d_ref.reshape(k * rows, cells)
    r_ref = r_ref.reshape(k * rows, cells)
    half = k // 2
    for part in range(2):
        g_ref = g_refs[part]

        def store(y, ch, at, base, value, last, part=part):
            p_ref[part, y, pl.ds(pl.multiple_of(base, 8), rows_at_once(half // chunks)), :] = value

        sweep_chunks(
            lambda y, base: g_ref[y, pl.ds(pl.multiple_of(base, 8), rows_at_once(half // chunks)), :],
            store,
            entering_states(rest[part * count : (part + 1) * count], chunks, block),
            lat_ref[part, :1],
            rows,
            half,
            chunks,
            True,
        )

    def load_row(y):
        return jnp.concatenate(swap_halves(p_ref[0, y], p_ref[1, y]), axis=0)

    acc = [jnp.zeros((8, cells), f32)] * 4

    def also(y, q):
        at = pl.ds(y, k, stride=rows)
        d, r = d_ref[at, :], r_ref[at, :]
        h = d + q
        fold = lambda v: v.reshape(k // 8, 8, cells).sum(axis=0)
        acc[:] = [a + fold(v) for a, v in zip(acc, (r * r, d * h, r * h, h * h))]

    total = lon_local_rows(load_row, table_ref, rows, cells, inside_ref, also)
    sent_ref[:k] = total + known_ref[...]
    out = [a.sum(axis=0, keepdims=True) for a in acc]
    sent_ref[k:] = jnp.concatenate(out + [jnp.zeros((4, cells), f32)], axis=0)


def k_known(rows, k, cells, d_ref, r_ref, lon_ref, out_ref):
    d_ref = d_ref.reshape(k * rows, cells)
    r_ref = r_ref.reshape(k * rows, cells)
    columns = entering_columns(lon_ref[...], rows, cells, True, 0)
    column = lax.broadcasted_iota(jnp.int32, (cells, cells), 1)
    total = [None, None]
    for y in range(rows):
        table = right3(jnp.where(lax.rem(column, rows) == y, columns, 0.0), 0)
        for i, ref in enumerate((d_ref, r_ref)):
            part = product3(left3(ref[pl.ds(y, k, stride=rows), :], 1), table)
            total[i] = part if total[i] is None else total[i] + part
    group = 4 * rows
    d, r = total
    out_ref[...] = pltpu.roll(d, group, 1) + pltpu.roll(r, 2 * group, 1) + pltpu.roll(d, cells - group, 1)


def k_sums(rows, k, cells, lon_ref, own_ref, other_ref, sums_ref, states_ref):
    lonc = lon_ref[...]
    group = 4 * rows
    own, other = own_ref[:k].T, other_ref[:k].T
    c, leak, _ = lon_consts(lonc)
    entering = lon_entering(c, leak, cells, True)
    sums = own_ref[k:] + other_ref[k:]
    extra = [jnp.zeros((rows, k), f32)] * 3
    for here, there in ((own, other), (other, own)):
        states = lon_incoming_states(lonc, [there[:group], here[:group]], rows, cells)
        if here is own:
            states_ref[...] = states
        v = [states[s * rows : (s + 1) * rows] for s in range(4)]
        for s in range(4):
            d, r, h = (here[g * group + s * rows : g * group + (s + 1) * rows] for g in (1, 2, 3))
            both = 2.0 * h
            for t in range(4):
                both = both + jnp.sum(entering[s] * entering[t], axis=1, keepdims=True) * v[t]
            extra = [extra[0] + v[s] * d, extra[1] + v[s] * r, extra[2] + v[s] * both]
    lane, row = iota(sums.shape, 1), iota(sums.shape, 0)
    for i, e in enumerate(extra):
        e = jnp.sum(jnp.sum(e, axis=1, keepdims=True), axis=0, keepdims=True)
        sums = sums + jnp.where((lane == 0.0) & (row == float(i + 1)), e, 0.0)
    sums_ref[...] = sums


def k_finish(rows, k, cells, inside_ref, lon_ref, d_ref, states_ref, h_ref):
    d_ref = d_ref.reshape(k * rows, cells)
    c, leak, _ = lon_consts(lon_ref[...])
    added = lon_correction(states_ref[...], lon_entering(c, leak, cells, True), rows, cells)
    for y in range(rows):
        at = pl.ds(y, k, stride=rows)
        h_ref[at, :] = inside_ref[y] + added(y) + d_ref[at, :]


def k_sums_any(rows, k, cells, n, *refs):
    inside_ref, lon_ref, d_ref, r_ref, *rest = refs
    d_ref = d_ref.reshape(k * rows, cells)
    r_ref = r_ref.reshape(k * rows, cells)
    blocks = [r[:k].T[: 4 * rows] for r in rest[:n]]
    h_ref, sums_ref = rest[n:]
    lonc = lon_ref[...]
    states = lon_incoming_states(lonc, blocks, rows, cells)
    c, leak, _ = lon_consts(lonc)
    added = lon_correction(states, lon_entering(c, leak, cells, True), rows, cells)
    acc = [jnp.zeros((8, cells), f32)] * 4
    fold = lambda v: v.reshape(k // 8, 8, cells).sum(axis=0)
    for y in range(rows):
        at = pl.ds(y, k, stride=rows)
        d, r = d_ref[at, :], r_ref[at, :]
        h = inside_ref[y] + added(y) + d
        h_ref[at, :] = h
        acc = [a + fold(v) for a, v in zip(acc, (r * r, d * h, r * h, h * h))]
    out = [a.sum(axis=0, keepdims=True) for a in acc]
    sums_ref[...] = jnp.concatenate(out + [jnp.zeros((4, cells), f32)], axis=0)


def k_update(pieces, sums_ref, control_ref, r_ref, d_ref, h_ref, *rest):
    outs, news, sems = rest[:3], rest[3:6], rest[6]
    sums = jnp.sum(sums_ref[...], axis=1, keepdims=True)
    rr, dh, rh, hh = (sums[i : i + 1].reshape(1, 1, 1) for i in range(4))
    step = rr / dh
    norm_new = rr - 2.0 * step * rh + step * step * hh
    beta = norm_new / rr
    size = d_ref.shape[0] // pieces
    copies = []
    for i in range(pieces):
        at = pl.ds(i * size, size)
        d = d_ref[at]
        nr = r_ref[at] - step * h_ref[at]
        for j, v in enumerate((control_ref[at] + step * d, nr, nr + beta * d)):
            news[j][at] = v
            copy = pltpu.make_async_copy(news[j].at[at], outs[j].at[at], sems.at[j, i])
            copy.start()
            copies.append(copy)
    for copy in copies:
        copy.wait()


def call(body, outs, ins, specs=None, out_specs=None, scratch=(), cost=None):
    return pl.pallas_call(
        body,
        out_shape=outs,
        in_specs=specs or [VM] * len(ins),
        out_specs=out_specs or jax.tree.map(lambda _: VM, outs),
        scratch_shapes=scratch,
        cost_estimate=None if cost is None else pl.CostEstimate(flops=cost, bytes_accessed=1000, transcendentals=0),
        compiler_params=pltpu.CompilerParams(vmem_limit_bytes=16 * 1024 * 1024),
    )(*ins)


def sds(*shape):
    return jax.ShapeDtypeStruct(shape, f32)


def lon_exchange(carried, backward):
    n = lax.axis_size("lon")
    sign = -1 if backward else 1
    got = [
        lax.ppermute(carried, "lon", [(j, (j + sign * r) % n) for j in range(n)]) for r in range(1, n)
    ]
    return got + [carried]


def pass_on(part, got, latc, rows, c):
    return call(functools.partial(k_pass_on, rows, c), sds(*part.shape), [part, got, latc])


def hop_pairs(a, b):
    n, n_mem = lax.axis_size("lat"), lax.axis_size("mem")
    if n_mem % 2:
        return [(a * n_mem + i, b * n_mem + i) for i in range(n_mem)]
    to = lambda z, i: (b, i) if z == a else (a, i) if z == b else (z, i ^ 1)
    flat = lambda z, i: z * n_mem + i
    return [(flat(z, i), flat(*to(z, i))) for z in range(n) for i in range(n_mem)]


def lat_carry(halves, latc, rows, backward):
    n = lax.axis_size("lat")
    at = (lambda i: n - 1 - i) if backward else (lambda i: i)
    got = [[[] for _ in chunks] for chunks in halves]
    for h in range(n - 1):
        pairs = hop_pairs(at(h), at(h + 1))
        for c, chunks in enumerate(halves):
            for i, part in enumerate(chunks):
                v = pass_on(part, got[c][i][-1], latc, rows, c) if h else part
                got[c][i].append(lax.ppermute(v, ("lat", "mem"), pairs))
    return [[g for chunk in half for g in chunk] for half in got]


def all_sum(v, axes, steps):
    total = 1
    for a in axes:
        total *= lax.axis_size(a)
    masks = [0]
    for s in steps:
        masks = masks + [m ^ s for m in masks]
    got = []
    for m in masks[:0:-1] if len(masks) < 4 else (masks[3], masks[1], masks[2]):
        got.append(lax.ppermute(v, axes, [(i, i ^ m) for i in range(total)]))
    for g in got:
        v = v + g
    return v


def powers(n):
    out, d = [], 1
    while d < n:
        out.append(d)
        d *= 2
    return out


def reduce_everywhere(v, over_lon):
    n_lon, n_lat, n_mem = (lax.axis_size(a) for a in ("lon", "lat", "mem"))
    for s in powers(n_mem):
        v = all_sum(v, ("mem",), [s])
    for s in powers(n_lon) if over_lon else ():
        v = all_sum(v, ("lon",), [s])
    lat = powers(n_lat)
    for i in range(0, len(lat), 2):
        v = all_sum(v, ("lat",), lat[i : i + 2])
    return v


def iteration(control, residual, direction, members, vert_modes, eig_count, lon_decay, lat_decay, obs_weight):
    k, rows, cells = direction.shape
    mcount, levels = members.shape[:2]
    n_lon, n_mem = lax.axis_size("lon"), lax.axis_size("mem")
    half = k // 2
    pairs = mcount // 2
    chunks, back_chunks = 2, 2
    states = lambda chunks: (sds(4, half // chunks, cells),) * chunks

    decays = jnp.concatenate([lat_decay, lon_decay]).reshape(1, cells + rows)
    lonc, latc, tables, block = call(
        functools.partial(k_tables, rows, cells),
        (sds(rows, cells), sds(2, 8, cells), jax.ShapeDtypeStruct((rows, 3 * cells, 2 * cells), bf16), sds(8, cells)),
        [decays],
        cost=4 * 10**8,
    )
    inside, carried = call(
        functools.partial(k_lon_fwd, rows, k, cells), (sds(rows, k, cells), sds(4 * rows, k)), [direction, tables]
    )
    packed = call(k_prepare, (sds(rows * row_spacing(pairs * levels), cells),) * 2, [members], cost=10**9)
    back_tables = call(k_back_tables, jax.ShapeDtypeStruct((rows, 3 * cells, 2 * cells), bf16), [lonc], cost=10**9)
    mask, out_modes = call(
        functools.partial(k_out_modes, pairs),
        (sds(half, cells), jax.ShapeDtypeStruct((pairs * levels, 3 * half), bf16)),
        [vert_modes, eig_count],
        specs=[VM, SM],
        cost=10**9,
    )
    in_modes = call(
        functools.partial(k_in_modes, pairs),
        jax.ShapeDtypeStruct((half, 3 * pairs * levels), bf16),
        [vert_modes],
        cost=10**9,
    )
    blocks = lon_exchange(carried, False)
    fa, fb, *parts = call(
        functools.partial(k_lat_first, rows, k, cells, n_lon, chunks),
        (sds(rows, half, cells),) * 2 + states(chunks) * 2,
        [inside, lonc, latc, *blocks],
    )
    got = lat_carry([parts[:chunks], parts[chunks:]], latc, rows, False)
    count = len(got[0])
    fields = (fa, fb)
    inc = [None, None]
    for part in range(2):
        inc[part] = call(
            functools.partial(k_increment, rows, half, part, chunks, count, pairs, levels),
            sds(rows, levels // 2, cells),
            [fields[part], latc, block, packed[part], mask, out_modes, *got[part]],
            scratch=[pltpu.VMEM((rows, half, cells), f32)],
        )
    grads, sends = [None, None], [None, None]
    for part in range(2):
        v = inc[part]
        step = 1
        while step * 2 < n_mem:
            v = v + lax.ppermute(v, "mem", [(i, i ^ step) for i in range(n_mem)])
            step *= 2
        other = lax.ppermute(v, "mem", [(i, i ^ step) for i in range(n_mem)])
        grads[part], *sends[part] = call(
            functools.partial(k_gradient, rows, half, part, back_chunks, pairs, levels),
            (sds(rows, half, cells),) + states(back_chunks),
            [v, other, obs_weight, packed[part], mask, in_modes, latc],
        )
    got = lat_carry(sends, latc, rows, True)
    count = len(got[0])
    known = call(functools.partial(k_known, rows, k, cells), sds(k, cells), [direction, residual, lonc], cost=10**9)
    inside, sent = call(
        functools.partial(k_lon_bwd, rows, k, cells, back_chunks, count, lax.axis_size("lat")),
        (sds(rows, k, cells), sds(k + 8, cells)),
        [*grads, latc, block, back_tables, *got[0], *got[1], direction, residual, known],
        scratch=[pltpu.VMEM((2, rows, half, cells), f32)],
    )
    blocks = lon_exchange(sent, True)
    if n_lon == 2:
        sums, states = call(
            functools.partial(k_sums, rows, k, cells), (sds(8, cells), sds(4 * rows, k)), [lonc, sent, blocks[0]]
        )
        sums = reduce_everywhere(sums, False)
        h = call(
            functools.partial(k_finish, rows, k, cells),
            sds(k * rows, cells),
            [inside, lonc, direction, states],
            cost=10**9,
        )
    else:
        h, sums = call(
            functools.partial(k_sums_any, rows, k, cells, n_lon),
            (sds(k * rows, cells), sds(8, cells)),
            [inside, lonc, direction, residual, *blocks],
        )
        sums = reduce_everywhere(sums, True)
    pieces = 4 if k % 4 == 0 else 1
    outs = call(
        functools.partial(k_update, pieces),
        (sds(k, rows, cells),) * 3,
        [sums, control, residual, direction, h.reshape(k, rows, cells)],
        out_specs=(pl.BlockSpec(memory_space=pl.ANY),) * 3,
        scratch=[pltpu.VMEM((k, rows, cells), f32)] * 3 + [pltpu.SemaphoreType.DMA((3, pieces))],
    )
    return tuple(outs)


def solution(mesh):
    field = P("mem", "lat", "lon")
    placed = (
        field,
        field,
        field,
        P("mem", None, "lat", "lon"),
        P(),
        P("mem"),
        P("lat"),
        P("lon"),
        P(None, "lat", "lon"),
    )
    return jax.shard_map(iteration, mesh=mesh, in_specs=placed, out_specs=(field,) * 3, check_vma=False)
```
